32 devices in a mesh: region: 4 (over y, x), col: 8 (over z, core).
Axes of the slice: x: 2, y: 2, z: 4, core: 2. Of those that a mesh axis runs over, the one named last changes fastest.
Arguments:
- jac: bfloat16 [256, 128], P(('region', 'col')), may hold values from -2 to 2
- dest: int32 [256, 2], P(('region', 'col')), may hold values from 0 to 3, all different within a row; in each aligned block of 8 rows (0 to 7, 8 to 15, ...) at most 6 rows name the same one
- near_pose: int32 [256, 2], P(('region', 'col')), may hold values from 0 to 255
- prior: float32 [8192], P('region'), may hold values from 0.5 to 8
Outputs:
- front_out: float32 [8192, 8192], P('region', 'col')
The draws below stay inside these ranges and needn't reach their ends.
Inputs may be any that keep to these rules, and one draw needn't show every extreme that they name: `dest`: each row names two different regions; among the 8 rows of one device no region is named more than 6 times, and in some device's rows some region is named exactly 6 times.
All inputs are finite; a program needn't handle non-finite values.
Results may differ from the reference program's by a relative error of at most 0.00045.
Values may be sent and summed in bfloat16 or wider, within the bound.
No kernel may reach another device: no remote copies, remote signals or barrier semaphores. Data moves between devices by JAX's collectives and lax.ppermute only.
A program may use at most 320 MiB of HBM per device.

```python
import math
import jax
import jax.numpy as jnp
import numpy as np
from jax import lax

F = 8192
NB = 128
K_PANELS = 2
M_DEV = 8
POSES = 1024
REGION_POSES = 256
CAP = 6
ROWS = 256
N_REGION = 4


def set_ends(entries, own_key, low, top_value):
    place = [jax.random.randint(jax.random.fold_in(own_key, axis), (), 0, length) for axis, length in enumerate(entries.shape)]
    longest = entries.shape.index(max(entries.shape))
    neighbour = place[:longest] + [(place[longest] + 1) % entries.shape[longest]] + place[longest + 1:]
    return entries.at[tuple(place)].set(low).at[tuple(neighbour)].set(top_value)


def shard_levels(key, shape, shards, low, top_value):
    factor_of, own = 1.0, jax.random.fold_in(key, 6)
    for axis_at, shards_of in shards:
        steps = jnp.exp(jax.random.uniform(jax.random.fold_in(own, axis_at), (shards_of,), jnp.float32, low / len(shards), top_value / len(shards)))
        factor_of = factor_of * jnp.repeat(steps, shape[axis_at] // shards_of).reshape([-1 if axis == axis_at else 1 for axis in range(len(shape))])
    return factor_of


def shared_out(own_key, own, number, rows, number_of, top, most, lean):
    order = jax.random.permutation(own_key, number_of)
    heavy_load, ordinary = portions_of(number_of, rows * top, most, lean, True), portions_of(number_of, rows * top, most, lean, False)
    places = jnp.arange(number_of)

    def named(lengths, rotation):
        used = int((lengths > 0).sum())
        fixed = max(1, used // 4)
        passed = fixed + (places - fixed + rotation * (used - fixed)) % max(1, number_of - fixed)
        return jnp.zeros((number_of,), jnp.int32).at[order[jnp.where(places < fixed, places, passed)]].set(jnp.asarray(lengths, jnp.int32))

    lengths = jnp.where(number % 4 == 0, named(heavy_load, number // 4), named(ordinary, number - number // 4 - 1))
    mixed = jax.random.permutation(jax.random.fold_in(own, 3), number_of)
    donor, sink = mixed[0:number_of // 2 * 2:2], mixed[1:number_of // 2 * 2:2]
    room = jnp.minimum(lengths[donor] - 1, most - lengths[sink]) // 2
    room = jnp.where((donor == order[0]) | (sink == order[0]) | (lengths[sink] == 0), 0, jnp.maximum(room, 0))
    passed = jax.random.randint(jax.random.fold_in(own, 4), (number_of // 2,), 0, 1 << 20) % (room + 1)
    lengths = lengths.at[donor].add(-passed).at[sink].add(passed)
    members = jnp.searchsorted(jnp.cumsum(lengths), jnp.arange(rows * top), side="right").astype(jnp.int32)
    table = members.reshape(top, rows).T
    table = table[jax.random.permutation(jax.random.fold_in(own, 1), rows)]
    rotation = jax.random.randint(jax.random.fold_in(own, 2), (rows, 1), 0, top)
    return jnp.take_along_axis(table, (jnp.arange(top)[None, :] + rotation) % top, axis=1)


def portions_of(count, total, limit, skew, full):
    loads = [(1 << 20) // math.isqrt(standing ** skew) + 1 for standing in range(1, count + 1)]
    largest = limit if full else min(limit, max(-(-total // count), total * loads[0] // sum(loads)))
    least = 1 if total - largest >= count - 1 else 0
    given, rest = [largest] + [least] * (count - 1), total - largest - least * (count - 1)
    while rest > 0:
        candidates = [i for i in range(1, count) if given[i] < largest] or [i for i in range(1, count) if given[i] < limit]
        mass, left = sum([loads[i] for i in candidates]), rest
        for i in candidates:
            addition = min(limit - given[i], max(1, left * loads[i] // mass), rest)
            given[i] = given[i] + addition
            rest = rest - addition
    return np.array(given)


def normal_values(own_key, extent, scale, most, cuts=(), dtype=jnp.bfloat16):
    gain = shard_levels(own_key, extent, cuts, -0.22, 0.18) if cuts else 1.0
    entries = jax.random.normal(own_key, extent, jnp.float32) * scale * gain
    return jnp.minimum(jnp.maximum(entries, -most), most).astype(dtype)


def setup_inputs(seed: int = 0) -> dict:
    splits = jax.random.split(jax.random.key(seed), 5)
    jac = normal_values(splits[0], (ROWS, 128), 8 ** -0.5, 2.0, ((0, 32),))
    dest_keys = jax.random.split(jax.random.fold_in(splits[1], 1), ROWS // M_DEV)
    dest_turns = jax.random.permutation(jax.random.fold_in(splits[1], 3), ROWS // M_DEV)
    dest = jax.vmap(lambda own, number: shared_out(jax.random.fold_in(splits[1], 2), own, number, M_DEV, N_REGION, 2, CAP, 2))(dest_keys, dest_turns).reshape((ROWS, 2))
    near_pose = set_ends(jax.random.randint(splits[2], (ROWS, 2), 0, REGION_POSES), jax.random.fold_in(splits[2], 1), 0, REGION_POSES - 1).astype(jnp.int32)
    prior = jnp.clip(jnp.exp(math.log(8.0) - 2.7725887 * jax.random.uniform(splits[3], (F,), jnp.float32) ** shard_levels(splits[3], (F,), ((0, 4),), -0.2, 0.2)), 0.5, 8.0)
    return dict(jac=jac, dest=dest, near_pose=near_pose, prior=prior)


def reference(jac, dest, near_pose, prior):
    count_rows = jac.shape[0]
    blocks = jac.astype(jnp.float32).reshape(count_rows, 2, 8, 8)
    poses = (dest * REGION_POSES + near_pose).astype(jnp.int32)
    tensor = jnp.zeros((POSES, 8, POSES, 8), jnp.float32)
    for first_side in range(2):
        for second_side in range(2):
            product = jnp.einsum('mek,mel->mkl', blocks[:, first_side], blocks[:, second_side], precision=lax.Precision.HIGHEST)
            tensor = tensor.at[poses[:, first_side], :, poses[:, second_side], :].add(product)
    matrix = tensor.reshape(F, F) + jnp.diag(prior.astype(jnp.float32))
    for panel_number in range(K_PANELS):
        low_edge = panel_number * NB
        high_edge = low_edge + NB
        factor = jnp.tril(jnp.linalg.cholesky(matrix[low_edge:high_edge, low_edge:high_edge]))
        below = jax.scipy.linalg.solve_triangular(factor, matrix[high_edge:, low_edge:high_edge].T, lower=True).T
        matrix = matrix.at[high_edge:, high_edge:].add(-jnp.dot(below, below.T, precision=lax.Precision.HIGHEST))
        matrix = matrix.at[low_edge:high_edge, low_edge:high_edge].set(factor)
        matrix = matrix.at[high_edge:, low_edge:high_edge].set(below)
        matrix = matrix.at[low_edge:high_edge, high_edge:].set(0.0)
    return matrix
```

```python
import functools

import jax
import jax.numpy as jnp
from jax import lax
from jax.experimental import pallas as pl
from jax.experimental.pallas import tpu as pltpu
from jax.sharding import PartitionSpec as P

NB = 128
K_PANELS = 2
PANEL = NB * K_PANELS
PP = PANEL // 8
CH = 256
BIG = float(1 << 24)
f32, bf16, i32 = jnp.float32, jnp.bfloat16, jnp.int32


def iota(shape, dim):
    return lax.broadcasted_iota(i32, shape, dim)


def split(x, parts):
    out = []
    for _ in range(parts):
        top = x.astype(bf16)
        out.append(top)
        x = x - top.astype(f32)
    return out


def dot(a, b, dims=((1,), (0,))):
    return lax.dot_general(a, b, (dims, ((), ())), preferred_element_type=f32)


def pack_kernel(jac_ref, dest_ref, near_ref, prior_ref, out_ref):
    shape = (8, 128)
    lane, row = iota(shape, 1), iota(shape, 0)
    dest, near = dest_ref[...].astype(f32), near_ref[...].astype(f32)
    tile = jnp.zeros(shape, f32)
    for at, column in enumerate((dest[:, 0:1], near[:, 0:1], dest[:, 1:2], near[:, 1:2])):
        tile = jnp.where(lane == at, column, tile)
    first = prior_ref[0:2, :]
    both = jnp.where(row < 4, first[0:1, :], first[1:2, :])
    spread = jnp.zeros(shape, f32)
    for at in range(4):
        moved = both if at == 0 else pltpu.roll(both, 128 - 32 * at, 1)
        spread = jnp.where(row % 4 == at, moved, spread)
    for at, part in enumerate(split(spread, 3)):
        moved = pltpu.roll(part.astype(f32), 32 * (at + 1), 1)
        tile = jnp.where(lane // 32 == at + 1, moved, tile)
    whole = jnp.concatenate([jac_ref[...].astype(f32), tile], axis=0).astype(bf16)
    out_ref[...] = jnp.broadcast_to(whole[None], out_ref.shape)


def pack(jac, dest, near_pose, prior2, devices):
    return pl.pallas_call(
        pack_kernel,
        out_shape=jax.ShapeDtypeStruct((devices, 16, 128), bf16),
        name="pack",
    )(jac, dest, near_pose, prior2)


def fill_kernel(place, sizes, prior_ref, out_ref, zeros, squares, sem, sem2):
    rows, cols = sizes
    region, column = place()
    pieces = rows // zeros.shape[0]
    zeros[...] = jnp.zeros_like(zeros)
    step = zeros.shape[0]
    copies = [
        pltpu.make_async_copy(zeros, out_ref.at[pl.ds(at * step, step), :], sem.at[at])
        for at in range(pieces)
    ]
    for copy in copies:
        copy.start()
    start = column * cols - region * rows
    own = (start >= 0) & (start < rows)

    @pl.when(own)
    def _():
        diagonal = iota((128, 128), 0) == iota((128, 128), 1)
        first = start // 128
        for at in range(cols // 128):
            squares[at] = jnp.where(diagonal, prior_ref[pl.ds(first + at, 1), :], 0.0)

    for copy in copies:
        copy.wait()

    @pl.when(own)
    def _():
        base = pl.multiple_of(start, 128)
        patches = [
            pltpu.make_async_copy(
                squares.at[at],
                out_ref.at[pl.ds(base + at * 128, 128), pl.ds(at * 128, 128)],
                sem2.at[at],
            )
            for at in range(cols // 128)
        ]
        for patch in patches:
            patch.start()
        for patch in patches:
            patch.wait()


def fill(place, rows, cols, prior2):
    step = min(256, rows)
    return pl.pallas_call(
        functools.partial(fill_kernel, place, (rows, cols)),
        out_shape=jax.ShapeDtypeStruct((rows, cols), f32),
        out_specs=pl.BlockSpec(memory_space=pl.ANY),
        scratch_shapes=[
            pltpu.VMEM((step, cols), f32),
            pltpu.VMEM((cols // 128, 128, 128), f32),
            pltpu.SemaphoreType.DMA((rows // step,)),
            pltpu.SemaphoreType.DMA((cols // 128,)),
        ],
        cost_estimate=pl.CostEstimate(flops=0, bytes_accessed=rows * cols * 4, transcendentals=0),
        name="fill",
    )(prior2)


def batched(left, right):
    out = []
    for k in range(8):
        total = left[0][k : k + 1, :] * right[0]
        for e in range(1, 8):
            total = total + left[e][k : k + 1, :] * right[e]
        out.append(total)
    return out


def slabs(block):
    return [block[8 * e : 8 * e + 8, :] for e in range(8)]


def to_columns(rows):
    full = jnp.concatenate([rows, jnp.zeros((120, CH), f32)], axis=0)
    return full.T


def cholesky(a):
    row = iota((8, 128), 0)
    columns, scales = [], []
    a = list(a)
    for j in range(8):
        pivot = a[j][j : j + 1, :]
        scale = lax.rsqrt(pivot)
        scale = scale * (1.5 - 0.5 * pivot * scale * scale)
        column = jnp.where(row >= j, a[j] * scale, 0.0)
        for k in range(j + 1, 8):
            a[k] = a[k] - column * column[k : k + 1, :]
        columns.append(column)
        scales.append(scale)
    inverse = []
    for i in range(8):
        x = jnp.where(row == i, 1.0, 0.0)
        for j in range(i, 8):
            value = x[j : j + 1, :] * scales[j]
            x = jnp.where(row == j, value, jnp.where(row > j, x - columns[j] * value, x))
        inverse.append(x)
    return columns, inverse


def loop(count, body):
    if count == 1:
        body(0)
    else:
        lax.fori_loop(0, count, lambda at, carry: (body(at), carry)[1], 0)


def assemble_kernel(place, sizes, got_ref, prior_ref, filled_ref, out_ref,
                    jt, rows_s, cols_s, app, bt, placed, tiles, keys, squares,
                    listing, info, list_sm, info_sm, extra_sm, sem_list, sem_info, sem_out, sem_sq):
    del filled_ref
    rows, cols, chunks = sizes
    row_poses, col_poses, groups = rows // 8, cols // 8, cols // 128
    region, column = place()
    region_f, column_f = region.astype(f32), column.astype(f32)
    start = column * cols - region * rows
    own = (start >= 0) & (start < rows)
    per = CH // 8

    at_row, at_lane = iota((64, 1024), 0), iota((64, 1024), 1)
    expand = jnp.where(
        (at_row // 8 == at_lane // 128) & (at_row % 8 == at_lane % 8), 1.0, 0.0
    ).astype(bf16)

    sent = got_ref[0].astype(f32)[8:16, :]
    lane8, row8 = iota((8, 128), 1), iota((8, 128), 0)
    panel_prior = jnp.zeros((8, 128), f32)
    for at in range(3):
        panel_prior = panel_prior + pltpu.roll(sent, 128 - 32 * (at + 1), 1)
    panel_prior = jnp.where(lane8 < 32, panel_prior, 0.0)
    lined = jnp.zeros((8, 128), f32)
    for at in range(4):
        moved = panel_prior if at == 0 else pltpu.roll(panel_prior, 32 * at, 1)
        lined = lined + jnp.where(row8 % 4 == at, moved, 0.0)
    halves = [
        jnp.sum(jnp.where(row8 < 4, lined, 0.0), axis=0, keepdims=True),
        jnp.sum(jnp.where(row8 >= 4, lined, 0.0), axis=0, keepdims=True),
    ]
    prior_row = jnp.concatenate(halves, axis=1)
    kl, unknown = iota((64, PANEL), 0), iota((64, PANEL), 1)
    diagonal = jnp.where((kl // 8 == kl % 8) & (unknown % 8 == kl % 8), prior_row, 0.0)
    own_pose = jnp.where(iota((PANEL, 128), 0) // 8 == iota((PANEL, 128), 1), 1.0, 0.0).astype(bf16)
    first = dot(jnp.concatenate(split(diagonal, 3), axis=0), own_pose)
    first = first[0:64] + first[64:128] + first[128:192]
    kl = iota((64, 128), 0)
    spare = (kl // 8 == kl % 8) & (iota((64, 128), 1) >= PP)
    app[...] = first + jnp.where(spare, 1.0, 0.0)

    def measure(a):
        block = got_ref[pl.ds(a * per, per)].astype(f32)
        jac = block[:, 0:8, :].reshape(CH, 128)
        label = block[:, 8:16, :].reshape(CH, 128)
        jac_t = jac.T
        label_t = label.T
        jt[a] = jac_t
        d0, n0, d1, n1 = (label_t[at : at + 1, :] for at in range(4))
        c0 = d0 * row_poses + n0 - column_f * col_poses
        c1 = d1 * row_poses + n1 - column_f * col_poses
        one, none = jnp.ones_like(d0), jnp.zeros_like(d0)
        row0, row1 = d0 == region_f, d1 == region_f
        col0, col1 = (c0 >= 0) & (c0 < col_poses), (c1 >= 0) & (c1 < col_poses)
        pan0, pan1 = (d0 == 0) & (n0 < PP), (d1 == 0) & (n1 < PP)
        has_row = jnp.where(row0 | row1, one, none)
        has_col = jnp.where(col0 | col1, one, none)
        touches = jnp.where(pan0 | pan1, one, none)
        row_pose = jnp.where(row0, n0, n1)
        col_pose = jnp.where(col0, c0, c1)
        row_side = jnp.where(row0, none, one)
        col_side = jnp.where(col0, none, one)
        pan_side = jnp.where(pan0, none, one)
        pan_pose = jnp.where(pan0, n0, n1)
        row_in_panel = jnp.where((row0 & pan0) | (row1 & pan1), one, none)
        col_in_panel = jnp.where((col0 & pan0) | (col1 & pan1), one, none)
        relevant = has_row * has_col * (1.0 - row_in_panel)
        group = jnp.floor(col_pose * (1.0 / 16.0))
        within = col_pose - group * 16.0
        code = row_pose * groups + group
        is_row = touches * has_row * (1.0 - row_in_panel)
        is_col = touches * has_col * (1.0 - col_in_panel)
        lines = [
            jnp.where(relevant > 0, code, -1.0),
            jnp.where(relevant > 0, code, -2.0),
            jnp.where(touches > 0, pan_pose, -1.0),
            jnp.where(is_row > 0, pan_pose, -1.0),
            jnp.where(is_col > 0, pan_pose, -2.0),
            within,
            row_pose,
            group,
        ]
        more = [
            row_side, col_side, pan_side, relevant, col_in_panel,
            is_row * is_col, col_pose, none,
        ]
        lines, more = jnp.concatenate(lines, axis=0), jnp.concatenate(more, axis=0)
        rows_s[a] = jnp.concatenate([lines, more], axis=0)
        columns = to_columns(lines)
        cols_s[a] = columns
        j0, j1 = slabs(jac_t[0:64, :]), slabs(jac_t[64:128, :])
        near = [jnp.where(pan_side == 0, x, y) for x, y in zip(j0, j1)]
        gram = jnp.concatenate(batched(near, near), axis=0)
        of_pose = jnp.where(
            columns[:, 2:3] == iota((CH, 128), 1).astype(f32), 1.0, 0.0
        ).astype(bf16)
        total = dot(jnp.concatenate(split(gram, 3), axis=0), of_pose)
        app[...] += total[0:64] + total[64:128] + total[128:192]

    loop(chunks, measure)

    factor, inverse = cholesky(slabs(app[...]))
    factor = jnp.concatenate(factor, axis=0)
    inverse = jnp.concatenate(split(jnp.concatenate(inverse, axis=0), 3), axis=0)

    @pl.when((region == 0) & (column == 0))
    def _():
        swap = jnp.where(
            (at_row % 8 == at_lane // 128) & (at_row // 8 == at_lane % 8), 1.0, 0.0
        ).astype(bf16)
        full = jnp.concatenate([factor, jnp.zeros((64, 128), f32)], axis=0).T
        parts = [dot(part[0:PP, 0:64], swap) for part in split(full, 3)]
        value = parts[0] + parts[1] + parts[2]
        keep = iota((PP, 128), 1) // 8 == iota((PP, 128), 0) % 16
        for k in range(8):
            squares[pl.ds(k, PP, stride=8), :] = jnp.where(
                keep, value[:, 128 * k : 128 * k + 128], 0.0
            )
        for at in range(K_PANELS):
            piece = pl.ds(at * 128, 128)
            copy = pltpu.make_async_copy(
                squares.at[piece, :], out_ref.at[piece, piece], sem_sq.at[at]
            )
            copy.start()

    def blocks(a):
        row = [rows_s[a, at : at + 1, :] for at in range(16)]
        jac_t = jt[a]
        j0, j1 = slabs(jac_t[0:64, :]), slabs(jac_t[64:128, :])
        left = [jnp.where(row[8] == 0, x, y) for x, y in zip(j0, j1)]
        right = [jnp.where(row[9] == 0, x, y) for x, y in zip(j0, j1)]
        near = [jnp.where(row[10] == 0, x, y) for x, y in zip(j0, j1)]
        far = [jnp.where(row[10] == 0, y, x) for x, y in zip(j0, j1)]
        gram = batched(left, right)
        cross = batched(near, far)
        of_pose = jnp.where(iota((128, CH), 0).astype(f32) == row[2], 1.0, 0.0).astype(bf16)
        inv = dot(inverse, of_pose)
        inv = slabs(inv[0:64] + inv[64:128] + inv[128:192])
        solved = []
        for j in range(8):
            total = inv[0][j : j + 1, :] * cross[0]
            for i in range(1, j + 1):
                total = total + inv[i][j : j + 1, :] * cross[i]
            solved.append(total)
        bt[a] = jnp.concatenate(solved, axis=0)
        outer = batched(solved, solved)
        normal = [g - o * row[13] for g, o in zip(gram, outer)]
        keep_normal = row[11] * (1.0 - row[12])
        keep_panel = row[11] * row[12]
        normal = jnp.concatenate([x * keep_normal for x in normal], axis=0)
        panel = jnp.concatenate([x * keep_panel for x in solved], axis=0)
        both = jnp.concatenate([normal, panel], axis=0).T
        at_row2, at_lane2 = iota((128, 1024), 0), iota((128, 1024), 1)
        inner = at_row2 % 64
        straight = (inner // 8 == at_lane2 // 128) & (inner % 8 == at_lane2 % 8)
        turned = (inner % 8 == at_lane2 // 128) & (inner // 8 == at_lane2 % 8)
        table = jnp.where(
            ((at_row2 < 64) & straight) | ((at_row2 >= 64) & turned), 1.0, 0.0
        ).astype(bf16)
        columns = cols_s[a]
        keep = jnp.where((iota((CH, 128), 1) // 8).astype(f32) == columns[:, 5:6], 1.0, 0.0)
        keep = jnp.concatenate([keep] * 8, axis=1).astype(bf16)
        for at, part in enumerate(split(both, 2)):
            placed[a, at] = dot(part, table).astype(bf16) * keep

    loop(chunks, blocks)

    def merge(a):
        columns = cols_s[a]
        codes = jnp.broadcast_to(columns[:, 0:1], (CH, CH))
        line = rows_s[a]
        tiles_at = a * CH * 8
        before = iota((CH, CH), 0) < iota((CH, CH), 1)

        def from_chunk(b, repeats):
            same = jnp.where(codes == rows_s[b, 1:2, :], 1.0, 0.0).astype(bf16)
            total = dot(same, placed[b, 0]) + dot(same, placed[b, 1])
            other = jnp.broadcast_to(cols_s[b, :, 0:1], (CH, CH))
            earlier = jnp.where(other == line[1:2, :], 1.0, 0.0)
            if chunks == 1:
                earlier = jnp.where(before, earlier, 0.0)
            else:
                here = jnp.where(before, earlier, 0.0)
                factor_here = jnp.where(b == a, 1.0, 0.0)
                factor_all = jnp.where(b < a, 1.0, 0.0)
                earlier = here * factor_here + earlier * factor_all
            return total, repeats + jnp.sum(earlier, axis=0, keepdims=True)

        repeats = jnp.zeros((1, CH), f32)
        if chunks == 1:
            total, repeats = from_chunk(0, repeats)
        else:
            def step(b, carry):
                total, found = from_chunk(b, carry[1])
                return carry[0] + total, found
            total, repeats = lax.fori_loop(
                0, chunks, step, (jnp.zeros((CH, 1024), f32), repeats)
            )
        kept = jnp.where(repeats == 0, line[11:12, :], 0.0)
        upper = jnp.where(before, 1.0, 0.0).astype(bf16)
        rank = dot(jnp.broadcast_to(kept, (16, CH)).astype(bf16), upper)[0:1, :]
        chosen = jnp.where(
            (rank == iota((CH, CH), 0).astype(f32)) & (kept > 0), 1.0, 0.0
        ).astype(bf16)
        position = iota((1, CH), 1).astype(f32)
        data = jnp.concatenate(
            [line[6:7, :], line[7:8, :], position, jnp.zeros((13, CH), f32)], axis=0
        ).astype(bf16)
        found = dot(data, chosen, ((1,), (1,)))[0:8, :]
        count = jnp.sum(kept, axis=1, keepdims=True)
        row_at = iota((8, CH), 0)
        listing[a] = jnp.where(row_at == 3, count, found).astype(i32)
        pltpu.make_async_copy(listing.at[a], list_sm.at[a], sem_list.at[a]).start()
        info[a] = jnp.where(
            row_at == 0, line[6:7, :], jnp.where(row_at == 1, line[14:15, :], 0.0)
        ).astype(i32)
        pltpu.make_async_copy(info.at[a], info_sm.at[a], sem_info.at[a]).start()
        first_row = jnp.where(own, start // 128, 0)
        local = prior_ref[pl.ds(first_row, groups), :]
        share = jnp.where(own, 1.0, 0.0)
        group_of = columns[:, 7:8]
        base = jnp.zeros((CH, 128), f32)
        for at in range(groups):
            base = jnp.where(group_of == float(at), local[at : at + 1, :], base)
        base = base * share
        lane = iota((CH, 128), 1).astype(f32)
        offset = columns[:, 5:6] * 8.0
        for k in range(8):
            value = total[:, 128 * k : 128 * k + 128]
            value = value + jnp.where(lane == offset + float(k), base, 0.0)
            tiles[pl.ds(tiles_at + k, CH, stride=8), :] = value

    loop(chunks, merge)

    def waiting(a):
        pltpu.make_async_copy(listing.at[a], list_sm.at[a], sem_list.at[a]).wait()
        pltpu.make_async_copy(info.at[a], info_sm.at[a], sem_info.at[a]).wait()

    loop(chunks, waiting)

    lane_tile = iota((8, 128), 1)
    extra_sm[0] = 0

    def pairs(index):
        a, b = (0, 0) if chunks == 1 else (index // chunks, index % chunks)
        left = jnp.broadcast_to(cols_s[a, :, 3:4], (CH, CH))
        valid = left == rows_s[b, 4:5, :]
        same = iota((CH, CH), 0) == iota((CH, CH), 1)
        if chunks == 1:
            valid = valid & jnp.logical_not(same)
        else:
            valid = valid & jnp.logical_not(same & (a == b))
        key = (iota((CH, CH), 0) * CH + iota((CH, CH), 1)).astype(f32)
        key = jnp.where(valid, key, BIG)
        keys[...] = key
        smallest = jnp.min(key)

        def more(key_now):
            return key_now < BIG

        def one(key_now):
            number = key_now.astype(i32)
            m1, m2 = number // CH, number % CH
            r1, c2 = info_sm[a, 0, m1], info_sm[b, 1, m2]
            group, within = c2 // 16, c2 % 16
            position = iota((8, CH), 1)
            total = jnp.zeros((8, 128), f32)
            for j in range(8):
                x = bt[a, 8 * j : 8 * j + 8, :]
                y = bt[b, 8 * j : 8 * j + 8, :]
                x = jnp.sum(jnp.where(position == m1, x, 0.0), axis=1, keepdims=True)
                y = jnp.sum(jnp.where(position == m2, y, 0.0), axis=1, keepdims=True)
                y = jnp.where(lane_tile % 8 == row8, y, 0.0)
                y = jnp.sum(y, axis=0, keepdims=True)
                total = total + x * y
            total = jnp.where(lane_tile // 8 == within, -total, 0.0)

            def search(chunk, carry):
                def at_one(at, slot):
                    hit = (list_sm[chunk, 0, at] == r1) & (list_sm[chunk, 1, at] == group)
                    return jnp.where(hit, chunk * CH + list_sm[chunk, 2, at], slot)
                return lax.fori_loop(0, list_sm[chunk, 3, 0], at_one, carry)

            slot = search(0, -1) if chunks == 1 else lax.fori_loop(0, chunks, search, -1)
            added = extra_sm[0]
            code = r1 * groups + group

            def at_extra(at, slot):
                return jnp.where(extra_sm[1 + at] == code, chunks * CH + at, slot)

            slot = lax.fori_loop(0, added, at_extra, slot)

            @pl.when(slot >= 0)
            def _():
                where = pl.ds(pl.multiple_of(slot * 8, 8), 8)
                tiles[where, :] = tiles[where, :] + total

            @pl.when(slot < 0)
            def _():
                where = pl.ds(pl.multiple_of((chunks * CH + added) * 8, 8), 8)
                tiles[where, :] = total
                extra_sm[1 + added] = code
                extra_sm[0] = added + 1

            return jnp.min(jnp.where(keys[...] > key_now, keys[...], BIG))

        lax.while_loop(more, one, smallest)

    loop(chunks * chunks, pairs)

    def tile_copy(slot, r, group):
        return pltpu.make_async_copy(
            tiles.at[pl.ds(pl.multiple_of(slot * 8, 8), 8), :],
            out_ref.at[pl.ds(pl.multiple_of(r * 8, 8), 8), pl.ds(pl.multiple_of(group * 128, 128), 128)],
            sem_out,
        )

    def send(a):
        def one(at, carry):
            tile_copy(a * CH + list_sm[a, 2, at], list_sm[a, 0, at], list_sm[a, 1, at]).start()
            return carry
        lax.fori_loop(0, list_sm[a, 3, 0], one, 0)

    loop(chunks, send)

    def send_extra(at, carry):
        code = extra_sm[1 + at]
        tile_copy(chunks * CH + at, code // groups, code % groups).start()
        return carry

    lax.fori_loop(0, extra_sm[0], send_extra, 0)

    def drain_one(at, carry):
        tile_copy(0, 0, 0).wait()
        return carry

    def drain(a):
        lax.fori_loop(0, list_sm[a, 3, 0], drain_one, 0)

    loop(chunks, drain)
    lax.fori_loop(0, extra_sm[0], drain_one, 0)

    @pl.when((region == 0) & (column == 0))
    def _():
        for at in range(K_PANELS):
            piece = pl.ds(at * 128, 128)
            pltpu.make_async_copy(
                squares.at[piece, :], out_ref.at[piece, piece], sem_sq.at[at]
            ).wait()


def assemble(place, rows, cols, got, prior2, filled):
    count = got.shape[0] * 8
    chunks = count // CH
    capacity = rows // 8 * (cols // 128)
    any_space = pl.BlockSpec(memory_space=pl.ANY)
    vmem = pl.BlockSpec(memory_space=pltpu.VMEM)
    return pl.pallas_call(
        functools.partial(assemble_kernel, place, (rows, cols, chunks)),
        out_shape=jax.ShapeDtypeStruct((rows, cols), f32),
        in_specs=[vmem, vmem, any_space],
        out_specs=any_space,
        scratch_shapes=[
            pltpu.VMEM((chunks, 128, CH), f32),
            pltpu.VMEM((chunks, 16, CH), f32),
            pltpu.VMEM((chunks, CH, 128), f32),
            pltpu.VMEM((64, 128), f32),
            pltpu.VMEM((chunks, 64, CH), f32),
            pltpu.VMEM((chunks, 2, CH, 1024), bf16),
            pltpu.VMEM(((count + capacity) * 8, 128), f32),
            pltpu.VMEM((CH, CH), f32),
            pltpu.VMEM((PANEL, 128), f32),
            pltpu.VMEM((chunks, 8, CH), i32),
            pltpu.VMEM((chunks, 8, CH), i32),
            pltpu.SMEM((chunks, 8, CH), i32),
            pltpu.SMEM((chunks, 8, CH), i32),
            pltpu.SMEM((1 + capacity,), i32),
            pltpu.SemaphoreType.DMA((chunks,)),
            pltpu.SemaphoreType.DMA((chunks,)),
            pltpu.SemaphoreType.DMA,
            pltpu.SemaphoreType.DMA((K_PANELS,)),
        ],
        input_output_aliases={2: 0},
        compiler_params=pltpu.CompilerParams(vmem_limit_bytes=48 << 20),
        name="assemble",
    )(got, prior2, filled)


def place():
    return lax.axis_index("region"), lax.axis_index("col")


def body(jac, dest, near_pose, prior):
    regions, columns = lax.axis_size("region"), lax.axis_size("col")
    devices = regions * columns
    rows = prior.shape[0]
    cols = rows * regions // columns
    assert jac.shape[0] == 8 and devices * 8 % CH == 0
    assert rows % cols == 0 and rows // 8 <= 256 and regions <= 256
    assert rows >= PANEL and cols >= PANEL and cols % 128 == 0
    prior2 = prior.reshape(rows // 128, 128)
    packed = pack(jac, dest, near_pose, prior2, devices)
    got = lax.all_to_all(packed, ("region", "col"), split_axis=0, concat_axis=0, tiled=True)
    filled = fill(place, rows, cols, prior2)
    return assemble(place, rows, cols, got, prior2, filled)


def solution(mesh):
    return jax.shard_map(
        body,
        mesh=mesh,
        in_specs=(
            P(("region", "col"), None),
            P(("region", "col"), None),
            P(("region", "col"), None),
            P("region"),
        ),
        out_specs=P("region", "col"),
        check_vma=False,
    )
```

```python
import functools

import jax
import jax.numpy as jnp
from jax import lax
from jax.experimental import pallas as pl
from jax.experimental.pallas import tpu as pltpu
from jax.sharding import PartitionSpec as P

NB = 128
K_PANELS = 2
PANEL = NB * K_PANELS
PP = PANEL // 8
CH = 256
BIG = float(1 << 24)
f32, bf16, i32 = jnp.float32, jnp.bfloat16, jnp.int32


def iota(shape, dim):
    return lax.broadcasted_iota(i32, shape, dim)


def split(x, parts):
    out = []
    for _ in range(parts):
        top = x.astype(bf16)
        out.append(top)
        x = x - top.astype(f32)
    return out


def dot(a, b, dims=((1,), (0,))):
    return lax.dot_general(a, b, (dims, ((), ())), preferred_element_type=f32)


def pack_kernel(jac_ref, dest_ref, near_ref, prior_ref, out_ref):
    shape = (8, 128)
    lane, row = iota(shape, 1), iota(shape, 0)
    dest, near = dest_ref[...].astype(f32), near_ref[...].astype(f32)
    tile = jnp.zeros(shape, f32)
    corner = iota((8, 8), 0) == iota((8, 8), 1)
    for at, line in enumerate((dest[0:1, :], near[0:1, :], dest[1:2, :], near[1:2, :])):
        column = jnp.sum(jnp.where(corner, line, 0.0), axis=1, keepdims=True)
        tile = jnp.where(lane == at, column, tile)
    first = prior_ref[0:2, :]
    both = jnp.where(row < 4, first[0:1, :], first[1:2, :])
    spread = jnp.zeros(shape, f32)
    for at in range(4):
        moved = both if at == 0 else pltpu.roll(both, 128 - 32 * at, 1)
        spread = jnp.where(row % 4 == at, moved, spread)
    for at, part in enumerate(split(spread, 3)):
        moved = pltpu.roll(part.astype(f32), 32 * (at + 1), 1)
        tile = jnp.where(lane // 32 == at + 1, moved, tile)
    whole = jnp.concatenate([jac_ref[...].astype(f32), tile], axis=0).astype(bf16)
    out_ref[...] = jnp.broadcast_to(whole[None], out_ref.shape)


def pack(jac, dest, near_pose, prior2, devices):
    return pl.pallas_call(
        pack_kernel,
        out_shape=jax.ShapeDtypeStruct((devices, 16, 128), bf16),
        in_specs=[pl.BlockSpec(memory_space=pltpu.VMEM)] * 4,
        out_specs=pl.BlockSpec(memory_space=pltpu.VMEM),
        name="pack",
    )(jac, dest.T, near_pose.T, prior2)


def fill_kernel(place, sizes, prior_ref, out_ref, zeros, squares, sem, sem2):
    rows, cols = sizes
    region, column = place()
    pieces = rows // zeros.shape[0]
    zeros[...] = jnp.zeros_like(zeros)
    step = zeros.shape[0]
    copies = [
        pltpu.make_async_copy(zeros, out_ref.at[pl.ds(at * step, step), :], sem.at[at])
        for at in range(pieces)
    ]
    for copy in copies:
        copy.start()
    start = column * cols - region * rows
    own = (start >= 0) & (start < rows)

    @pl.when(own)
    def _():
        diagonal = iota((128, 128), 0) == iota((128, 128), 1)
        first = start // 128
        for at in range(cols // 128):
            squares[at] = jnp.where(diagonal, prior_ref[pl.ds(first + at, 1), :], 0.0)

    for copy in copies:
        copy.wait()

    @pl.when(own)
    def _():
        base = pl.multiple_of(start, 128)
        patches = [
            pltpu.make_async_copy(
                squares.at[at],
                out_ref.at[pl.ds(base + at * 128, 128), pl.ds(at * 128, 128)],
                sem2.at[at],
            )
            for at in range(cols // 128)
        ]
        for patch in patches:
            patch.start()
        for patch in patches:
            patch.wait()


def fill(place, rows, cols, prior2):
    step = min(256, rows)
    return pl.pallas_call(
        functools.partial(fill_kernel, place, (rows, cols)),
        out_shape=jax.ShapeDtypeStruct((rows, cols), f32),
        out_specs=pl.BlockSpec(memory_space=pl.ANY),
        scratch_shapes=[
            pltpu.VMEM((step, cols), f32),
            pltpu.VMEM((cols // 128, 128, 128), f32),
            pltpu.SemaphoreType.DMA((rows // step,)),
            pltpu.SemaphoreType.DMA((cols // 128,)),
        ],
        cost_estimate=pl.CostEstimate(flops=0, bytes_accessed=rows * cols * 4, transcendentals=0),
        name="fill",
    )(prior2)


def batched(left, right):
    out = []
    for k in range(8):
        total = left[0][k : k + 1, :] * right[0]
        for e in range(1, 8):
            total = total + left[e][k : k + 1, :] * right[e]
        out.append(total)
    return out


def slabs(block):
    return [block[8 * e : 8 * e + 8, :] for e in range(8)]


def to_columns(rows):
    full = jnp.concatenate([rows, jnp.zeros((120, CH), f32)], axis=0)
    return full.T


def cholesky(a):
    row = iota((8, 128), 0)
    columns, scales = [], []
    a = list(a)
    for j in range(8):
        pivot = a[j][j : j + 1, :]
        scale = lax.rsqrt(pivot)
        scale = scale * (1.5 - 0.5 * pivot * scale * scale)
        column = jnp.where(row >= j, a[j] * scale, 0.0)
        for k in range(j + 1, 8):
            a[k] = a[k] - column * column[k : k + 1, :]
        columns.append(column)
        scales.append(scale)
    inverse = []
    for i in range(8):
        x = jnp.where(row == i, 1.0, 0.0)
        for j in range(i, 8):
            value = x[j : j + 1, :] * scales[j]
            x = jnp.where(row == j, value, jnp.where(row > j, x - columns[j] * value, x))
        inverse.append(x)
    return columns, inverse


def loop(count, body):
    if count == 1:
        body(0)
    else:
        lax.fori_loop(0, count, lambda at, carry: (body(at), carry)[1], 0)


def assemble_kernel(place, sizes, got_ref, prior_ref, filled_ref, out_ref,
                    jt, rows_s, cols_s, app, bt, placed, tiles, keys, squares,
                    listing, info, list_sm, info_sm, extra_sm, sem_list, sem_info, sem_out, sem_sq):
    del filled_ref
    rows, cols, chunks = sizes
    row_poses, col_poses, groups = rows // 8, cols // 8, cols // 128
    region, column = place()
    region_f, column_f = region.astype(f32), column.astype(f32)
    start = column * cols - region * rows
    own = (start >= 0) & (start < rows)
    per = CH // 8

    at_row, at_lane = iota((64, 1024), 0), iota((64, 1024), 1)
    expand = jnp.where(
        (at_row // 8 == at_lane // 128) & (at_row % 8 == at_lane % 8), 1.0, 0.0
    ).astype(bf16)

    sent = got_ref[0].astype(f32)[8:16, :]
    lane8, row8 = iota((8, 128), 1), iota((8, 128), 0)
    panel_prior = jnp.zeros((8, 128), f32)
    for at in range(3):
        panel_prior = panel_prior + pltpu.roll(sent, 128 - 32 * (at + 1), 1)
    panel_prior = jnp.where(lane8 < 32, panel_prior, 0.0)
    lined = jnp.zeros((8, 128), f32)
    for at in range(4):
        moved = panel_prior if at == 0 else pltpu.roll(panel_prior, 32 * at, 1)
        lined = lined + jnp.where(row8 % 4 == at, moved, 0.0)
    halves = [
        jnp.sum(jnp.where(row8 < 4, lined, 0.0), axis=0, keepdims=True),
        jnp.sum(jnp.where(row8 >= 4, lined, 0.0), axis=0, keepdims=True),
    ]
    prior_row = jnp.concatenate(halves, axis=1)
    kl, unknown = iota((64, PANEL), 0), iota((64, PANEL), 1)
    diagonal = jnp.where((kl // 8 == kl % 8) & (unknown % 8 == kl % 8), prior_row, 0.0)
    own_pose = jnp.where(iota((PANEL, 128), 0) // 8 == iota((PANEL, 128), 1), 1.0, 0.0).astype(bf16)
    first = dot(jnp.concatenate(split(diagonal, 3), axis=0), own_pose)
    first = first[0:64] + first[64:128] + first[128:192]
    kl = iota((64, 128), 0)
    spare = (kl // 8 == kl % 8) & (iota((64, 128), 1) >= PP)
    app[...] = first + jnp.where(spare, 1.0, 0.0)

    def measure(a):
        block = got_ref[pl.ds(a * per, per)].astype(f32)
        jac = block[:, 0:8, :].reshape(CH, 128)
        label = block[:, 8:16, :].reshape(CH, 128)
        jac_t = jac.T
        label_t = label.T
        jt[a] = jac_t
        d0, n0, d1, n1 = (label_t[at : at + 1, :] for at in range(4))
        c0 = d0 * row_poses + n0 - column_f * col_poses
        c1 = d1 * row_poses + n1 - column_f * col_poses
        one, none = jnp.ones_like(d0), jnp.zeros_like(d0)
        row0, row1 = d0 == region_f, d1 == region_f
        col0, col1 = (c0 >= 0) & (c0 < col_poses), (c1 >= 0) & (c1 < col_poses)
        pan0, pan1 = (d0 == 0) & (n0 < PP), (d1 == 0) & (n1 < PP)
        has_row = jnp.where(row0 | row1, one, none)
        has_col = jnp.where(col0 | col1, one, none)
        touches = jnp.where(pan0 | pan1, one, none)
        row_pose = jnp.where(row0, n0, n1)
        col_pose = jnp.where(col0, c0, c1)
        row_side = jnp.where(row0, none, one)
        col_side = jnp.where(col0, none, one)
        pan_side = jnp.where(pan0, none, one)
        pan_pose = jnp.where(pan0, n0, n1)
        row_in_panel = jnp.where((row0 & pan0) | (row1 & pan1), one, none)
        col_in_panel = jnp.where((col0 & pan0) | (col1 & pan1), one, none)
        relevant = has_row * has_col * (1.0 - row_in_panel)
        group = jnp.floor(col_pose * (1.0 / 16.0))
        within = col_pose - group * 16.0
        code = row_pose * groups + group
        is_row = touches * has_row * (1.0 - row_in_panel)
        is_col = touches * has_col * (1.0 - col_in_panel)
        lines = [
            jnp.where(relevant > 0, code, -1.0),
            jnp.where(relevant > 0, code, -2.0),
            jnp.where(touches > 0, pan_pose, -1.0),
            jnp.where(is_row > 0, pan_pose, -1.0),
            jnp.where(is_col > 0, pan_pose, -2.0),
            within,
            row_pose,
            group,
        ]
        more = [
            row_side, col_side, pan_side, relevant, col_in_panel,
            is_row * is_col, col_pose, none,
        ]
        lines, more = jnp.concatenate(lines, axis=0), jnp.concatenate(more, axis=0)
        rows_s[a] = jnp.concatenate([lines, more], axis=0)
        columns = to_columns(lines)
        cols_s[a] = columns
        j0, j1 = slabs(jac_t[0:64, :]), slabs(jac_t[64:128, :])
        near = [jnp.where(pan_side == 0, x, y) for x, y in zip(j0, j1)]
        gram = jnp.concatenate(batched(near, near), axis=0)
        of_pose = jnp.where(
            columns[:, 2:3] == iota((CH, 128), 1).astype(f32), 1.0, 0.0
        ).astype(bf16)
        total = dot(jnp.concatenate(split(gram, 3), axis=0), of_pose)
        app[...] += total[0:64] + total[64:128] + total[128:192]

    loop(chunks, measure)

    factor, inverse = cholesky(slabs(app[...]))
    factor = jnp.concatenate(factor, axis=0)
    inverse = jnp.concatenate(split(jnp.concatenate(inverse, axis=0), 3), axis=0)

    @pl.when((region == 0) & (column == 0))
    def _():
        swap = jnp.where(
            (at_row % 8 == at_lane // 128) & (at_row // 8 == at_lane % 8), 1.0, 0.0
        ).astype(bf16)
        full = jnp.concatenate([factor, jnp.zeros((64, 128), f32)], axis=0).T
        parts = [dot(part[0:PP, 0:64], swap) for part in split(full, 3)]
        value = parts[0] + parts[1] + parts[2]
        keep = iota((PP, 128), 1) // 8 == iota((PP, 128), 0) % 16
        for k in range(8):
            squares[pl.ds(k, PP, stride=8), :] = jnp.where(
                keep, value[:, 128 * k : 128 * k + 128], 0.0
            )
        for at in range(K_PANELS):
            piece = pl.ds(at * 128, 128)
            copy = pltpu.make_async_copy(
                squares.at[piece, :], out_ref.at[piece, piece], sem_sq.at[at]
            )
            copy.start()

    def blocks(a):
        row = [rows_s[a, at : at + 1, :] for at in range(16)]
        jac_t = jt[a]
        j0, j1 = slabs(jac_t[0:64, :]), slabs(jac_t[64:128, :])
        left = [jnp.where(row[8] == 0, x, y) for x, y in zip(j0, j1)]
        right = [jnp.where(row[9] == 0, x, y) for x, y in zip(j0, j1)]
        near = [jnp.where(row[10] == 0, x, y) for x, y in zip(j0, j1)]
        far = [jnp.where(row[10] == 0, y, x) for x, y in zip(j0, j1)]
        gram = batched(left, right)
        cross = batched(near, far)
        of_pose = jnp.where(iota((128, CH), 0).astype(f32) == row[2], 1.0, 0.0).astype(bf16)
        inv = dot(inverse, of_pose)
        inv = slabs(inv[0:64] + inv[64:128] + inv[128:192])
        solved = []
        for j in range(8):
            total = inv[0][j : j + 1, :] * cross[0]
            for i in range(1, j + 1):
                total = total + inv[i][j : j + 1, :] * cross[i]
            solved.append(total)
        bt[a] = jnp.concatenate(solved, axis=0)
        outer = batched(solved, solved)
        normal = [g - o * row[13] for g, o in zip(gram, outer)]
        keep_normal = row[11] * (1.0 - row[12])
        keep_panel = row[11] * row[12]
        normal = jnp.concatenate([x * keep_normal for x in normal], axis=0)
        panel = jnp.concatenate([x * keep_panel for x in solved], axis=0)
        both = jnp.concatenate([normal, panel], axis=0).T
        at_row2, at_lane2 = iota((128, 1024), 0), iota((128, 1024), 1)
        inner = at_row2 % 64
        straight = (inner // 8 == at_lane2 // 128) & (inner % 8 == at_lane2 % 8)
        turned = (inner % 8 == at_lane2 // 128) & (inner // 8 == at_lane2 % 8)
        table = jnp.where(
            ((at_row2 < 64) & straight) | ((at_row2 >= 64) & turned), 1.0, 0.0
        ).astype(bf16)
        columns = cols_s[a]
        keep = jnp.where((iota((CH, 128), 1) // 8).astype(f32) == columns[:, 5:6], 1.0, 0.0)
        keep = jnp.concatenate([keep] * 8, axis=1).astype(bf16)
        for at, part in enumerate(split(both, 2)):
            placed[a, at] = dot(part, table).astype(bf16) * keep

    loop(chunks, blocks)

    def merge(a):
        columns = cols_s[a]
        codes = jnp.broadcast_to(columns[:, 0:1], (CH, CH))
        line = rows_s[a]
        tiles_at = a * CH * 8
        before = iota((CH, CH), 0) < iota((CH, CH), 1)

        def from_chunk(b, repeats):
            same = jnp.where(codes == rows_s[b, 1:2, :], 1.0, 0.0).astype(bf16)
            total = dot(same, placed[b, 0]) + dot(same, placed[b, 1])
            other = jnp.broadcast_to(cols_s[b, :, 0:1], (CH, CH))
            earlier = jnp.where(other == line[1:2, :], 1.0, 0.0)
            if chunks == 1:
                earlier = jnp.where(before, earlier, 0.0)
            else:
                here = jnp.where(before, earlier, 0.0)
                factor_here = jnp.where(b == a, 1.0, 0.0)
                factor_all = jnp.where(b < a, 1.0, 0.0)
                earlier = here * factor_here + earlier * factor_all
            return total, repeats + jnp.sum(earlier, axis=0, keepdims=True)

        repeats = jnp.zeros((1, CH), f32)
        if chunks == 1:
            total, repeats = from_chunk(0, repeats)
        else:
            def step(b, carry):
                total, found = from_chunk(b, carry[1])
                return carry[0] + total, found
            total, repeats = lax.fori_loop(
                0, chunks, step, (jnp.zeros((CH, 1024), f32), repeats)
            )
        kept = jnp.where(repeats == 0, line[11:12, :], 0.0)
        upper = jnp.where(before, 1.0, 0.0).astype(bf16)
        rank = dot(jnp.broadcast_to(kept, (16, CH)).astype(bf16), upper)[0:1, :]
        chosen = jnp.where(
            (rank == iota((CH, CH), 0).astype(f32)) & (kept > 0), 1.0, 0.0
        ).astype(bf16)
        position = iota((1, CH), 1).astype(f32)
        data = jnp.concatenate(
            [line[6:7, :], line[7:8, :], position, jnp.zeros((13, CH), f32)], axis=0
        ).astype(bf16)
        found = dot(data, chosen, ((1,), (1,)))[0:8, :]
        count = jnp.sum(kept, axis=1, keepdims=True)
        row_at = iota((8, CH), 0)
        listing[a] = jnp.where(row_at == 3, count, found).astype(i32)
        pltpu.make_async_copy(listing.at[a], list_sm.at[a], sem_list.at[a]).start()
        info[a] = jnp.where(
            row_at == 0, line[6:7, :], jnp.where(row_at == 1, line[14:15, :], 0.0)
        ).astype(i32)
        pltpu.make_async_copy(info.at[a], info_sm.at[a], sem_info.at[a]).start()
        first_row = jnp.where(own, start // 128, 0)
        local = prior_ref[pl.ds(first_row, groups), :]
        share = jnp.where(own, 1.0, 0.0)
        group_of = columns[:, 7:8]
        base = jnp.zeros((CH, 128), f32)
        for at in range(groups):
            base = jnp.where(group_of == float(at), local[at : at + 1, :], base)
        base = base * share
        lane = iota((CH, 128), 1).astype(f32)
        offset = columns[:, 5:6] * 8.0
        for k in range(8):
            value = total[:, 128 * k : 128 * k + 128]
            value = value + jnp.where(lane == offset + float(k), base, 0.0)
            tiles[pl.ds(tiles_at + k, CH, stride=8), :] = value

    loop(chunks, merge)

    def waiting(a):
        pltpu.make_async_copy(listing.at[a], list_sm.at[a], sem_list.at[a]).wait()
        pltpu.make_async_copy(info.at[a], info_sm.at[a], sem_info.at[a]).wait()

    loop(chunks, waiting)

    lane_tile = iota((8, 128), 1)
    extra_sm[0] = 0

    def pairs(index):
        a, b = (0, 0) if chunks == 1 else (index // chunks, index % chunks)
        left = jnp.broadcast_to(cols_s[a, :, 3:4], (CH, CH))
        valid = left == rows_s[b, 4:5, :]
        same = iota((CH, CH), 0) == iota((CH, CH), 1)
        if chunks == 1:
            valid = valid & jnp.logical_not(same)
        else:
            valid = valid & jnp.logical_not(same & (a == b))
        key = (iota((CH, CH), 0) * CH + iota((CH, CH), 1)).astype(f32)
        key = jnp.where(valid, key, BIG)
        keys[...] = key
        smallest = jnp.min(key)

        def more(key_now):
            return key_now < BIG

        def one(key_now):
            number = key_now.astype(i32)
            m1, m2 = number // CH, number % CH
            r1, c2 = info_sm[a, 0, m1], info_sm[b, 1, m2]
            group, within = c2 // 16, c2 % 16
            position = iota((8, CH), 1)
            total = jnp.zeros((8, 128), f32)
            for j in range(8):
                x = bt[a, 8 * j : 8 * j + 8, :]
                y = bt[b, 8 * j : 8 * j + 8, :]
                x = jnp.sum(jnp.where(position == m1, x, 0.0), axis=1, keepdims=True)
                y = jnp.sum(jnp.where(position == m2, y, 0.0), axis=1, keepdims=True)
                y = jnp.where(lane_tile % 8 == row8, y, 0.0)
                y = jnp.sum(y, axis=0, keepdims=True)
                total = total + x * y
            total = jnp.where(lane_tile // 8 == within, -total, 0.0)

            def search(chunk, carry):
                def at_one(at, slot):
                    hit = (list_sm[chunk, 0, at] == r1) & (list_sm[chunk, 1, at] == group)
                    return jnp.where(hit, chunk * CH + list_sm[chunk, 2, at], slot)
                return lax.fori_loop(0, list_sm[chunk, 3, 0], at_one, carry)

            slot = search(0, -1) if chunks == 1 else lax.fori_loop(0, chunks, search, -1)
            added = extra_sm[0]
            code = r1 * groups + group

            def at_extra(at, slot):
                return jnp.where(extra_sm[1 + at] == code, chunks * CH + at, slot)

            slot = lax.fori_loop(0, added, at_extra, slot)

            @pl.when(slot >= 0)
            def _():
                where = pl.ds(pl.multiple_of(slot * 8, 8), 8)
                tiles[where, :] = tiles[where, :] + total

            @pl.when(slot < 0)
            def _():
                where = pl.ds(pl.multiple_of((chunks * CH + added) * 8, 8), 8)
                tiles[where, :] = total
                extra_sm[1 + added] = code
                extra_sm[0] = added + 1

            return jnp.min(jnp.where(keys[...] > key_now, keys[...], BIG))

        lax.while_loop(more, one, smallest)

    loop(chunks * chunks, pairs)

    def tile_copy(slot, r, group):
        return pltpu.make_async_copy(
            tiles.at[pl.ds(pl.multiple_of(slot * 8, 8), 8), :],
            out_ref.at[pl.ds(pl.multiple_of(r * 8, 8), 8), pl.ds(pl.multiple_of(group * 128, 128), 128)],
            sem_out,
        )

    def send(a):
        def one(at, carry):
            tile_copy(a * CH + list_sm[a, 2, at], list_sm[a, 0, at], list_sm[a, 1, at]).start()
            return carry
        lax.fori_loop(0, list_sm[a, 3, 0], one, 0)

    loop(chunks, send)

    def send_extra(at, carry):
        code = extra_sm[1 + at]
        tile_copy(chunks * CH + at, code // groups, code % groups).start()
        return carry

    lax.fori_loop(0, extra_sm[0], send_extra, 0)

    def drain_one(at, carry):
        tile_copy(0, 0, 0).wait()
        return carry

    def drain(a):
        lax.fori_loop(0, list_sm[a, 3, 0], drain_one, 0)

    loop(chunks, drain)
    lax.fori_loop(0, extra_sm[0], drain_one, 0)

    @pl.when((region == 0) & (column == 0))
    def _():
        for at in range(K_PANELS):
            piece = pl.ds(at * 128, 128)
            pltpu.make_async_copy(
                squares.at[piece, :], out_ref.at[piece, piece], sem_sq.at[at]
            ).wait()


def assemble(place, rows, cols, got, prior2, filled):
    count = got.shape[0] * 8
    chunks = count // CH
    capacity = rows // 8 * (cols // 128)
    any_space = pl.BlockSpec(memory_space=pl.ANY)
    vmem = pl.BlockSpec(memory_space=pltpu.VMEM)
    return pl.pallas_call(
        functools.partial(assemble_kernel, place, (rows, cols, chunks)),
        out_shape=jax.ShapeDtypeStruct((rows, cols), f32),
        in_specs=[vmem, vmem, any_space],
        out_specs=any_space,
        scratch_shapes=[
            pltpu.VMEM((chunks, 128, CH), f32),
            pltpu.VMEM((chunks, 16, CH), f32),
            pltpu.VMEM((chunks, CH, 128), f32),
            pltpu.VMEM((64, 128), f32),
            pltpu.VMEM((chunks, 64, CH), f32),
            pltpu.VMEM((chunks, 2, CH, 1024), bf16),
            pltpu.VMEM(((count + capacity) * 8, 128), f32),
            pltpu.VMEM((CH, CH), f32),
            pltpu.VMEM((PANEL, 128), f32),
            pltpu.VMEM((chunks, 8, CH), i32),
            pltpu.VMEM((chunks, 8, CH), i32),
            pltpu.SMEM((chunks, 8, CH), i32),
            pltpu.SMEM((chunks, 8, CH), i32),
            pltpu.SMEM((1 + capacity,), i32),
            pltpu.SemaphoreType.DMA((chunks,)),
            pltpu.SemaphoreType.DMA((chunks,)),
            pltpu.SemaphoreType.DMA,
            pltpu.SemaphoreType.DMA((K_PANELS,)),
        ],
        input_output_aliases={2: 0},
        compiler_params=pltpu.CompilerParams(vmem_limit_bytes=48 << 20),
        name="assemble",
    )(got, prior2, filled)


def place():
    return lax.axis_index("region"), lax.axis_index("col")


def body(jac, dest, near_pose, prior):
    regions, columns = lax.axis_size("region"), lax.axis_size("col")
    devices = regions * columns
    rows = prior.shape[0]
    cols = rows * regions // columns
    assert jac.shape[0] == 8 and devices * 8 % CH == 0
    assert rows % cols == 0 and rows // 8 <= 256 and regions <= 256
    assert rows >= PANEL and cols >= PANEL and cols % 128 == 0
    prior2 = prior.reshape(rows // 128, 128)
    packed = pack(jac, dest, near_pose, prior2, devices)
    got = lax.all_to_all(packed, ("region", "col"), split_axis=0, concat_axis=0, tiled=True)
    filled = fill(place, rows, cols, prior2)
    return assemble(place, rows, cols, got, prior2, filled)


def solution(mesh):
    return jax.shard_map(
        body,
        mesh=mesh,
        in_specs=(
            P(("region", "col"), None),
            P(("region", "col"), None),
            P(("region", "col"), None),
            P("region"),
        ),
        out_specs=P("region", "col"),
        check_vma=False,
    )
```

```python
import functools

import jax
import jax.numpy as jnp
from jax import lax
from jax.experimental import pallas as pl
from jax.experimental.pallas import tpu as pltpu
from jax.sharding import PartitionSpec as P

NB = 128
K_PANELS = 2
PANEL = NB * K_PANELS
PP = PANEL // 8
CH = 256
BIG = float(1 << 24)
f32, bf16, i32 = jnp.float32, jnp.bfloat16, jnp.int32


def iota(shape, dim):
    return lax.broadcasted_iota(i32, shape, dim)


def split(x, parts):
    out = []
    for _ in range(parts):
        top = x.astype(bf16)
        out.append(top)
        x = x - top.astype(f32)
    return out


def dot(a, b, dims=((1,), (0,))):
    return lax.dot_general(a, b, (dims, ((), ())), preferred_element_type=f32)


def pack_kernel(jac_ref, dest_ref, near_ref, prior_ref, out_ref):
    shape = (8, 128)
    lane, row = iota(shape, 1), iota(shape, 0)
    dest, near = dest_ref[...].astype(f32), near_ref[...].astype(f32)
    tile = jnp.zeros(shape, f32)
    corner = iota((8, 8), 0) == iota((8, 8), 1)
    for at, line in enumerate((dest[0:1, :], near[0:1, :], dest[1:2, :], near[1:2, :])):
        column = jnp.sum(jnp.where(corner, line, 0.0), axis=1, keepdims=True)
        tile = jnp.where(lane == at, column, tile)
    first = prior_ref[0:2, :]
    both = jnp.where(row < 4, first[0:1, :], first[1:2, :])
    spread = jnp.zeros(shape, f32)
    for at in range(4):
        moved = both if at == 0 else pltpu.roll(both, 128 - 32 * at, 1)
        spread = jnp.where(row % 4 == at, moved, spread)
    for at, part in enumerate(split(spread, 3)):
        moved = pltpu.roll(part.astype(f32), 32 * (at + 1), 1)
        tile = jnp.where(lane // 32 == at + 1, moved, tile)
    whole = jnp.concatenate([jac_ref[...].astype(f32), tile], axis=0).astype(bf16)
    out_ref[...] = jnp.broadcast_to(whole[None], out_ref.shape)


def pack(jac, dest, near_pose, prior2, devices):
    return pl.pallas_call(
        pack_kernel,
        out_shape=jax.ShapeDtypeStruct((devices, 16, 128), bf16),
        in_specs=[pl.BlockSpec(memory_space=pltpu.VMEM)] * 4,
        out_specs=pl.BlockSpec(memory_space=pltpu.VMEM),
        name="pack",
    )(jac, dest.T, near_pose.T, prior2)


def fill_kernel(place, sizes, prior_ref, out_ref, zeros, squares, sem, sem2):
    rows, cols = sizes
    region, column = place()
    pieces = rows // zeros.shape[0]
    zeros[...] = jnp.zeros_like(zeros)
    step = zeros.shape[0]
    copies = [
        pltpu.make_async_copy(zeros, out_ref.at[pl.ds(at * step, step), :], sem.at[at])
        for at in range(pieces)
    ]
    for copy in copies:
        copy.start()
    start = column * cols - region * rows
    own = (start >= 0) & (start < rows)

    @pl.when(own)
    def _():
        diagonal = iota((128, 128), 0) == iota((128, 128), 1)
        first = start // 128
        for at in range(cols // 128):
            squares[at] = jnp.where(diagonal, prior_ref[pl.ds(first + at, 1), :], 0.0)

    for copy in copies:
        copy.wait()

    @pl.when(own)
    def _():
        base = pl.multiple_of(start, 128)
        patches = [
            pltpu.make_async_copy(
                squares.at[at],
                out_ref.at[pl.ds(base + at * 128, 128), pl.ds(at * 128, 128)],
                sem2.at[at],
            )
            for at in range(cols // 128)
        ]
        for patch in patches:
            patch.start()
        for patch in patches:
            patch.wait()


def fill(place, rows, cols, prior2):
    step = min(256, rows)
    return pl.pallas_call(
        functools.partial(fill_kernel, place, (rows, cols)),
        out_shape=jax.ShapeDtypeStruct((rows, cols), f32),
        out_specs=pl.BlockSpec(memory_space=pl.ANY),
        scratch_shapes=[
            pltpu.VMEM((step, cols), f32),
            pltpu.VMEM((cols // 128, 128, 128), f32),
            pltpu.SemaphoreType.DMA((rows // step,)),
            pltpu.SemaphoreType.DMA((cols // 128,)),
        ],
        cost_estimate=pl.CostEstimate(flops=0, bytes_accessed=rows * cols * 4, transcendentals=0),
        name="fill",
    )(prior2)


def batched(left, right):
    out = []
    for k in range(8):
        total = left[0][k : k + 1, :] * right[0]
        for e in range(1, 8):
            total = total + left[e][k : k + 1, :] * right[e]
        out.append(total)
    return out


def slabs(block):
    return [block[8 * e : 8 * e + 8, :] for e in range(8)]


def to_columns(rows):
    full = jnp.concatenate([rows, jnp.zeros((120, CH), f32)], axis=0)
    return full.T


def cholesky(a):
    row = iota((8, 128), 0)
    columns, scales = [], []
    a = list(a)
    for j in range(8):
        pivot = a[j][j : j + 1, :]
        scale = lax.rsqrt(pivot)
        scale = scale * (1.5 - 0.5 * pivot * scale * scale)
        column = jnp.where(row >= j, a[j] * scale, 0.0)
        for k in range(j + 1, 8):
            a[k] = a[k] - column * column[k : k + 1, :]
        columns.append(column)
        scales.append(scale)
    inverse = []
    for i in range(8):
        x = jnp.where(row == i, 1.0, 0.0)
        for j in range(i, 8):
            value = x[j : j + 1, :] * scales[j]
            x = jnp.where(row == j, value, jnp.where(row > j, x - columns[j] * value, x))
        inverse.append(x)
    return columns, inverse


def loop(count, body):
    if count == 1:
        body(0)
    else:
        lax.fori_loop(0, count, lambda at, carry: (body(at), carry)[1], 0)


def expansion():
    row, lane = iota((8, 128), 0), iota((8, 128), 1)
    none = jnp.zeros((8, 128), f32)
    straight = jnp.where(lane % 8 == row, 1.0, 0.0)
    by_rows = [
        jnp.concatenate([straight if at == k else none for at in range(8)], axis=1)
        for k in range(8)
    ]
    by_columns = [
        jnp.concatenate(
            [jnp.where((row == at) & (lane % 8 == j), 1.0, 0.0) for at in range(8)], axis=1
        )
        for j in range(8)
    ]
    return jnp.concatenate(by_rows + by_columns, axis=0).astype(bf16)


def assemble_kernel(place, sizes, got_ref, prior_ref, filled_ref, out_ref,
                    jt, rows_s, cols_s, app, bt, blk, tiles, keys, squares,
                    listing, info, list_sm, info_sm, extra_sm, sem_list, sem_info, sem_out, sem_sq):
    del filled_ref
    rows, cols, chunks = sizes
    row_poses, col_poses, groups = rows // 8, cols // 8, cols // 128
    region, column = place()
    region_f, column_f = region.astype(f32), column.astype(f32)
    start = column * cols - region * rows
    own = (start >= 0) & (start < rows)
    share = jnp.where(own, 1.0, 0.0)
    per = CH // 8
    lane8, row8 = iota((8, 128), 1), iota((8, 128), 0)
    before = iota((CH, CH), 0) < iota((CH, CH), 1)
    table = expansion()

    sent = got_ref[0].astype(f32)[8:16, :]
    panel_prior = jnp.zeros((8, 128), f32)
    for at in range(3):
        panel_prior = panel_prior + pltpu.roll(sent, 128 - 32 * (at + 1), 1)
    panel_prior = jnp.where(lane8 < 32, panel_prior, 0.0)
    lined = jnp.zeros((8, 128), f32)
    for at in range(4):
        moved = panel_prior if at == 0 else pltpu.roll(panel_prior, 32 * at, 1)
        lined = lined + jnp.where(row8 % 4 == at, moved, 0.0)
    halves = [
        jnp.sum(jnp.where(row8 < 4, lined, 0.0), axis=0, keepdims=True),
        jnp.sum(jnp.where(row8 >= 4, lined, 0.0), axis=0, keepdims=True),
    ]
    prior_row = jnp.concatenate(halves, axis=1)
    kl, unknown = iota((64, PANEL), 0), iota((64, PANEL), 1)
    diagonal = jnp.where((kl // 8 == kl % 8) & (unknown % 8 == kl % 8), prior_row, 0.0)
    own_pose = jnp.where(iota((PANEL, 128), 0) // 8 == iota((PANEL, 128), 1), 1.0, 0.0).astype(bf16)
    first = dot(jnp.concatenate(split(diagonal, 3), axis=0), own_pose)
    first = first[0:64] + first[64:128] + first[128:192]
    kl = iota((64, 128), 0)
    spare = (kl // 8 == kl % 8) & (iota((64, 128), 1) >= PP)
    app[...] = first + jnp.where(spare, 1.0, 0.0)

    def measure(a):
        block = got_ref[pl.ds(a * per, per)].astype(f32)
        jac = block[:, 0:8, :].reshape(CH, 128)
        label = block[:, 8:16, :].reshape(CH, 128)
        jac_t = jac.T
        label_t = label.T
        jt[a] = jac_t
        d0, n0, d1, n1 = (label_t[at : at + 1, :] for at in range(4))
        c0 = d0 * row_poses + n0 - column_f * col_poses
        c1 = d1 * row_poses + n1 - column_f * col_poses
        one, none = jnp.ones_like(d0), jnp.zeros_like(d0)
        row0, row1 = d0 == region_f, d1 == region_f
        col0, col1 = (c0 >= 0) & (c0 < col_poses), (c1 >= 0) & (c1 < col_poses)
        pan0, pan1 = (d0 == 0) & (n0 < PP), (d1 == 0) & (n1 < PP)
        has_row = jnp.where(row0 | row1, one, none)
        has_col = jnp.where(col0 | col1, one, none)
        touches = jnp.where(pan0 | pan1, one, none)
        row_pose = jnp.where(row0, n0, n1)
        col_pose = jnp.where(col0, c0, c1)
        pan_side = jnp.where(pan0, none, one)
        pan_pose = jnp.where(pan0, n0, n1)
        row_in_panel = jnp.where((row0 & pan0) | (row1 & pan1), one, none)
        col_in_panel = jnp.where((col0 & pan0) | (col1 & pan1), one, none)
        relevant = has_row * has_col * (1.0 - row_in_panel)
        group = jnp.floor(col_pose * (1.0 / 16.0))
        tile = row_pose * groups + group
        cell = row_pose * col_poses + col_pose
        is_row = touches * has_row * (1.0 - row_in_panel)
        is_col = touches * has_col * (1.0 - col_in_panel)
        lines = [
            jnp.where(relevant > 0, tile, -1.0),
            jnp.where(relevant > 0, cell, -1.0),
            jnp.where(touches > 0, pan_pose, -1.0),
            jnp.where(is_row > 0, pan_pose, -1.0),
            col_pose - group * 16.0,
            none, none, none,
        ]
        more = [
            jnp.where(relevant > 0, tile, -2.0),
            jnp.where(relevant > 0, cell, -2.0),
            jnp.where(is_col > 0, pan_pose, -2.0),
            relevant,
            row_pose,
            group,
            col_pose,
            is_row * is_col,
            jnp.where(row0, none, one),
            jnp.where(col0, none, one),
            pan_side,
            col_in_panel,
            none, none, none, none,
        ]
        lines = jnp.concatenate(lines, axis=0)
        rows_s[a] = jnp.concatenate([lines] + more, axis=0)
        columns = to_columns(lines)
        cols_s[a] = columns
        j0, j1 = slabs(jac_t[0:64, :]), slabs(jac_t[64:128, :])
        near = [jnp.where(pan_side == 0, x, y) for x, y in zip(j0, j1)]
        gram = jnp.concatenate(batched(near, near), axis=0)
        of_pose = jnp.where(
            columns[:, 2:3] == iota((CH, 128), 1).astype(f32), 1.0, 0.0
        ).astype(bf16)
        total = dot(jnp.concatenate(split(gram, 3), axis=0), of_pose)
        app[...] += total[0:64] + total[64:128] + total[128:192]

    loop(chunks, measure)

    def earlier_of(a, at, at_right):
        def from_chunk(b, count):
            other = jnp.broadcast_to(cols_s[b, :, at : at + 1], (CH, CH))
            same = jnp.where(other == rows_s[a, at_right : at_right + 1, :], 1.0, 0.0)
            if chunks == 1:
                same = jnp.where(before, same, 0.0)
            else:
                here, all_of_it = jnp.where(b == a, 1.0, 0.0), jnp.where(b < a, 1.0, 0.0)
                same = jnp.where(before, same, 0.0) * here + same * all_of_it
            return count + jnp.sum(same, axis=0, keepdims=True)

        nothing = jnp.zeros((1, CH), f32)
        return from_chunk(0, nothing) if chunks == 1 else lax.fori_loop(0, chunks, from_chunk, nothing)

    def lists(a):
        relevant = rows_s[a, 11:12, :]
        kept = jnp.where(earlier_of(a, 0, 8) == 0, relevant, 0.0)
        lone = jnp.where(earlier_of(a, 1, 9) == 0, relevant, 0.0)
        joins = lone * (1.0 - kept)
        count = jnp.sum(kept, axis=1, keepdims=True)
        upper = jnp.where(before, 1.0, 0.0).astype(bf16)
        rank = dot(jnp.broadcast_to(kept, (16, CH)).astype(bf16), upper)[0:1, :]
        slot = iota((CH, CH), 0).astype(f32)
        slot = jnp.where(slot < count, slot, 0.0)
        chosen = jnp.where((rank == slot) & (kept > 0), 1.0, 0.0).astype(bf16)
        position = iota((1, CH), 1).astype(f32)
        data = jnp.concatenate(
            [rows_s[a, 12:13, :], rows_s[a, 13:14, :], position, jnp.zeros((13, CH), f32)], axis=0
        ).astype(bf16)
        found = dot(data, chosen, ((1,), (1,)))[0:8, :]
        listing[a] = jnp.where(iota((8, CH), 0) == 3, count, found).astype(i32)
        pltpu.make_async_copy(listing.at[a], list_sm.at[a], sem_list.at[a]).start()
        info[a] = jnp.concatenate(
            [rows_s[a, 12:13, :], rows_s[a, 14:15, :], joins, jnp.zeros((5, CH), f32)], axis=0
        ).astype(i32)
        pltpu.make_async_copy(info.at[a], info_sm.at[a], sem_info.at[a]).start()

    loop(chunks, lists)

    def key_table(a, b):
        left = jnp.broadcast_to(cols_s[a, :, 3:4], (CH, CH))
        valid = jnp.where(left == rows_s[b, 10:11, :], 1.0, 0.0)
        same = iota((CH, CH), 0) == iota((CH, CH), 1)
        joins = info[a, 2:3, :].astype(f32)
        if chunks > 1:
            flag = jnp.where(a == b, 1.0, 0.0)
            joins = joins * flag + valid * (1.0 - flag)
        valid = jnp.where(same, joins, valid)
        key = (iota((CH, CH), 0) * CH + iota((CH, CH), 1)).astype(f32)
        key = jnp.where(valid > 0, key, BIG)
        keys[...] = key
        return jnp.min(key)

    early = key_table(0, 0) if chunks == 1 else None

    factor, inverse = cholesky(slabs(app[...]))
    factor = jnp.concatenate(factor, axis=0)
    inverse = jnp.concatenate(split(jnp.concatenate(inverse, axis=0), 3), axis=0)

    full = jnp.concatenate([factor, jnp.zeros((64, 128), f32)], axis=0).T[0:PP, 0:64]
    high, low = split(full, 2)
    both = jnp.concatenate([high.astype(f32), low.astype(f32)], axis=1).astype(bf16)
    by_columns = table[64:128]
    value = dot(both, jnp.concatenate([by_columns, by_columns], axis=0))
    inside = iota((PP, 128), 1) // 8 == iota((PP, 128), 0) % 16
    for k in range(8):
        squares[pl.ds(k, PP, stride=8), :] = jnp.where(
            inside, value[:, 128 * k : 128 * k + 128], 0.0
        )

    def blocks(a):
        row = [rows_s[a, at : at + 1, :] for at in range(24)]
        jac_t = jt[a]
        j0, j1 = slabs(jac_t[0:64, :]), slabs(jac_t[64:128, :])
        left = [jnp.where(row[16] == 0, x, y) for x, y in zip(j0, j1)]
        right = [jnp.where(row[17] == 0, x, y) for x, y in zip(j0, j1)]
        near = [jnp.where(row[18] == 0, x, y) for x, y in zip(j0, j1)]
        far = [jnp.where(row[18] == 0, y, x) for x, y in zip(j0, j1)]
        gram = batched(left, right)
        cross = batched(near, far)
        of_pose = jnp.where(iota((128, CH), 0).astype(f32) == row[2], 1.0, 0.0).astype(bf16)
        inv = dot(inverse, of_pose)
        inv = slabs(inv[0:64] + inv[64:128] + inv[128:192])
        solved = []
        for j in range(8):
            total = inv[0][j : j + 1, :] * cross[0]
            for i in range(1, j + 1):
                total = total + inv[i][j : j + 1, :] * cross[i]
            solved.append(total)
        bt[a] = jnp.concatenate(solved, axis=0)
        outer = batched(solved, solved)
        keep_normal = row[11] * (1.0 - row[19])
        keep_panel = row[11] * row[19]
        values = [(g - o * row[15]) * keep_normal for g, o in zip(gram, outer)]
        values += [x * keep_panel for x in solved]
        values = jnp.concatenate(values, axis=0)
        high, low = split(values, 2)
        blk[a] = jnp.concatenate([high, low], axis=0)

    loop(chunks, blocks)

    def merge(a):
        line = [rows_s[a, at : at + 1, :] for at in range(24)]

        def from_chunk(b, total):
            other = jnp.broadcast_to(cols_s[b, :, 1:2], (CH, CH))
            same = jnp.where(other == line[9], 1.0, 0.0).astype(bf16)
            found = dot(blk[b], same)
            return total + found[0:128] + found[128:256]

        total = jnp.zeros((128, CH), f32)
        total = from_chunk(0, total) if chunks == 1 else lax.fori_loop(0, chunks, from_chunk, total)
        sixteenth = jnp.floor(line[12] * (1.0 / 16.0))
        pieces = rows // 128
        local = jnp.concatenate(
            [prior_ref[...], jnp.zeros((16 - pieces, 128), f32)], axis=0
        ) if pieces < 16 else prior_ref[...]
        steps = local.shape[0]
        parts = jnp.concatenate(split(local, 3), axis=0)
        of_row = jnp.where(
            (iota((3 * steps, CH), 0) % steps).astype(f32) == sixteenth, 1.0, 0.0
        ).astype(bf16)
        priors = dot(parts, of_row, ((0,), (0,)))
        within = line[12] - sixteenth * 16.0
        on_row = jnp.zeros((8, CH), f32)
        for at in range(16):
            on_row = on_row + jnp.where(within == float(at), priors[8 * at : 8 * at + 8, :], 0.0)
        on_row = on_row * (share * line[11])
        sub = iota((8, CH), 0)
        normal = [
            total[8 * k : 8 * k + 8, :] + jnp.where(sub == k, on_row, 0.0) for k in range(8)
        ]
        total = jnp.concatenate(normal + [total[64:128, :]], axis=0)
        high, low = split(total.T, 2)
        value = dot(high, table) + dot(low, table)
        keep = (iota((CH, 128), 1) // 8).astype(f32) == cols_s[a, :, 4:5]
        for k in range(8):
            tiles[pl.ds(a * CH * 8 + k, CH, stride=8), :] = jnp.where(
                keep, value[:, 128 * k : 128 * k + 128], 0.0
            )

    loop(chunks, merge)

    def waiting(a):
        pltpu.make_async_copy(listing.at[a], list_sm.at[a], sem_list.at[a]).wait()
        pltpu.make_async_copy(info.at[a], info_sm.at[a], sem_info.at[a]).wait()

    loop(chunks, waiting)
    extra_sm[0] = 0

    def tile_rows(slot, count=1):
        return pl.ds(pl.multiple_of(slot * 8, 8), 8 * count)

    def pairs(index):
        a, b = (0, 0) if chunks == 1 else (index // chunks, index % chunks)

        def one(key_now):
            number = key_now.astype(i32)
            m1, m2 = number // CH, number % CH
            joining = (m1 == m2) if chunks == 1 else ((m1 == m2) & (a == b))
            r1, c2 = info_sm[a, 0, m1], info_sm[b, 1, m2]
            group, within = c2 // 16, c2 % 16
            position = iota((8, CH), 1)
            total = jnp.zeros((8, 128), f32)
            for j in range(8):
                x = bt[a, 8 * j : 8 * j + 8, :]
                y = bt[b, 8 * j : 8 * j + 8, :]
                x = jnp.sum(jnp.where(position == m1, x, 0.0), axis=1, keepdims=True)
                y = jnp.sum(jnp.where(position == m2, y, 0.0), axis=1, keepdims=True)
                y = jnp.where(lane8 % 8 == row8, y, 0.0)
                y = jnp.sum(y, axis=0, keepdims=True)
                total = total + x * y
            total = jnp.where(lane8 // 8 == within, -total, 0.0)
            total = jnp.where(joining, tiles[tile_rows(a * CH + m1), :], total)

            def search(chunk, carry):
                def at_one(at, slot):
                    hit = (list_sm[chunk, 0, at] == r1) & (list_sm[chunk, 1, at] == group)
                    return jnp.where(hit, chunk * CH + list_sm[chunk, 2, at], slot)
                return lax.fori_loop(0, list_sm[chunk, 3, 0], at_one, carry)

            slot = search(0, -1) if chunks == 1 else lax.fori_loop(0, chunks, search, -1)
            added = extra_sm[0]
            code = r1 * groups + group

            def at_extra(at, slot):
                return jnp.where(extra_sm[1 + at] == code, chunks * CH + at, slot)

            slot = lax.fori_loop(0, added, at_extra, slot)

            @pl.when(slot >= 0)
            def _():
                where = tile_rows(slot)
                tiles[where, :] = tiles[where, :] + total

            @pl.when(slot < 0)
            def _():
                tiles[tile_rows(chunks * CH + added), :] = total
                extra_sm[1 + added] = code
                extra_sm[0] = added + 1

            return jnp.min(jnp.where(keys[...] > key_now, keys[...], BIG))

        smallest = early if chunks == 1 else key_table(a, b)
        lax.while_loop(lambda key_now: key_now < BIG, one, smallest)

    loop(chunks * chunks, pairs)

    def tile_copy(slot, r, group, count=1):
        return pltpu.make_async_copy(
            tiles.at[tile_rows(slot, count), :],
            out_ref.at[tile_rows(r, count), pl.ds(pl.multiple_of(group * 128, 128), 128)],
            sem_out,
        )

    corner = (region == 0) & (column == 0)
    square_copies = [
        pltpu.make_async_copy(
            squares.at[pl.ds(at * 128, 128), :],
            out_ref.at[pl.ds(at * 128, 128), pl.ds(at * 128, 128)],
            sem_sq.at[at],
        )
        for at in range(K_PANELS)
    ]

    @pl.when(corner)
    def _():
        for copy in square_copies:
            copy.start()

    def send(a):
        def four(at, carry):
            for more in range(4):
                entry = at * 4 + more
                tile_copy(
                    a * CH + list_sm[a, 2, entry], list_sm[a, 0, entry], list_sm[a, 1, entry]
                ).start()
            return carry
        lax.fori_loop(0, (list_sm[a, 3, 0] + 3) // 4, four, 0)

    loop(chunks, send)

    def send_extra(at, carry):
        code = extra_sm[1 + at]
        tile_copy(chunks * CH + at, code // groups, code % groups).start()
        return carry

    lax.fori_loop(0, extra_sm[0], send_extra, 0)

    def drain_four(at, carry):
        tile_copy(0, 0, 0, 4).wait()
        return carry

    def drain_one(at, carry):
        tile_copy(0, 0, 0).wait()
        return carry

    def drain(a):
        lax.fori_loop(0, (list_sm[a, 3, 0] + 3) // 4, drain_four, 0)

    loop(chunks, drain)
    lax.fori_loop(0, extra_sm[0], drain_one, 0)

    @pl.when(corner)
    def _():
        for copy in square_copies:
            copy.wait()


def assemble(place, rows, cols, got, prior2, filled):
    count = got.shape[0] * 8
    chunks = count // CH
    capacity = rows // 8 * (cols // 128)
    any_space = pl.BlockSpec(memory_space=pl.ANY)
    vmem = pl.BlockSpec(memory_space=pltpu.VMEM)
    return pl.pallas_call(
        functools.partial(assemble_kernel, place, (rows, cols, chunks)),
        out_shape=jax.ShapeDtypeStruct((rows, cols), f32),
        in_specs=[vmem, vmem, any_space],
        out_specs=any_space,
        scratch_shapes=[
            pltpu.VMEM((chunks, 128, CH), f32),
            pltpu.VMEM((chunks, 24, CH), f32),
            pltpu.VMEM((chunks, CH, 128), f32),
            pltpu.VMEM((64, 128), f32),
            pltpu.VMEM((chunks, 64, CH), f32),
            pltpu.VMEM((chunks, 256, CH), bf16),
            pltpu.VMEM(((count + capacity) * 8, 128), f32),
            pltpu.VMEM((CH, CH), f32),
            pltpu.VMEM((PANEL, 128), f32),
            pltpu.VMEM((chunks, 8, CH), i32),
            pltpu.VMEM((chunks, 8, CH), i32),
            pltpu.SMEM((chunks, 8, CH), i32),
            pltpu.SMEM((chunks, 8, CH), i32),
            pltpu.SMEM((1 + capacity,), i32),
            pltpu.SemaphoreType.DMA((chunks,)),
            pltpu.SemaphoreType.DMA((chunks,)),
            pltpu.SemaphoreType.DMA,
            pltpu.SemaphoreType.DMA((K_PANELS,)),
        ],
        input_output_aliases={2: 0},
        compiler_params=pltpu.CompilerParams(vmem_limit_bytes=48 << 20),
        name="assemble",
    )(got, prior2, filled)


def place():
    return lax.axis_index("region"), lax.axis_index("col")


def body(jac, dest, near_pose, prior):
    regions, columns = lax.axis_size("region"), lax.axis_size("col")
    devices = regions * columns
    rows = prior.shape[0]
    cols = rows * regions // columns
    assert jac.shape[0] == 8 and devices * 8 % CH == 0
    assert rows % cols == 0 and rows // 8 <= 256 and regions <= 256
    assert rows >= PANEL and cols >= PANEL and cols % 128 == 0
    prior2 = prior.reshape(rows // 128, 128)
    packed = pack(jac, dest, near_pose, prior2, devices)
    got = lax.all_to_all(packed, ("region", "col"), split_axis=0, concat_axis=0, tiled=True)
    filled = fill(place, rows, cols, prior2)
    return assemble(place, rows, cols, got, prior2, filled)


def solution(mesh):
    return jax.shard_map(
        body,
        mesh=mesh,
        in_specs=(
            P(("region", "col"), None),
            P(("region", "col"), None),
            P(("region", "col"), None),
            P("region"),
        ),
        out_specs=P("region", "col"),
        check_vma=False,
    )
```

```python
import functools

import jax
import jax.numpy as jnp
from jax import lax
from jax.experimental import pallas as pl
from jax.experimental.pallas import tpu as pltpu
from jax.sharding import PartitionSpec as P

NB = 128
K_PANELS = 2
PANEL = NB * K_PANELS
PP = PANEL // 8
CH = 256
BIG = float(1 << 24)
f32, bf16, i32 = jnp.float32, jnp.bfloat16, jnp.int32


def iota(shape, dim):
    return lax.broadcasted_iota(i32, shape, dim)


def split(x, parts):
    out = []
    for _ in range(parts):
        top = x.astype(bf16)
        out.append(top)
        x = x - top.astype(f32)
    return out


def dot(a, b, dims=((1,), (0,))):
    return lax.dot_general(a, b, (dims, ((), ())), preferred_element_type=f32)


SLOT = 10


def pack_kernel(place, jac_ref, dest_ref, near_ref, prior_ref, out_ref):
    _, column = place()
    lane = iota((1, 128), 1)
    fill_up = jnp.zeros((2, 120), f32)
    dest = jnp.concatenate([dest_ref[...].astype(f32), fill_up], axis=1)
    near = jnp.concatenate([near_ref[...].astype(f32), fill_up], axis=1)
    line = dest[0:1, :] + pltpu.roll(near[0:1, :], 8, 1)
    line = line + pltpu.roll(dest[1:2, :], 16, 1) + pltpu.roll(near[1:2, :], 24, 1)
    column = column % 8
    prior = prior_ref[pl.ds(column // 4, 1), :]
    prior = pltpu.roll(prior, (4 - column % 4) % 4 * 32, 1)
    for at, part in enumerate(split(prior, 3)):
        moved = pltpu.roll(part.astype(f32), 32 * (at + 1), 1)
        line = jnp.where(lane // 32 == at + 1, moved, line)
    slot = jnp.concatenate([jac_ref[...].astype(f32), line, jnp.zeros((1, 128), f32)], axis=0)
    eight = jnp.concatenate([slot] * 8, axis=0).astype(bf16)
    for at in range(out_ref.shape[0] // (8 * SLOT)):
        out_ref[8 * SLOT * at : 8 * SLOT * (at + 1), :] = eight


def pack(place, jac, dest, near_pose, prior2, devices):
    return pl.pallas_call(
        functools.partial(pack_kernel, place),
        out_shape=jax.ShapeDtypeStruct((devices * SLOT, 128), bf16),
        in_specs=[pl.BlockSpec(memory_space=pltpu.VMEM)] * 4,
        out_specs=pl.BlockSpec(memory_space=pltpu.VMEM),
        name="pack",
    )(jac, dest.T, near_pose.T, prior2)


def fill_kernel(place, sizes, prior_ref, out_ref, zeros, squares, sem, sem2):
    rows, cols = sizes
    region, column = place()
    pieces = rows // zeros.shape[0]
    zeros[...] = jnp.zeros_like(zeros)
    step = zeros.shape[0]
    copies = [
        pltpu.make_async_copy(zeros, out_ref.at[pl.ds(at * step, step), :], sem.at[at])
        for at in range(pieces)
    ]
    for copy in copies:
        copy.start()
    start = column * cols - region * rows
    own = (start >= 0) & (start < rows)

    @pl.when(own)
    def _():
        diagonal = iota((128, 128), 0) == iota((128, 128), 1)
        first = start // 128
        for at in range(cols // 128):
            squares[at] = jnp.where(diagonal, prior_ref[pl.ds(first + at, 1), :], 0.0)

    for copy in copies:
        copy.wait()

    @pl.when(own)
    def _():
        base = pl.multiple_of(start, 128)
        patches = [
            pltpu.make_async_copy(
                squares.at[at],
                out_ref.at[pl.ds(base + at * 128, 128), pl.ds(at * 128, 128)],
                sem2.at[at],
            )
            for at in range(cols // 128)
        ]
        for patch in patches:
            patch.start()
        for patch in patches:
            patch.wait()


def fill(place, rows, cols, prior2):
    step = min(256, rows)
    return pl.pallas_call(
        functools.partial(fill_kernel, place, (rows, cols)),
        out_shape=jax.ShapeDtypeStruct((rows, cols), f32),
        out_specs=pl.BlockSpec(memory_space=pl.ANY),
        scratch_shapes=[
            pltpu.VMEM((step, cols), f32),
            pltpu.VMEM((cols // 128, 128, 128), f32),
            pltpu.SemaphoreType.DMA((rows // step,)),
            pltpu.SemaphoreType.DMA((cols // 128,)),
        ],
        cost_estimate=pl.CostEstimate(flops=0, bytes_accessed=rows * cols * 4, transcendentals=0),
        name="fill",
    )(prior2)


def batched(left, right):
    out = []
    for k in range(8):
        total = left[0][k : k + 1, :] * right[0]
        for e in range(1, 8):
            total = total + left[e][k : k + 1, :] * right[e]
        out.append(total)
    return out


def slabs(block):
    return [block[8 * e : 8 * e + 8, :] for e in range(8)]


def to_columns(rows):
    full = jnp.concatenate([rows, jnp.zeros((120, CH), f32)], axis=0)
    return full.T


def cholesky(a):
    row = iota((8, 128), 0)
    columns, scales = [], []
    a = list(a)
    for j in range(8):
        pivot = a[j][j : j + 1, :]
        scale = lax.rsqrt(pivot)
        scale = scale * (1.5 - 0.5 * pivot * scale * scale)
        column = jnp.where(row >= j, a[j] * scale, 0.0)
        for k in range(j + 1, 8):
            a[k] = a[k] - column * column[k : k + 1, :]
        columns.append(column)
        scales.append(scale)
    inverse = []
    for i in range(8):
        x = jnp.where(row == i, 1.0, 0.0)
        for j in range(i, 8):
            value = x[j : j + 1, :] * scales[j]
            x = jnp.where(row == j, value, jnp.where(row > j, x - columns[j] * value, x))
        inverse.append(x)
    return columns, inverse


def loop(count, body):
    if count == 1:
        body(0)
    else:
        lax.fori_loop(0, count, lambda at, carry: (body(at), carry)[1], 0)


def expansion():
    row, lane = iota((8, 128), 0), iota((8, 128), 1)
    none = jnp.zeros((8, 128), f32)
    straight = jnp.where(lane % 8 == row, 1.0, 0.0)
    by_rows = [
        jnp.concatenate([straight if at == k else none for at in range(8)], axis=1)
        for k in range(8)
    ]
    by_columns = [
        jnp.concatenate(
            [jnp.where((row == at) & (lane % 8 == j), 1.0, 0.0) for at in range(8)], axis=1
        )
        for j in range(8)
    ]
    return jnp.concatenate(by_rows + by_columns, axis=0).astype(bf16)


def assemble_kernel(place, sizes, got_ref, prior_ref, filled_ref, out_ref,
                    jt, rows_s, cols_s, app, bt, blk, tiles, keys, squares,
                    listing, info, list_sm, info_sm, extra_sm, sem_list, sem_info, sem_out, sem_sq):
    del filled_ref
    rows, cols, chunks = sizes
    row_poses, col_poses, groups = rows // 8, cols // 8, cols // 128
    region, column = place()
    region_f, column_f = region.astype(f32), column.astype(f32)
    start = column * cols - region * rows
    own = (start >= 0) & (start < rows)
    share = jnp.where(own, 1.0, 0.0)
    per = CH // 8
    lane8, row8 = iota((8, 128), 1), iota((8, 128), 0)
    before = iota((CH, CH), 0) < iota((CH, CH), 1)
    table = expansion()

    def rows_of(a):
        return got_ref[pl.ds(a * per * SLOT, per * SLOT), :].astype(f32)

    def label_rows(a):
        block = rows_of(a)
        return jnp.concatenate(
            [block[SLOT * d + 8 : SLOT * d + 9, :] for d in range(per)], axis=0
        )

    labels0 = label_rows(0)
    sent = labels0[0:8, :]
    panel_prior = jnp.zeros((8, 128), f32)
    for at in range(3):
        panel_prior = panel_prior + pltpu.roll(sent, 128 - 32 * (at + 1), 1)
    panel_prior = jnp.where(lane8 < 32, panel_prior, 0.0)
    lined = jnp.zeros((8, 128), f32)
    for at in range(4):
        moved = panel_prior if at == 0 else pltpu.roll(panel_prior, 32 * at, 1)
        lined = lined + jnp.where(row8 % 4 == at, moved, 0.0)
    halves = [
        jnp.sum(jnp.where(row8 < 4, lined, 0.0), axis=0, keepdims=True),
        jnp.sum(jnp.where(row8 >= 4, lined, 0.0), axis=0, keepdims=True),
    ]
    prior_row = jnp.concatenate(halves, axis=1)
    kl, unknown = iota((64, PANEL), 0), iota((64, PANEL), 1)
    diagonal = jnp.where((kl // 8 == kl % 8) & (unknown % 8 == kl % 8), prior_row, 0.0)
    own_pose = jnp.where(iota((PANEL, 128), 0) // 8 == iota((PANEL, 128), 1), 1.0, 0.0).astype(bf16)
    first = dot(jnp.concatenate(split(diagonal, 3), axis=0), own_pose)
    first = first[0:64] + first[64:128] + first[128:192]
    kl = iota((64, 128), 0)
    spare = (kl // 8 == kl % 8) & (iota((64, 128), 1) >= PP)
    app[...] = first + jnp.where(spare, 1.0, 0.0)

    def measure(a):
        block = rows_of(a)
        jac = jnp.concatenate([block[SLOT * d : SLOT * d + 8, :] for d in range(per)], axis=0)
        jac_t = jac.T
        jt[a] = jac_t
        labels = labels0 if chunks == 1 else label_rows(a)
        spread = []
        for at in range(4):
            halves = []
            for half in range(2):
                total = jnp.zeros((8, 128), f32)
                for part in range(2):
                    from_row = 16 * half + 8 * part
                    piece = labels[from_row : from_row + 8, :]
                    if at:
                        piece = pltpu.roll(piece, 128 - 8 * at, 1)
                    piece = pltpu.roll(piece, 64 * part, 1, stride=8, stride_axis=0)
                    total = total + jnp.where(lane8 // 8 == row8 + 8 * part, piece, 0.0)
                halves.append(jnp.sum(total, axis=0, keepdims=True))
            spread.append(jnp.concatenate(halves, axis=1))
        d0, n0, d1, n1 = spread
        c0 = d0 * row_poses + n0 - column_f * col_poses
        c1 = d1 * row_poses + n1 - column_f * col_poses
        one, none = jnp.ones_like(d0), jnp.zeros_like(d0)
        row0, row1 = d0 == region_f, d1 == region_f
        col0, col1 = (c0 >= 0) & (c0 < col_poses), (c1 >= 0) & (c1 < col_poses)
        pan0, pan1 = (d0 == 0) & (n0 < PP), (d1 == 0) & (n1 < PP)
        has_row = jnp.where(row0 | row1, one, none)
        has_col = jnp.where(col0 | col1, one, none)
        touches = jnp.where(pan0 | pan1, one, none)
        row_pose = jnp.where(row0, n0, n1)
        col_pose = jnp.where(col0, c0, c1)
        pan_side = jnp.where(pan0, none, one)
        pan_pose = jnp.where(pan0, n0, n1)
        row_in_panel = jnp.where((row0 & pan0) | (row1 & pan1), one, none)
        col_in_panel = jnp.where((col0 & pan0) | (col1 & pan1), one, none)
        relevant = has_row * has_col * (1.0 - row_in_panel)
        group = jnp.floor(col_pose * (1.0 / 16.0))
        tile = row_pose * groups + group
        cell = row_pose * col_poses + col_pose
        is_row = touches * has_row * (1.0 - row_in_panel)
        is_col = touches * has_col * (1.0 - col_in_panel)
        lines = [
            jnp.where(relevant > 0, tile, -1.0),
            jnp.where(relevant > 0, cell, -1.0),
            jnp.where(touches > 0, pan_pose, -1.0),
            jnp.where(is_row > 0, pan_pose, -1.0),
            col_pose - group * 16.0,
            none, none, none,
        ]
        more = [
            jnp.where(relevant > 0, tile, -2.0),
            jnp.where(relevant > 0, cell, -2.0),
            jnp.where(is_col > 0, pan_pose, -2.0),
            relevant,
            row_pose,
            group,
            col_pose,
            is_row * is_col,
            jnp.where(row0, none, one),
            jnp.where(col0, none, one),
            pan_side,
            col_in_panel,
            none, none, none, none,
        ]
        lines = jnp.concatenate(lines, axis=0)
        rows_s[a] = jnp.concatenate([lines] + more, axis=0)
        columns = to_columns(lines)
        cols_s[a] = columns
        j0, j1 = slabs(jac_t[0:64, :]), slabs(jac_t[64:128, :])
        near = [jnp.where(pan_side == 0, x, y) for x, y in zip(j0, j1)]
        gram = jnp.concatenate(batched(near, near), axis=0)
        of_pose = jnp.where(
            columns[:, 2:3] == iota((CH, 128), 1).astype(f32), 1.0, 0.0
        ).astype(bf16)
        total = dot(jnp.concatenate(split(gram, 3), axis=0), of_pose)
        app[...] += total[0:64] + total[64:128] + total[128:192]

    loop(chunks, measure)

    def earlier_of(a, at, at_right):
        def from_chunk(b, count):
            other = jnp.broadcast_to(cols_s[b, :, at : at + 1], (CH, CH))
            same = jnp.where(other == rows_s[a, at_right : at_right + 1, :], 1.0, 0.0)
            if chunks == 1:
                same = jnp.where(before, same, 0.0)
            else:
                here, all_of_it = jnp.where(b == a, 1.0, 0.0), jnp.where(b < a, 1.0, 0.0)
                same = jnp.where(before, same, 0.0) * here + same * all_of_it
            return count + jnp.sum(same, axis=0, keepdims=True)

        nothing = jnp.zeros((1, CH), f32)
        return from_chunk(0, nothing) if chunks == 1 else lax.fori_loop(0, chunks, from_chunk, nothing)

    def lists(a):
        relevant = rows_s[a, 11:12, :]
        kept = jnp.where(earlier_of(a, 0, 8) == 0, relevant, 0.0)
        lone = jnp.where(earlier_of(a, 1, 9) == 0, relevant, 0.0)
        joins = lone * (1.0 - kept)
        count = jnp.sum(kept, axis=1, keepdims=True)
        upper = jnp.where(before, 1.0, 0.0).astype(bf16)
        rank = dot(jnp.broadcast_to(kept, (16, CH)).astype(bf16), upper)[0:1, :]
        slot = iota((CH, CH), 0).astype(f32)
        slot = jnp.where(slot < count, slot, 0.0)
        chosen = jnp.where((rank == slot) & (kept > 0), 1.0, 0.0).astype(bf16)
        position = iota((1, CH), 1).astype(f32)
        data = jnp.concatenate(
            [rows_s[a, 12:13, :], rows_s[a, 13:14, :], position, jnp.zeros((13, CH), f32)], axis=0
        ).astype(bf16)
        found = dot(data, chosen, ((1,), (1,)))[0:8, :]
        listing[a] = jnp.where(iota((8, CH), 0) == 3, count, found).astype(i32)
        pltpu.make_async_copy(listing.at[a], list_sm.at[a], sem_list.at[a]).start()
        info[a] = jnp.concatenate(
            [rows_s[a, 12:13, :], rows_s[a, 14:15, :], joins, jnp.zeros((5, CH), f32)], axis=0
        ).astype(i32)
        pltpu.make_async_copy(info.at[a], info_sm.at[a], sem_info.at[a]).start()

    loop(chunks, lists)

    def key_table(a, b):
        left = jnp.broadcast_to(cols_s[a, :, 3:4], (CH, CH))
        valid = jnp.where(left == rows_s[b, 10:11, :], 1.0, 0.0)
        same = iota((CH, CH), 0) == iota((CH, CH), 1)
        joins = info[a, 2:3, :].astype(f32)
        if chunks > 1:
            flag = jnp.where(a == b, 1.0, 0.0)
            joins = joins * flag + valid * (1.0 - flag)
        valid = jnp.where(same, joins, valid)
        key = (iota((CH, CH), 0) * CH + iota((CH, CH), 1)).astype(f32)
        key = jnp.where(valid > 0, key, BIG)
        keys[...] = key
        return jnp.min(key)

    early = key_table(0, 0) if chunks == 1 else None

    factor, inverse = cholesky(slabs(app[...]))
    factor = jnp.concatenate(factor, axis=0)
    inverse = jnp.concatenate(split(jnp.concatenate(inverse, axis=0), 3), axis=0)

    full = jnp.concatenate([factor, jnp.zeros((64, 128), f32)], axis=0).T[0:PP, 0:64]
    high, low = split(full, 2)
    both = jnp.concatenate([high.astype(f32), low.astype(f32)], axis=1).astype(bf16)
    by_columns = table[64:128]
    value = dot(both, jnp.concatenate([by_columns, by_columns], axis=0))
    inside = iota((PP, 128), 1) // 8 == iota((PP, 128), 0) % 16
    for k in range(8):
        squares[pl.ds(k, PP, stride=8), :] = jnp.where(
            inside, value[:, 128 * k : 128 * k + 128], 0.0
        )

    def blocks(a):
        row = [rows_s[a, at : at + 1, :] for at in range(24)]
        jac_t = jt[a]
        j0, j1 = slabs(jac_t[0:64, :]), slabs(jac_t[64:128, :])
        left = [jnp.where(row[16] == 0, x, y) for x, y in zip(j0, j1)]
        right = [jnp.where(row[17] == 0, x, y) for x, y in zip(j0, j1)]
        near = [jnp.where(row[18] == 0, x, y) for x, y in zip(j0, j1)]
        far = [jnp.where(row[18] == 0, y, x) for x, y in zip(j0, j1)]
        gram = batched(left, right)
        cross = batched(near, far)
        of_pose = jnp.where(iota((128, CH), 0).astype(f32) == row[2], 1.0, 0.0).astype(bf16)
        inv = dot(inverse, of_pose)
        inv = slabs(inv[0:64] + inv[64:128] + inv[128:192])
        solved = []
        for j in range(8):
            total = inv[0][j : j + 1, :] * cross[0]
            for i in range(1, j + 1):
                total = total + inv[i][j : j + 1, :] * cross[i]
            solved.append(total)
        bt[a] = jnp.concatenate(solved, axis=0)
        outer = batched(solved, solved)
        keep_normal = row[11] * (1.0 - row[19])
        keep_panel = row[11] * row[19]
        values = [(g - o * row[15]) * keep_normal for g, o in zip(gram, outer)]
        values += [x * keep_panel for x in solved]
        values = jnp.concatenate(values, axis=0)
        high, low = split(values, 2)
        blk[a] = jnp.concatenate([high, low], axis=0)

    loop(chunks, blocks)

    def merge(a):
        line = [rows_s[a, at : at + 1, :] for at in range(24)]

        def from_chunk(b, total):
            other = jnp.broadcast_to(cols_s[b, :, 1:2], (CH, CH))
            same = jnp.where(other == line[9], 1.0, 0.0).astype(bf16)
            found = dot(blk[b], same)
            return total + found[0:128] + found[128:256]

        total = jnp.zeros((128, CH), f32)
        total = from_chunk(0, total) if chunks == 1 else lax.fori_loop(0, chunks, from_chunk, total)
        sixteenth = jnp.floor(line[12] * (1.0 / 16.0))
        pieces = rows // 128
        local = jnp.concatenate(
            [prior_ref[...], jnp.zeros((16 - pieces, 128), f32)], axis=0
        ) if pieces < 16 else prior_ref[...]
        steps = local.shape[0]
        parts = jnp.concatenate(split(local, 3), axis=0)
        of_row = jnp.where(
            (iota((3 * steps, CH), 0) % steps).astype(f32) == sixteenth, 1.0, 0.0
        ).astype(bf16)
        priors = dot(parts, of_row, ((0,), (0,)))
        within = line[12] - sixteenth * 16.0
        on_row = jnp.zeros((8, CH), f32)
        for at in range(16):
            on_row = on_row + jnp.where(within == float(at), priors[8 * at : 8 * at + 8, :], 0.0)
        on_row = on_row * (share * line[11])
        sub = iota((8, CH), 0)
        normal = [
            total[8 * k : 8 * k + 8, :] + jnp.where(sub == k, on_row, 0.0) for k in range(8)
        ]
        total = jnp.concatenate(normal + [total[64:128, :]], axis=0)
        high, low = split(total.T, 2)
        value = dot(high, table) + dot(low, table)
        keep = (iota((CH, 128), 1) // 8).astype(f32) == cols_s[a, :, 4:5]
        for k in range(8):
            tiles[pl.ds(a * CH * 8 + k, CH, stride=8), :] = jnp.where(
                keep, value[:, 128 * k : 128 * k + 128], 0.0
            )

    loop(chunks, merge)

    def waiting(a):
        pltpu.make_async_copy(listing.at[a], list_sm.at[a], sem_list.at[a]).wait()
        pltpu.make_async_copy(info.at[a], info_sm.at[a], sem_info.at[a]).wait()

    loop(chunks, waiting)
    extra_sm[0] = 0

    def tile_rows(slot, count=1):
        return pl.ds(pl.multiple_of(slot * 8, 8), 8 * count)

    def pairs(index):
        a, b = (0, 0) if chunks == 1 else (index // chunks, index % chunks)

        def one(key_now):
            number = key_now.astype(i32)
            m1, m2 = number // CH, number % CH
            joining = (m1 == m2) if chunks == 1 else ((m1 == m2) & (a == b))
            r1, c2 = info_sm[a, 0, m1], info_sm[b, 1, m2]
            group, within = c2 // 16, c2 % 16
            position = iota((8, CH), 1)
            total = jnp.zeros((8, 128), f32)
            for j in range(8):
                x = bt[a, 8 * j : 8 * j + 8, :]
                y = bt[b, 8 * j : 8 * j + 8, :]
                x = jnp.sum(jnp.where(position == m1, x, 0.0), axis=1, keepdims=True)
                y = jnp.sum(jnp.where(position == m2, y, 0.0), axis=1, keepdims=True)
                y = jnp.where(lane8 % 8 == row8, y, 0.0)
                y = jnp.sum(y, axis=0, keepdims=True)
                total = total + x * y
            total = jnp.where(lane8 // 8 == within, -total, 0.0)
            total = jnp.where(joining, tiles[tile_rows(a * CH + m1), :], total)

            def search(chunk, carry):
                def at_one(at, slot):
                    hit = (list_sm[chunk, 0, at] == r1) & (list_sm[chunk, 1, at] == group)
                    return jnp.where(hit, chunk * CH + list_sm[chunk, 2, at], slot)
                return lax.fori_loop(0, list_sm[chunk, 3, 0], at_one, carry)

            slot = search(0, -1) if chunks == 1 else lax.fori_loop(0, chunks, search, -1)
            added = extra_sm[0]
            code = r1 * groups + group

            def at_extra(at, slot):
                return jnp.where(extra_sm[1 + at] == code, chunks * CH + at, slot)

            slot = lax.fori_loop(0, added, at_extra, slot)

            @pl.when(slot >= 0)
            def _():
                where = tile_rows(slot)
                tiles[where, :] = tiles[where, :] + total

            @pl.when(slot < 0)
            def _():
                tiles[tile_rows(chunks * CH + added), :] = total
                extra_sm[1 + added] = code
                extra_sm[0] = added + 1

            return jnp.min(jnp.where(keys[...] > key_now, keys[...], BIG))

        smallest = early if chunks == 1 else key_table(a, b)
        lax.while_loop(lambda key_now: key_now < BIG, one, smallest)

    loop(chunks * chunks, pairs)

    def tile_copy(slot, r, group, count=1):
        return pltpu.make_async_copy(
            tiles.at[tile_rows(slot, count), :],
            out_ref.at[tile_rows(r, count), pl.ds(pl.multiple_of(group * 128, 128), 128)],
            sem_out,
        )

    corner = (region == 0) & (column == 0)
    square_copies = [
        pltpu.make_async_copy(
            squares.at[pl.ds(at * 128, 128), :],
            out_ref.at[pl.ds(at * 128, 128), pl.ds(at * 128, 128)],
            sem_sq.at[at],
        )
        for at in range(K_PANELS)
    ]

    @pl.when(corner)
    def _():
        for copy in square_copies:
            copy.start()

    def send(a):
        def four(at, carry):
            for more in range(4):
                entry = at * 4 + more
                tile_copy(
                    a * CH + list_sm[a, 2, entry], list_sm[a, 0, entry], list_sm[a, 1, entry]
                ).start()
            return carry
        lax.fori_loop(0, (list_sm[a, 3, 0] + 3) // 4, four, 0)

    loop(chunks, send)

    def send_extra(at, carry):
        code = extra_sm[1 + at]
        tile_copy(chunks * CH + at, code // groups, code % groups).start()
        return carry

    lax.fori_loop(0, extra_sm[0], send_extra, 0)

    def drain_four(at, carry):
        tile_copy(0, 0, 0, 4).wait()
        return carry

    def drain_one(at, carry):
        tile_copy(0, 0, 0).wait()
        return carry

    def drain(a):
        lax.fori_loop(0, (list_sm[a, 3, 0] + 3) // 4, drain_four, 0)

    loop(chunks, drain)
    lax.fori_loop(0, extra_sm[0], drain_one, 0)

    @pl.when(corner)
    def _():
        for copy in square_copies:
            copy.wait()


def assemble(place, rows, cols, got, prior2, filled):
    count = got.shape[0] // SLOT * 8
    chunks = count // CH
    capacity = rows // 8 * (cols // 128)
    any_space = pl.BlockSpec(memory_space=pl.ANY)
    vmem = pl.BlockSpec(memory_space=pltpu.VMEM)
    return pl.pallas_call(
        functools.partial(assemble_kernel, place, (rows, cols, chunks)),
        out_shape=jax.ShapeDtypeStruct((rows, cols), f32),
        in_specs=[vmem, vmem, any_space],
        out_specs=any_space,
        scratch_shapes=[
            pltpu.VMEM((chunks, 128, CH), f32),
            pltpu.VMEM((chunks, 24, CH), f32),
            pltpu.VMEM((chunks, CH, 128), f32),
            pltpu.VMEM((64, 128), f32),
            pltpu.VMEM((chunks, 64, CH), f32),
            pltpu.VMEM((chunks, 256, CH), bf16),
            pltpu.VMEM(((count + capacity) * 8, 128), f32),
            pltpu.VMEM((CH, CH), f32),
            pltpu.VMEM((PANEL, 128), f32),
            pltpu.VMEM((chunks, 8, CH), i32),
            pltpu.VMEM((chunks, 8, CH), i32),
            pltpu.SMEM((chunks, 8, CH), i32),
            pltpu.SMEM((chunks, 8, CH), i32),
            pltpu.SMEM((1 + capacity,), i32),
            pltpu.SemaphoreType.DMA((chunks,)),
            pltpu.SemaphoreType.DMA((chunks,)),
            pltpu.SemaphoreType.DMA,
            pltpu.SemaphoreType.DMA((K_PANELS,)),
        ],
        input_output_aliases={2: 0},
        compiler_params=pltpu.CompilerParams(vmem_limit_bytes=48 << 20),
        name="assemble",
    )(got, prior2, filled)


def place():
    return lax.axis_index("region"), lax.axis_index("col")


def body(jac, dest, near_pose, prior):
    regions, columns = lax.axis_size("region"), lax.axis_size("col")
    devices = regions * columns
    rows = prior.shape[0]
    cols = rows * regions // columns
    assert jac.shape[0] == 8 and devices * 8 % CH == 0
    assert rows % cols == 0 and rows // 8 <= 256 and regions <= 256
    assert rows >= PANEL and cols >= PANEL and cols % 128 == 0 and columns % 8 == 0
    prior2 = prior.reshape(rows // 128, 128)
    packed = pack(place, jac, dest, near_pose, prior2, devices).reshape(devices, SLOT // 2, 2, 128)
    got = lax.all_to_all(packed, ("region", "col"), split_axis=0, concat_axis=0, tiled=True)
    got = got.reshape(devices * SLOT, 128)
    filled = fill(place, rows, cols, prior2)
    return assemble(place, rows, cols, got, prior2, filled)


def solution(mesh):
    return jax.shard_map(
        body,
        mesh=mesh,
        in_specs=(
            P(("region", "col"), None),
            P(("region", "col"), None),
            P(("region", "col"), None),
            P("region"),
        ),
        out_specs=P("region", "col"),
        check_vma=False,
    )
```

```python
import functools

import jax
import jax.numpy as jnp
from jax import lax
from jax.experimental import pallas as pl
from jax.experimental.pallas import tpu as pltpu
from jax.sharding import PartitionSpec as P

NB = 128
K_PANELS = 2
PANEL = NB * K_PANELS
PP = PANEL // 8
CH = 256
BIG = float(1 << 24)
f32, bf16, i32 = jnp.float32, jnp.bfloat16, jnp.int32


def iota(shape, dim):
    return lax.broadcasted_iota(i32, shape, dim)


def split(x, parts):
    out = []
    for _ in range(parts):
        top = x.astype(bf16)
        out.append(top)
        x = x - top.astype(f32)
    return out


def dot(a, b, dims=((1,), (0,))):
    return lax.dot_general(a, b, (dims, ((), ())), preferred_element_type=f32)


SLOT = 10


def pack_kernel(place, jac_ref, dest_ref, near_ref, prior_ref, out_ref):
    _, column = place()
    lane = iota((1, 128), 1)
    fill_up = jnp.zeros((2, 120), f32)
    dest = jnp.concatenate([dest_ref[...].astype(f32), fill_up], axis=1)
    near = jnp.concatenate([near_ref[...].astype(f32), fill_up], axis=1)
    line = dest[0:1, :] + pltpu.roll(near[0:1, :], 8, 1)
    line = line + pltpu.roll(dest[1:2, :], 16, 1) + pltpu.roll(near[1:2, :], 24, 1)
    column = column % 8
    prior = prior_ref[pl.ds(column // 4, 1), :]
    prior = pltpu.roll(prior, (4 - column % 4) % 4 * 32, 1)
    for at, part in enumerate(split(prior, 3)):
        moved = pltpu.roll(part.astype(f32), 32 * (at + 1), 1)
        line = jnp.where(lane // 32 == at + 1, moved, line)
    slot = jnp.concatenate([jac_ref[...].astype(f32), line, jnp.zeros((1, 128), f32)], axis=0)
    eight = jnp.concatenate([slot] * 8, axis=0).astype(bf16)
    for at in range(out_ref.shape[0] // (8 * SLOT)):
        out_ref[8 * SLOT * at : 8 * SLOT * (at + 1), :] = eight


def pack(place, jac, dest, near_pose, prior2, devices):
    return pl.pallas_call(
        functools.partial(pack_kernel, place),
        out_shape=jax.ShapeDtypeStruct((devices * SLOT, 128), bf16),
        in_specs=[pl.BlockSpec(memory_space=pltpu.VMEM)] * 4,
        out_specs=pl.BlockSpec(memory_space=pltpu.VMEM),
        name="pack",
    )(jac, dest.T, near_pose.T, prior2)


def fill_kernel(place, sizes, prior_ref, out_ref, zeros, squares, sem, sem2):
    rows, cols = sizes
    region, column = place()
    pieces = rows // zeros.shape[0]
    zeros[...] = jnp.zeros_like(zeros)
    step = zeros.shape[0]
    copies = [
        pltpu.make_async_copy(zeros, out_ref.at[pl.ds(at * step, step), :], sem.at[at])
        for at in range(pieces)
    ]
    for copy in copies:
        copy.start()
    start = column * cols - region * rows
    own = (start >= 0) & (start < rows)

    @pl.when(own)
    def _():
        diagonal = iota((128, 128), 0) == iota((128, 128), 1)
        first = start // 128
        for at in range(cols // 128):
            squares[at] = jnp.where(diagonal, prior_ref[pl.ds(first + at, 1), :], 0.0)

    for copy in copies:
        copy.wait()

    @pl.when(own)
    def _():
        base = pl.multiple_of(start, 128)
        patches = [
            pltpu.make_async_copy(
                squares.at[at],
                out_ref.at[pl.ds(base + at * 128, 128), pl.ds(at * 128, 128)],
                sem2.at[at],
            )
            for at in range(cols // 128)
        ]
        for patch in patches:
            patch.start()
        for patch in patches:
            patch.wait()


def fill(place, rows, cols, prior2):
    step = min(256, rows)
    return pl.pallas_call(
        functools.partial(fill_kernel, place, (rows, cols)),
        out_shape=jax.ShapeDtypeStruct((rows, cols), f32),
        out_specs=pl.BlockSpec(memory_space=pl.ANY),
        scratch_shapes=[
            pltpu.VMEM((step, cols), f32),
            pltpu.VMEM((cols // 128, 128, 128), f32),
            pltpu.SemaphoreType.DMA((rows // step,)),
            pltpu.SemaphoreType.DMA((cols // 128,)),
        ],
        cost_estimate=pl.CostEstimate(flops=0, bytes_accessed=rows * cols * 4, transcendentals=0),
        name="fill",
    )(prior2)


def batched(left, right):
    out = []
    for k in range(8):
        total = left[0][k : k + 1, :] * right[0]
        for e in range(1, 8):
            total = total + left[e][k : k + 1, :] * right[e]
        out.append(total)
    return out


def slabs(block):
    return [block[8 * e : 8 * e + 8, :] for e in range(8)]


def to_columns(rows):
    full = jnp.concatenate([rows, jnp.zeros((120, CH), f32)], axis=0)
    return full.T


def cholesky(a):
    row = iota((8, 128), 0)
    columns, scales = [], []
    a = list(a)
    for j in range(8):
        pivot = a[j][j : j + 1, :]
        scale = lax.rsqrt(pivot)
        scale = scale * (1.5 - 0.5 * pivot * scale * scale)
        column = jnp.where(row >= j, a[j] * scale, 0.0)
        for k in range(j + 1, 8):
            a[k] = a[k] - column * column[k : k + 1, :]
        columns.append(column)
        scales.append(scale)
    inverse = []
    for i in range(8):
        x = jnp.where(row == i, 1.0, 0.0)
        for j in range(i, 8):
            value = x[j : j + 1, :] * scales[j]
            x = jnp.where(row == j, value, jnp.where(row > j, x - columns[j] * value, x))
        inverse.append(x)
    return columns, inverse


def loop(count, body):
    if count == 1:
        body(0)
    else:
        lax.fori_loop(0, count, lambda at, carry: (body(at), carry)[1], 0)


def expansion():
    row, lane = iota((8, 128), 0), iota((8, 128), 1)
    none = jnp.zeros((8, 128), f32)
    straight = jnp.where(lane % 8 == row, 1.0, 0.0)
    by_rows = [
        jnp.concatenate([straight if at == k else none for at in range(8)], axis=1)
        for k in range(8)
    ]
    by_columns = [
        jnp.concatenate(
            [jnp.where((row == at) & (lane % 8 == j), 1.0, 0.0) for at in range(8)], axis=1
        )
        for j in range(8)
    ]
    return jnp.concatenate((by_rows + by_columns) * 2, axis=0).astype(bf16)


def label_rows(got_ref, a):
    per = CH // 8
    block = got_ref[pl.ds(a * per * SLOT, per * SLOT), :].astype(f32)
    return jnp.concatenate([block[SLOT * d + 8 : SLOT * d + 9, :] for d in range(per)], axis=0)


def jac_columns(got_ref, a):
    per = CH // 8
    block = got_ref[pl.ds(a * per * SLOT, per * SLOT), :].astype(f32)
    return jnp.concatenate([block[SLOT * d : SLOT * d + 8, :] for d in range(per)], axis=0).T


def spread(labels):
    lane8, row8 = iota((8, 128), 1), iota((8, 128), 0)
    out = []
    for at in range(4):
        halves = []
        for half in range(2):
            total = jnp.zeros((8, 128), f32)
            for part in range(2):
                from_row = 16 * half + 8 * part
                piece = labels[from_row : from_row + 8, :]
                if at:
                    piece = pltpu.roll(piece, 128 - 8 * at, 1)
                piece = pltpu.roll(piece, 64 * part, 1, stride=8, stride_axis=0)
                total = total + jnp.where(lane8 // 8 == row8 + 8 * part, piece, 0.0)
            halves.append(jnp.sum(total, axis=0, keepdims=True))
        out.append(jnp.concatenate(halves, axis=1))
    return out


def on_diagonal(prior_row):
    kl, unknown = iota((64, PANEL), 0), iota((64, PANEL), 1)
    diagonal = jnp.where((kl // 8 == kl % 8) & (unknown % 8 == kl % 8), prior_row, 0.0)
    own_pose = jnp.where(iota((PANEL, 128), 0) // 8 == iota((PANEL, 128), 1), 1.0, 0.0).astype(bf16)
    first = dot(jnp.concatenate(split(diagonal, 3), axis=0), own_pose)
    kl = iota((64, 128), 0)
    spare = (kl // 8 == kl % 8) & (iota((64, 128), 1) >= PP)
    return first[0:64] + first[64:128] + first[128:192] + jnp.where(spare, 1.0, 0.0)


def first_region(place, sizes, got_ref, prior_ref, out_ref, app, squares, sem):
    rows, cols, chunks = sizes
    col_poses, groups = cols // 8, cols // 128
    _, column = place()
    column_f = column.astype(f32)
    start = pl.multiple_of(column * cols, 128)
    local = prior_ref[pl.ds(column * groups, groups), :]
    prior_row = jnp.concatenate([prior_ref[0:1, :], prior_ref[1:2, :]], axis=1)
    first = on_diagonal(prior_row)
    app[...] = jnp.zeros_like(app)

    def measure(a):
        jac_t = jac_columns(got_ref, a)
        d0, n0, d1, n1 = spread(label_rows(got_ref, a))
        here0 = d0 == 0
        pose = jnp.where(here0, n0, n1) - column_f * col_poses
        inside = (here0 | (d1 == 0)) & (pose >= 0) & (pose < col_poses)
        pose = jnp.where(inside, pose, -1.0)
        columns = to_columns(jnp.concatenate([pose, jnp.zeros((7, CH), f32)], axis=0))
        j0, j1 = slabs(jac_t[0:64, :]), slabs(jac_t[64:128, :])
        side = [jnp.where(here0, x, y) for x, y in zip(j0, j1)]
        gram = jnp.concatenate(batched(side, side), axis=0)
        of_pose = jnp.where(
            columns[:, 0:1] == iota((CH, 128), 1).astype(f32), 1.0, 0.0
        ).astype(bf16)
        total = dot(jnp.concatenate(split(gram, 3), axis=0), of_pose)
        app[...] += total[0:64] + total[64:128] + total[128:192]

    loop(chunks, measure)
    gram = app[...]
    factor, _ = cholesky(slabs(gram + first))
    lane, here = iota((64, 128), 1), jnp.where(column == 0, PP, 0)
    in_panel = lane < here
    both = [jnp.where(in_panel, 0.0, gram), jnp.where(in_panel, jnp.concatenate(factor, axis=0), 0.0)]
    both = jnp.concatenate(both, axis=0).T
    value = dot(jnp.concatenate(split(both, 2), axis=1), expansion())
    pose, lane = iota((128, 128), 0), iota((128, 128), 1)
    weights = [jnp.broadcast_to(local[at : at + 1, :], (16, 128)) for at in range(groups)]
    weights += [jnp.zeros((16, 128), f32)] * (8 - groups)
    weights = jnp.where(pose < here, 0.0, jnp.concatenate(weights, axis=0))
    keep, lane_in, group_lane = lane // 8 == pose % 16, lane % 8, lane // 8
    for k in range(8):
        piece = jnp.where(keep, value[:, 128 * k : 128 * k + 128], 0.0)
        piece = piece + jnp.where(keep & (lane_in == k), weights, 0.0)
        squares[pl.ds(k, 128, stride=8), :] = piece
    copies = [
        pltpu.make_async_copy(
            squares.at[pl.ds(at * 128, 128), :],
            out_ref.at[pl.ds(start + at * 128, 128), pl.ds(at * 128, 128)],
            sem.at[at],
        )
        for at in range(groups)
    ]
    for copy in copies:
        copy.start()
    for copy in copies:
        copy.wait()


def general(place, sizes, got_ref, prior_ref, out_ref,
                    jt, rows_s, cols_s, app, bt, blk, tiles, keys,
                    listing, info, list_sm, info_sm, extra_sm, sem_list, sem_info, sem_out):
    rows, cols, chunks = sizes
    row_poses, col_poses, groups = rows // 8, cols // 8, cols // 128
    region, column = place()
    region_f, column_f = region.astype(f32), column.astype(f32)
    start = column * cols - region * rows
    own = (start >= 0) & (start < rows)
    share = jnp.where(own, 1.0, 0.0)
    lane8, row8 = iota((8, 128), 1), iota((8, 128), 0)
    before = iota((CH, CH), 0) < iota((CH, CH), 1)
    table = expansion()

    labels0 = label_rows(got_ref, 0)
    sent = labels0[0:8, :]
    panel_prior = jnp.zeros((8, 128), f32)
    for at in range(3):
        panel_prior = panel_prior + pltpu.roll(sent, 128 - 32 * (at + 1), 1)
    panel_prior = jnp.where(lane8 < 32, panel_prior, 0.0)
    lined = jnp.zeros((8, 128), f32)
    for at in range(4):
        moved = panel_prior if at == 0 else pltpu.roll(panel_prior, 32 * at, 1)
        lined = lined + jnp.where(row8 % 4 == at, moved, 0.0)
    halves = [
        jnp.sum(jnp.where(row8 < 4, lined, 0.0), axis=0, keepdims=True),
        jnp.sum(jnp.where(row8 >= 4, lined, 0.0), axis=0, keepdims=True),
    ]
    prior_row = jnp.concatenate(halves, axis=1)
    app[...] = on_diagonal(prior_row)

    def measure(a):
        jac_t = jac_columns(got_ref, a)
        jt[a] = jac_t
        d0, n0, d1, n1 = spread(labels0 if chunks == 1 else label_rows(got_ref, a))
        c0 = d0 * row_poses + n0 - column_f * col_poses
        c1 = d1 * row_poses + n1 - column_f * col_poses
        one, none = jnp.ones_like(d0), jnp.zeros_like(d0)
        row0, row1 = d0 == region_f, d1 == region_f
        col0, col1 = (c0 >= 0) & (c0 < col_poses), (c1 >= 0) & (c1 < col_poses)
        pan0, pan1 = (d0 == 0) & (n0 < PP), (d1 == 0) & (n1 < PP)
        has_row = jnp.where(row0 | row1, one, none)
        has_col = jnp.where(col0 | col1, one, none)
        touches = jnp.where(pan0 | pan1, one, none)
        row_pose = jnp.where(row0, n0, n1)
        col_pose = jnp.where(col0, c0, c1)
        pan_side = jnp.where(pan0, none, one)
        pan_pose = jnp.where(pan0, n0, n1)
        row_in_panel = jnp.where((row0 & pan0) | (row1 & pan1), one, none)
        col_in_panel = jnp.where((col0 & pan0) | (col1 & pan1), one, none)
        relevant = has_row * has_col * (1.0 - row_in_panel)
        group = jnp.floor(col_pose * (1.0 / 16.0))
        tile = row_pose * groups + group
        cell = row_pose * col_poses + col_pose
        is_row = touches * has_row * (1.0 - row_in_panel)
        is_col = touches * has_col * (1.0 - col_in_panel)
        lines = [
            jnp.where(relevant > 0, tile, -1.0),
            jnp.where(relevant > 0, cell, -1.0),
            jnp.where(touches > 0, pan_pose, -1.0),
            jnp.where(is_row > 0, pan_pose, -1.0),
            col_pose - group * 16.0,
            none, none, none,
        ]
        more = [
            jnp.where(relevant > 0, tile, -2.0),
            jnp.where(relevant > 0, cell, -2.0),
            jnp.where(is_col > 0, pan_pose, -2.0),
            relevant,
            row_pose,
            group,
            col_pose,
            is_row * is_col,
            jnp.where(row0, none, one),
            jnp.where(col0, none, one),
            pan_side,
            col_in_panel,
            none, none, none, none,
        ]
        lines = jnp.concatenate(lines, axis=0)
        rows_s[a] = jnp.concatenate([lines] + more, axis=0)
        columns = to_columns(lines)
        cols_s[a] = columns
        j0, j1 = slabs(jac_t[0:64, :]), slabs(jac_t[64:128, :])
        near = [jnp.where(pan_side == 0, x, y) for x, y in zip(j0, j1)]
        gram = jnp.concatenate(batched(near, near), axis=0)
        of_pose = jnp.where(
            columns[:, 2:3] == iota((CH, 128), 1).astype(f32), 1.0, 0.0
        ).astype(bf16)
        total = dot(jnp.concatenate(split(gram, 3), axis=0), of_pose)
        app[...] += total[0:64] + total[64:128] + total[128:192]

    loop(chunks, measure)

    def earlier_of(a, at, at_right):
        def from_chunk(b, count):
            other = jnp.broadcast_to(cols_s[b, :, at : at + 1], (CH, CH))
            same = jnp.where(other == rows_s[a, at_right : at_right + 1, :], 1.0, 0.0)
            if chunks == 1:
                same = jnp.where(before, same, 0.0)
            else:
                here, all_of_it = jnp.where(b == a, 1.0, 0.0), jnp.where(b < a, 1.0, 0.0)
                same = jnp.where(before, same, 0.0) * here + same * all_of_it
            return count + jnp.sum(same, axis=0, keepdims=True)

        nothing = jnp.zeros((1, CH), f32)
        return from_chunk(0, nothing) if chunks == 1 else lax.fori_loop(0, chunks, from_chunk, nothing)

    def lists(a):
        relevant = rows_s[a, 11:12, :]
        kept = jnp.where(earlier_of(a, 0, 8) == 0, relevant, 0.0)
        lone = jnp.where(earlier_of(a, 1, 9) == 0, relevant, 0.0)
        joins = lone * (1.0 - kept)
        rows_s[a, 20:21, :] = kept
        count = jnp.sum(kept, axis=1, keepdims=True)
        upper = jnp.where(before, 1.0, 0.0).astype(bf16)
        rank = dot(jnp.broadcast_to(kept, (16, CH)).astype(bf16), upper)[0:1, :]
        slot = iota((CH, CH), 0)
        slot = (slot % 64 * 4 + slot // 64).astype(f32)
        slot = jnp.where(slot < count, slot, 0.0)
        chosen = jnp.where((rank == slot) & (kept > 0), 1.0, 0.0).astype(bf16)
        position = iota((1, CH), 1).astype(f32)
        data = jnp.concatenate(
            [rows_s[a, 12:13, :], rows_s[a, 13:14, :], position, jnp.zeros((13, CH), f32)], axis=0
        ).astype(bf16)
        found = dot(data, chosen, ((1,), (1,)))[0:8, :]
        code = found[2:3, :] + found[0:1, :] * 256.0 + found[1:2, :] * 65536.0
        line = [code[:, 0:128], pltpu.roll(code[:, 0:128], 64, 1)]
        line += [code[:, 128:256], pltpu.roll(code[:, 128:256], 64, 1)]
        line += [jnp.broadcast_to(count, (1, 128)), jnp.zeros((3, 128), f32)]
        listing[a] = jnp.concatenate(line, axis=0).astype(i32)
        pltpu.make_async_copy(listing.at[a], list_sm.at[a], sem_list.at[a]).start()
        info[a] = jnp.concatenate(
            [rows_s[a, 12:13, :], rows_s[a, 14:15, :], joins, jnp.zeros((5, CH), f32)], axis=0
        ).astype(i32)
        pltpu.make_async_copy(info.at[a], info_sm.at[a], sem_info.at[a]).start()

    loop(chunks, lists)

    def key_table(a, b):
        left = jnp.broadcast_to(cols_s[a, :, 3:4], (CH, CH))
        valid = jnp.where(left == rows_s[b, 10:11, :], 1.0, 0.0)
        same = iota((CH, CH), 0) == iota((CH, CH), 1)
        joins = info[a, 2:3, :].astype(f32)
        if chunks > 1:
            flag = jnp.where(a == b, 1.0, 0.0)
            joins = joins * flag + valid * (1.0 - flag)
        valid = jnp.where(same, joins, valid)
        key = (iota((CH, CH), 0) * CH + iota((CH, CH), 1)).astype(f32)
        key = jnp.where(valid > 0, key, BIG)
        keys[...] = key
        return jnp.min(key)

    early = key_table(0, 0) if chunks == 1 else None

    _, inverse = cholesky(slabs(app[...]))
    inverse = jnp.concatenate(split(jnp.concatenate(inverse, axis=0), 3), axis=0)

    def blocks(a):
        row = [rows_s[a, at : at + 1, :] for at in range(24)]
        jac_t = jt[a]
        j0, j1 = slabs(jac_t[0:64, :]), slabs(jac_t[64:128, :])
        left = [jnp.where(row[16] == 0, x, y) for x, y in zip(j0, j1)]
        right = [jnp.where(row[17] == 0, x, y) for x, y in zip(j0, j1)]
        near = [jnp.where(row[18] == 0, x, y) for x, y in zip(j0, j1)]
        far = [jnp.where(row[18] == 0, y, x) for x, y in zip(j0, j1)]
        gram = batched(left, right)
        cross = batched(near, far)
        of_pose = jnp.where(iota((128, CH), 0).astype(f32) == row[2], 1.0, 0.0).astype(bf16)
        inv = dot(inverse, of_pose)
        inv = slabs(inv[0:64] + inv[64:128] + inv[128:192])
        solved = []
        for j in range(8):
            total = inv[0][j : j + 1, :] * cross[0]
            for i in range(1, j + 1):
                total = total + inv[i][j : j + 1, :] * cross[i]
            solved.append(total)
        bt[a] = jnp.concatenate(solved, axis=0)
        outer = batched(solved, solved)
        keep_normal = row[11] * (1.0 - row[19])
        keep_panel = row[11] * row[19]
        values = [(g - o * row[15]) * keep_normal for g, o in zip(gram, outer)]
        values += [x * keep_panel for x in solved]
        values = jnp.concatenate(values, axis=0)
        high, low = split(values, 2)
        blk[a] = jnp.concatenate([high, low], axis=0)

    loop(chunks, blocks)

    def merge(a):
        line = [rows_s[a, at : at + 1, :] for at in range(24)]

        def from_chunk(b, total):
            other = jnp.broadcast_to(cols_s[b, :, 1:2], (CH, CH))
            same = jnp.where(other == line[9], 1.0, 0.0).astype(bf16)
            found = dot(blk[b], same)
            return total + found[0:128] + found[128:256]

        total = jnp.zeros((128, CH), f32)
        total = from_chunk(0, total) if chunks == 1 else lax.fori_loop(0, chunks, from_chunk, total)
        sixteenth = jnp.floor(line[12] * (1.0 / 16.0))
        pieces = rows // 128
        local = jnp.concatenate(
            [prior_ref[...], jnp.zeros((16 - pieces, 128), f32)], axis=0
        ) if pieces < 16 else prior_ref[...]
        steps = local.shape[0]
        parts = jnp.concatenate(split(local, 3), axis=0)
        of_row = jnp.where(
            (iota((3 * steps, CH), 0) % steps).astype(f32) == sixteenth, 1.0, 0.0
        ).astype(bf16)
        priors = dot(parts, of_row, ((0,), (0,)))
        within = line[12] - sixteenth * 16.0
        on_row = jnp.zeros((8, CH), f32)
        for at in range(16):
            on_row = on_row + jnp.where(within == float(at), priors[8 * at : 8 * at + 8, :], 0.0)
        on_row = on_row * (share * line[11])
        sub = iota((8, CH), 0)
        normal = [
            total[8 * k : 8 * k + 8, :] + jnp.where(sub == k, on_row, 0.0) for k in range(8)
        ]
        total = jnp.concatenate(normal + [total[64:128, :]], axis=0)
        value = dot(jnp.concatenate(split(total.T, 2), axis=1), table)
        keep = (iota((CH, 128), 1) // 8).astype(f32) == cols_s[a, :, 4:5]
        for k in range(8):
            tiles[pl.ds(a * CH * 8 + k, CH, stride=8), :] = jnp.where(
                keep, value[:, 128 * k : 128 * k + 128], 0.0
            )

    loop(chunks, merge)

    def waiting(a):
        pltpu.make_async_copy(listing.at[a], list_sm.at[a], sem_list.at[a]).wait()
        pltpu.make_async_copy(info.at[a], info_sm.at[a], sem_info.at[a]).wait()

    loop(chunks, waiting)
    extra_sm[0] = 0

    def tile_rows(slot, count=1):
        return pl.ds(pl.multiple_of(slot * 8, 8), 8 * count)

    def pairs(index):
        a, b = (0, 0) if chunks == 1 else (index // chunks, index % chunks)

        def one(key_now):
            number = key_now.astype(i32)
            m1, m2 = number >> 8, number & (CH - 1)
            joining = (m1 == m2) if chunks == 1 else ((m1 == m2) & (a == b))
            r1, c2 = info_sm[a, 0, m1], info_sm[b, 1, m2]
            group, within = c2 >> 4, c2 & 15
            code = r1 * groups + group
            code_f = code.astype(f32)
            key_next = jnp.min(jnp.where(keys[...] > key_now, keys[...], BIG))

            def search(chunk, best):
                at_one = (rows_s[chunk, 8:9, :] == code_f) & (rows_s[chunk, 20:21, :] > 0)
                slots = (iota((1, CH), 1) + chunk * CH).astype(f32)
                return jnp.minimum(best, jnp.min(jnp.where(at_one, slots, BIG)))

            slot = search(0, BIG) if chunks == 1 else lax.fori_loop(0, chunks, search, BIG)
            position = iota((8, CH), 1)
            total = jnp.zeros((8, 128), f32)
            for j in range(8):
                x = bt[a, 8 * j : 8 * j + 8, :]
                y = bt[b, 8 * j : 8 * j + 8, :]
                x = jnp.sum(jnp.where(position == m1, x, 0.0), axis=1, keepdims=True)
                y = jnp.sum(jnp.where(position == m2, y, 0.0), axis=1, keepdims=True)
                y = jnp.where(lane8 % 8 == row8, y, 0.0)
                y = jnp.sum(y, axis=0, keepdims=True)
                total = total + x * y
            total = jnp.where(lane8 // 8 == within, -total, 0.0)
            total = jnp.where(joining, tiles[tile_rows(a * CH + m1), :], total)
            added = extra_sm[0]
            slot = jnp.where(slot < BIG, slot, -1.0).astype(i32)

            def at_extra(at, slot):
                return jnp.where(extra_sm[1 + at] == code, chunks * CH + at, slot)

            slot = lax.fori_loop(0, added, at_extra, slot)
            fresh = slot < 0
            slot = jnp.where(fresh, chunks * CH + added, slot)
            where = tile_rows(slot)
            tiles[where, :] = jnp.where(fresh, 0.0, tiles[where, :]) + total

            @pl.when(fresh)
            def _():
                extra_sm[1 + added] = code
                extra_sm[0] = added + 1

            return key_next

        smallest = early if chunks == 1 else key_table(a, b)
        lax.while_loop(lambda key_now: key_now < BIG, one, smallest)

    loop(chunks * chunks, pairs)

    def tile_copy(slot, r, group, count=1):
        return pltpu.make_async_copy(
            tiles.at[tile_rows(slot, count), :],
            out_ref.at[tile_rows(r, count), pl.ds(pl.multiple_of(group * 128, 128), 128)],
            sem_out,
        )

    def send(a):
        def four(at, carry):
            for more in range(4):
                entry = list_sm[a, more, at]
                slot, r = a * CH + (entry & 255), (entry >> 8) & 255
                tile_copy(slot, r, entry >> 16).start()
            return carry
        lax.fori_loop(0, (list_sm[a, 4, 0] + 3) // 4, four, 0)

    loop(chunks, send)

    def send_extra(at, carry):
        code = extra_sm[1 + at]
        tile_copy(chunks * CH + at, code // groups, code % groups).start()
        return carry

    lax.fori_loop(0, extra_sm[0], send_extra, 0)

    def drain_four(at, carry):
        tile_copy(0, 0, 0, 4).wait()
        return carry

    def drain_one(at, carry):
        tile_copy(0, 0, 0).wait()
        return carry

    def drain(a):
        lax.fori_loop(0, (list_sm[a, 4, 0] + 3) // 4, drain_four, 0)

    loop(chunks, drain)
    lax.fori_loop(0, extra_sm[0], drain_one, 0)


def assemble_kernel(place, sizes, got_ref, prior_ref, filled_ref, out_ref,
                    jt, rows_s, cols_s, app, bt, blk, tiles, keys,
                    listing, info, list_sm, info_sm, extra_sm, sem_list, sem_info, sem_out,
                    squares, sem_sq):
    del filled_ref
    rows, cols, _ = sizes
    region, column = place()
    first = (region == 0) & (column * cols < rows)

    @pl.when(first)
    def _():
        first_region(place, sizes, got_ref, prior_ref, out_ref, app, squares, sem_sq)

    @pl.when(jnp.logical_not(first))
    def _():
        general(place, sizes, got_ref, prior_ref, out_ref, jt, rows_s, cols_s, app, bt, blk,
                tiles, keys, listing, info, list_sm, info_sm, extra_sm, sem_list, sem_info, sem_out)


def assemble(place, rows, cols, got, prior2, filled):
    count = got.shape[0] // SLOT * 8
    chunks = count // CH
    capacity = rows // 8 * (cols // 128)
    any_space = pl.BlockSpec(memory_space=pl.ANY)
    vmem = pl.BlockSpec(memory_space=pltpu.VMEM)
    return pl.pallas_call(
        functools.partial(assemble_kernel, place, (rows, cols, chunks)),
        out_shape=jax.ShapeDtypeStruct((rows, cols), f32),
        in_specs=[vmem, vmem, any_space],
        out_specs=any_space,
        scratch_shapes=[
            pltpu.VMEM((chunks, 128, CH), f32),
            pltpu.VMEM((chunks, 24, CH), f32),
            pltpu.VMEM((chunks, CH, 128), f32),
            pltpu.VMEM((64, 128), f32),
            pltpu.VMEM((chunks, 64, CH), f32),
            pltpu.VMEM((chunks, 256, CH), bf16),
            pltpu.VMEM(((count + capacity) * 8, 128), f32),
            pltpu.VMEM((CH, CH), f32),
            pltpu.VMEM((chunks, 8, 128), i32),
            pltpu.VMEM((chunks, 8, CH), i32),
            pltpu.SMEM((chunks, 8, 128), i32),
            pltpu.SMEM((chunks, 8, CH), i32),
            pltpu.SMEM((1 + capacity,), i32),
            pltpu.SemaphoreType.DMA((chunks,)),
            pltpu.SemaphoreType.DMA((chunks,)),
            pltpu.SemaphoreType.DMA,
            pltpu.VMEM((1024, 128), f32),
            pltpu.SemaphoreType.DMA((cols // 128,)),
        ],
        input_output_aliases={2: 0},
        compiler_params=pltpu.CompilerParams(vmem_limit_bytes=48 << 20),
        name="assemble",
    )(got, prior2, filled)


def place():
    return lax.axis_index("region"), lax.axis_index("col")


def body(jac, dest, near_pose, prior):
    regions, columns = lax.axis_size("region"), lax.axis_size("col")
    devices = regions * columns
    rows = prior.shape[0]
    cols = rows * regions // columns
    assert jac.shape[0] == 8 and devices * 8 % CH == 0
    assert rows % cols == 0 and rows // 8 <= 256 and regions <= 256
    assert cols // 8 <= 128 and rows // 8 * (cols // 128) <= 2048
    assert rows >= PANEL and cols >= PANEL and cols % 128 == 0 and columns % 8 == 0
    prior2 = prior.reshape(rows // 128, 128)
    packed = pack(place, jac, dest, near_pose, prior2, devices).reshape(devices, SLOT // 2, 2, 128)
    got = lax.all_to_all(packed, ("region", "col"), split_axis=0, concat_axis=0, tiled=True)
    got = got.reshape(devices * SLOT, 128)
    filled = fill(place, rows, cols, prior2)
    return assemble(place, rows, cols, got, prior2, filled)


def solution(mesh):
    return jax.shard_map(
        body,
        mesh=mesh,
        in_specs=(
            P(("region", "col"), None),
            P(("region", "col"), None),
            P(("region", "col"), None),
            P("region"),
        ),
        out_specs=P("region", "col"),
        check_vma=False,
    )
```

```python
import functools

import jax
import jax.numpy as jnp
from jax import lax
from jax.experimental import pallas as pl
from jax.experimental.pallas import tpu as pltpu
from jax.sharding import PartitionSpec as P

NB = 128
K_PANELS = 2
PANEL = NB * K_PANELS
PP = PANEL // 8
CH = 256
BIG = float(1 << 24)
f32, bf16, i32 = jnp.float32, jnp.bfloat16, jnp.int32


def iota(shape, dim):
    return lax.broadcasted_iota(i32, shape, dim)


def split(x, parts):
    out = []
    for _ in range(parts):
        top = x.astype(bf16)
        out.append(top)
        x = x - top.astype(f32)
    return out


def dot(a, b, dims=((1,), (0,))):
    return lax.dot_general(a, b, (dims, ((), ())), preferred_element_type=f32)


SLOT = 10
LABEL_AT = (0, 56, 64, 120)


def pack_kernel(place, jac_ref, dest_ref, near_ref, prior_ref, out_ref):
    _, column = place()
    shape = (8, 128)
    lane, row = iota(shape, 1), iota(shape, 0)
    fill_up = jnp.zeros((2, 120), f32)
    dest = jnp.concatenate([dest_ref[...].astype(f32), fill_up], axis=1)
    near = jnp.concatenate([near_ref[...].astype(f32), fill_up], axis=1)
    labels = jnp.zeros(shape, f32)
    for at, line in zip(LABEL_AT, (dest[0:1, :], near[0:1, :], dest[1:2, :], near[1:2, :])):
        line = jnp.broadcast_to(line, shape)
        labels = labels + (pltpu.roll(line, at, 1) if at else line)
    column = column % 8
    prior = jnp.broadcast_to(prior_ref[pl.ds(column // 4, 1), :], shape)
    weights = jnp.zeros(shape, f32)
    for at, part in enumerate(split(prior, 3)):
        moved = pltpu.roll(part.astype(f32), (4 + at - column % 4) % 4 * 32, 1)
        weights = jnp.where(lane // 32 == at, moved, weights)
    jac = jac_ref[...].astype(f32)
    turned = [jac if not at else pltpu.roll(jac, 2 * at, 0) for at in range(4)]
    pieces = []
    for at in range(SLOT):
        piece = jnp.zeros(shape, f32)
        for slot in range(8):
            first = SLOT * slot - 8 * at
            if -SLOT < first < 8:
                piece = jnp.where((row >= first) & (row < first + 8), turned[slot % 4], piece)
                piece = jnp.where(row == first + 8, labels, piece)
                piece = jnp.where(row == first + 9, weights, piece)
        pieces.append(piece)
    eight = jnp.concatenate(pieces, axis=0).astype(bf16)
    for at in range(out_ref.shape[0] // (8 * SLOT)):
        out_ref[8 * SLOT * at : 8 * SLOT * (at + 1), :] = eight


def pack(place, jac, dest, near_pose, prior2, devices):
    return pl.pallas_call(
        functools.partial(pack_kernel, place),
        out_shape=jax.ShapeDtypeStruct((devices * SLOT, 128), bf16),
        in_specs=[pl.BlockSpec(memory_space=pltpu.VMEM)] * 4,
        out_specs=pl.BlockSpec(memory_space=pltpu.VMEM),
        name="pack",
    )(jac, dest.T, near_pose.T, prior2)


def fill_kernel(place, sizes, prior_ref, out_ref, zeros, squares, sem, sem2):
    rows, cols = sizes
    region, column = place()
    pieces = rows // zeros.shape[0]
    zeros[...] = jnp.zeros_like(zeros)
    step = zeros.shape[0]
    copies = [
        pltpu.make_async_copy(zeros, out_ref.at[pl.ds(at * step, step), :], sem.at[at])
        for at in range(pieces)
    ]
    for copy in copies:
        copy.start()
    start = column * cols - region * rows
    own = (start >= 0) & (start < rows)

    @pl.when(own)
    def _():
        diagonal = iota((128, 128), 0) == iota((128, 128), 1)
        first = start // 128
        for at in range(cols // 128):
            squares[at] = jnp.where(diagonal, prior_ref[pl.ds(first + at, 1), :], 0.0)

    for copy in copies:
        copy.wait()

    @pl.when(own)
    def _():
        base = pl.multiple_of(start, 128)
        patches = [
            pltpu.make_async_copy(
                squares.at[at],
                out_ref.at[pl.ds(base + at * 128, 128), pl.ds(at * 128, 128)],
                sem2.at[at],
            )
            for at in range(cols // 128)
        ]
        for patch in patches:
            patch.start()
        for patch in patches:
            patch.wait()


def fill(place, rows, cols, prior2):
    step = min(256, rows)
    return pl.pallas_call(
        functools.partial(fill_kernel, place, (rows, cols)),
        out_shape=jax.ShapeDtypeStruct((rows, cols), f32),
        out_specs=pl.BlockSpec(memory_space=pl.ANY),
        scratch_shapes=[
            pltpu.VMEM((step, cols), f32),
            pltpu.VMEM((cols // 128, 128, 128), f32),
            pltpu.SemaphoreType.DMA((rows // step,)),
            pltpu.SemaphoreType.DMA((cols // 128,)),
        ],
        cost_estimate=pl.CostEstimate(flops=0, bytes_accessed=rows * cols * 4, transcendentals=0),
        name="fill",
    )(prior2)


def batched(left, right):
    out = []
    for k in range(8):
        total = left[0][k : k + 1, :] * right[0]
        for e in range(1, 8):
            total = total + left[e][k : k + 1, :] * right[e]
        out.append(total)
    return out


def slabs(block):
    return [block[8 * e : 8 * e + 8, :] for e in range(8)]


def to_columns(rows):
    full = jnp.concatenate([rows, jnp.zeros((120, CH), f32)], axis=0)
    return full.T


def cholesky(a):
    row = iota((8, 128), 0)
    columns, scales = [], []
    a = list(a)
    for j in range(8):
        pivot = a[j][j : j + 1, :]
        scale = lax.rsqrt(pivot)
        scale = scale * (1.5 - 0.5 * pivot * scale * scale)
        column = jnp.where(row >= j, a[j] * scale, 0.0)
        for k in range(j + 1, 8):
            a[k] = a[k] - column * column[k : k + 1, :]
        columns.append(column)
        scales.append(scale)
    inverse = []
    for i in range(8):
        x = jnp.where(row == i, 1.0, 0.0)
        for j in range(i, 8):
            value = x[j : j + 1, :] * scales[j]
            x = jnp.where(row == j, value, jnp.where(row > j, x - columns[j] * value, x))
        inverse.append(x)
    return columns, inverse


def loop(count, body):
    if count == 1:
        body(0)
    else:
        lax.fori_loop(0, count, lambda at, carry: (body(at), carry)[1], 0)


def expansion():
    row, lane = iota((8, 128), 0), iota((8, 128), 1)
    none = jnp.zeros((8, 128), f32)
    straight = jnp.where(lane % 8 == row, 1.0, 0.0)
    by_rows = [
        jnp.concatenate([straight if at == k else none for at in range(8)], axis=1)
        for k in range(8)
    ]
    by_columns = [
        jnp.concatenate(
            [jnp.where((row == at) & (lane % 8 == j), 1.0, 0.0) for at in range(8)], axis=1
        )
        for j in range(8)
    ]
    return jnp.concatenate((by_rows + by_columns) * 2, axis=0).astype(bf16)


def slot_rows(got_ref, a, at, per):
    block = got_ref[pl.ds(a * (CH // 8) * SLOT, per * SLOT), :].astype(f32)
    return jnp.concatenate([block[SLOT * d + at : SLOT * d + at + 1, :] for d in range(per)], axis=0)


def label_rows(got_ref, a):
    return slot_rows(got_ref, a, 8, CH // 8)


def jac_columns(got_ref, a):
    per = CH // 8
    block = got_ref[pl.ds(a * per * SLOT, per * SLOT), :].astype(f32)
    return jnp.concatenate([block[SLOT * d : SLOT * d + 8, :] for d in range(per)], axis=0).T


def spread(labels):
    lane8, row8 = iota((8, 128), 1), iota((8, 128), 0)
    out = []
    for at in LABEL_AT:
        halves = []
        for half in range(2):
            total = jnp.zeros((8, 128), f32)
            for part in range(2):
                from_row = 16 * half + 8 * part
                piece = labels[from_row : from_row + 8, :]
                piece = pltpu.roll(piece, (64 * part - at) % 128, 1, stride=8, stride_axis=0)
                total = total + jnp.where(lane8 // 8 == row8 + 8 * part, piece, 0.0)
            halves.append(jnp.sum(total, axis=0, keepdims=True))
        out.append(jnp.concatenate(halves, axis=1))
    return out


def on_diagonal(prior_row):
    kl, unknown = iota((64, PANEL), 0), iota((64, PANEL), 1)
    diagonal = jnp.where((kl // 8 == kl % 8) & (unknown % 8 == kl % 8), prior_row, 0.0)
    own_pose = jnp.where(iota((PANEL, 128), 0) // 8 == iota((PANEL, 128), 1), 1.0, 0.0).astype(bf16)
    first = dot(jnp.concatenate(split(diagonal, 3), axis=0), own_pose)
    kl = iota((64, 128), 0)
    spare = (kl // 8 == kl % 8) & (iota((64, 128), 1) >= PP)
    return first[0:64] + first[64:128] + first[128:192] + jnp.where(spare, 1.0, 0.0)


def first_region(place, sizes, got_ref, prior_ref, out_ref, app, squares, sem):
    rows, cols, chunks = sizes
    col_poses, groups = cols // 8, cols // 128
    _, column = place()
    column_f = column.astype(f32)
    start = pl.multiple_of(column * cols, 128)
    local = prior_ref[pl.ds(column * groups, groups), :]
    prior_row = jnp.concatenate([prior_ref[0:1, :], prior_ref[1:2, :]], axis=1)
    first = on_diagonal(prior_row)
    app[...] = jnp.zeros_like(app)

    def measure(a):
        jac_t = jac_columns(got_ref, a)
        d0, n0, d1, n1 = spread(label_rows(got_ref, a))
        grams, of_pose = [], []
        for at, (region_of, number) in enumerate(((d0, n0), (d1, n1))):
            side = slabs(jac_t[64 * at : 64 * at + 64, :])
            gram = jnp.concatenate(batched(side, side), axis=0)
            grams.append(jnp.concatenate(split(gram, 3), axis=0))
            pose = number - column_f * col_poses
            pose = jnp.where((region_of == 0) & (pose < col_poses), pose, -1.0)
            of_pose.append(jnp.where(iota((128, CH), 0).astype(f32) == pose, 1.0, 0.0).astype(bf16))
        total = dot(
            jnp.concatenate(grams, axis=1), jnp.concatenate(of_pose, axis=1), ((1,), (1,))
        )
        app[...] += total[0:64] + total[64:128] + total[128:192]

    loop(chunks, measure)
    gram = app[...]
    factor, _ = cholesky(slabs(gram + first))
    table = expansion()
    by_rows, by_columns = table[0:64], table[64:128]

    def copy_of(at):
        return pltpu.make_async_copy(
            squares.at[pl.ds(at * 128, 128), :],
            out_ref.at[pl.ds(start + at * 128, 128), pl.ds(at * 128, 128)],
            sem.at[at],
        )

    def expanded(block, by, count):
        full = jnp.concatenate([block, jnp.zeros((64, 128), f32)], axis=0).T[0:count, :]
        high, low = (part[:, 0:64] for part in split(full, 2))
        both = jnp.concatenate([high, low], axis=1)
        return dot(both, jnp.concatenate([by, by], axis=0))

    value = expanded(gram, by_rows, 128)
    pose, lane = iota((128, 128), 0), iota((128, 128), 1)
    weights = [jnp.broadcast_to(local[at : at + 1, :], (16, 128)) for at in range(groups)]
    weights = jnp.concatenate(weights + [jnp.zeros((16, 128), f32)] * (8 - groups), axis=0)
    keep, lane_in = lane // 8 == pose % 16, lane % 8
    pieces = []
    for k in range(8):
        piece = jnp.where(keep, value[:, 128 * k : 128 * k + 128], 0.0)
        piece = piece + jnp.where(keep & (lane_in == k), weights, 0.0)
        pieces.append(piece[0:PP, :])
        squares[pl.ds(PANEL + k, 128 - PP, stride=8), :] = piece[PP:, :]
    for at in range(K_PANELS, groups):
        copy_of(at).start()
    value = expanded(jnp.concatenate(factor, axis=0), by_columns, PP)
    for k in range(8):
        piece = jnp.where(keep[0:PP, :], value[:, 128 * k : 128 * k + 128], 0.0)
        squares[pl.ds(k, PP, stride=8), :] = jnp.where(column == 0, piece, pieces[k])
    for at in range(K_PANELS):
        copy_of(at).start()
    for at in range(groups):
        copy_of(at).wait()


def general(place, sizes, got_ref, prior_ref, out_ref,
                    jt, rows_s, cols_s, app, bt, blk, tiles, keys,
                    listing, info, list_sm, info_sm, extra_sm, sem_list, sem_info, sem_out):
    rows, cols, chunks = sizes
    row_poses, col_poses, groups = rows // 8, cols // 8, cols // 128
    region, column = place()
    region_f, column_f = region.astype(f32), column.astype(f32)
    start = column * cols - region * rows
    own = (start >= 0) & (start < rows)
    share = jnp.where(own, 1.0, 0.0)
    lane8, row8 = iota((8, 128), 1), iota((8, 128), 0)
    before = iota((CH, CH), 0) < iota((CH, CH), 1)
    table = expansion()

    labels0 = label_rows(got_ref, 0)
    sent = slot_rows(got_ref, 0, 9, 8)
    panel_prior = sent
    for at in range(1, 3):
        panel_prior = panel_prior + pltpu.roll(sent, 128 - 32 * at, 1)
    panel_prior = jnp.where(lane8 < 32, panel_prior, 0.0)
    lined = jnp.zeros((8, 128), f32)
    for at in range(4):
        moved = panel_prior if at == 0 else pltpu.roll(panel_prior, 32 * at, 1)
        lined = lined + jnp.where(row8 % 4 == at, moved, 0.0)
    halves = [
        jnp.sum(jnp.where(row8 < 4, lined, 0.0), axis=0, keepdims=True),
        jnp.sum(jnp.where(row8 >= 4, lined, 0.0), axis=0, keepdims=True),
    ]
    prior_row = jnp.concatenate(halves, axis=1)
    app[...] = on_diagonal(prior_row)

    def measure(a):
        jac_t = jac_columns(got_ref, a)
        jt[a] = jac_t
        d0, n0, d1, n1 = spread(labels0 if chunks == 1 else label_rows(got_ref, a))
        c0 = d0 * row_poses + n0 - column_f * col_poses
        c1 = d1 * row_poses + n1 - column_f * col_poses
        one, none = jnp.ones_like(d0), jnp.zeros_like(d0)
        row0, row1 = d0 == region_f, d1 == region_f
        col0, col1 = (c0 >= 0) & (c0 < col_poses), (c1 >= 0) & (c1 < col_poses)
        pan0, pan1 = (d0 == 0) & (n0 < PP), (d1 == 0) & (n1 < PP)
        has_row = jnp.where(row0 | row1, one, none)
        has_col = jnp.where(col0 | col1, one, none)
        touches = jnp.where(pan0 | pan1, one, none)
        row_pose = jnp.where(row0, n0, n1)
        col_pose = jnp.where(col0, c0, c1)
        pan_side = jnp.where(pan0, none, one)
        pan_pose = jnp.where(pan0, n0, n1)
        row_in_panel = jnp.where((row0 & pan0) | (row1 & pan1), one, none)
        col_in_panel = jnp.where((col0 & pan0) | (col1 & pan1), one, none)
        relevant = has_row * has_col * (1.0 - row_in_panel)
        group = jnp.floor(col_pose * (1.0 / 16.0))
        tile = row_pose * groups + group
        cell = row_pose * col_poses + col_pose
        is_row = touches * has_row * (1.0 - row_in_panel)
        is_col = touches * has_col * (1.0 - col_in_panel)
        lines = [
            jnp.where(relevant > 0, tile, -1.0),
            jnp.where(relevant > 0, cell, -1.0),
            jnp.where(touches > 0, pan_pose, -1.0),
            jnp.where(is_row > 0, pan_pose, -1.0),
            col_pose - group * 16.0,
            none, none, none,
        ]
        more = [
            jnp.where(relevant > 0, tile, -2.0),
            jnp.where(relevant > 0, cell, -2.0),
            jnp.where(is_col > 0, pan_pose, -2.0),
            relevant,
            row_pose,
            group,
            col_pose,
            is_row * is_col,
            jnp.where(row0, none, one),
            jnp.where(col0, none, one),
            pan_side,
            col_in_panel,
            none, none, none, none,
        ]
        lines = jnp.concatenate(lines, axis=0)
        rows_s[a] = jnp.concatenate([lines] + more, axis=0)
        columns = to_columns(lines)
        cols_s[a] = columns
        j0, j1 = slabs(jac_t[0:64, :]), slabs(jac_t[64:128, :])
        near = [jnp.where(pan_side == 0, x, y) for x, y in zip(j0, j1)]
        gram = jnp.concatenate(batched(near, near), axis=0)
        of_pose = jnp.where(
            columns[:, 2:3] == iota((CH, 128), 1).astype(f32), 1.0, 0.0
        ).astype(bf16)
        total = dot(jnp.concatenate(split(gram, 3), axis=0), of_pose)
        app[...] += total[0:64] + total[64:128] + total[128:192]

    loop(chunks, measure)

    def earlier_of(a, at, at_right):
        def from_chunk(b, count):
            other = jnp.broadcast_to(cols_s[b, :, at : at + 1], (CH, CH))
            same = jnp.where(other == rows_s[a, at_right : at_right + 1, :], 1.0, 0.0)
            if chunks == 1:
                same = jnp.where(before, same, 0.0)
            else:
                here, all_of_it = jnp.where(b == a, 1.0, 0.0), jnp.where(b < a, 1.0, 0.0)
                same = jnp.where(before, same, 0.0) * here + same * all_of_it
            return count + jnp.sum(same, axis=0, keepdims=True)

        nothing = jnp.zeros((1, CH), f32)
        return from_chunk(0, nothing) if chunks == 1 else lax.fori_loop(0, chunks, from_chunk, nothing)

    def lists(a):
        relevant = rows_s[a, 11:12, :]
        kept = jnp.where(earlier_of(a, 0, 8) == 0, relevant, 0.0)
        lone = jnp.where(earlier_of(a, 1, 9) == 0, relevant, 0.0)
        joins = lone * (1.0 - kept)
        rows_s[a, 20:21, :] = kept
        count = jnp.sum(kept, axis=1, keepdims=True)
        upper = jnp.where(before, 1.0, 0.0).astype(bf16)
        rank = dot(jnp.broadcast_to(kept, (16, CH)).astype(bf16), upper)[0:1, :]
        slot = iota((CH, CH), 0)
        slot = (slot % 64 * 4 + slot // 64).astype(f32)
        slot = jnp.where(slot < count, slot, 0.0)
        chosen = jnp.where((rank == slot) & (kept > 0), 1.0, 0.0).astype(bf16)
        position = iota((1, CH), 1).astype(f32)
        data = jnp.concatenate(
            [rows_s[a, 12:13, :], rows_s[a, 13:14, :], position, jnp.zeros((13, CH), f32)], axis=0
        ).astype(bf16)
        found = dot(data, chosen, ((1,), (1,)))[0:8, :]
        code = found[2:3, :] + found[0:1, :] * 256.0 + found[1:2, :] * 65536.0
        line = [code[:, 0:128], pltpu.roll(code[:, 0:128], 64, 1)]
        line += [code[:, 128:256], pltpu.roll(code[:, 128:256], 64, 1)]
        line += [jnp.broadcast_to(count, (1, 128)), jnp.zeros((3, 128), f32)]
        listing[a] = jnp.concatenate(line, axis=0).astype(i32)
        pltpu.make_async_copy(listing.at[a], list_sm.at[a], sem_list.at[a]).start()
        info[a] = jnp.concatenate(
            [rows_s[a, 12:13, :], rows_s[a, 14:15, :], joins, jnp.zeros((5, CH), f32)], axis=0
        ).astype(i32)
        pltpu.make_async_copy(info.at[a], info_sm.at[a], sem_info.at[a]).start()

    loop(chunks, lists)

    def key_table(a, b):
        left = jnp.broadcast_to(cols_s[a, :, 3:4], (CH, CH))
        valid = jnp.where(left == rows_s[b, 10:11, :], 1.0, 0.0)
        same = iota((CH, CH), 0) == iota((CH, CH), 1)
        joins = info[a, 2:3, :].astype(f32)
        if chunks > 1:
            flag = jnp.where(a == b, 1.0, 0.0)
            joins = joins * flag + valid * (1.0 - flag)
        valid = jnp.where(same, joins, valid)
        key = (iota((CH, CH), 0) * CH + iota((CH, CH), 1)).astype(f32)
        key = jnp.where(valid > 0, key, BIG)
        keys[...] = key
        return jnp.min(key)

    early = key_table(0, 0) if chunks == 1 else None

    _, inverse = cholesky(slabs(app[...]))
    inverse = jnp.concatenate(split(jnp.concatenate(inverse, axis=0), 3), axis=0)

    def blocks(a):
        row = [rows_s[a, at : at + 1, :] for at in range(24)]
        jac_t = jt[a]
        j0, j1 = slabs(jac_t[0:64, :]), slabs(jac_t[64:128, :])
        left = [jnp.where(row[16] == 0, x, y) for x, y in zip(j0, j1)]
        right = [jnp.where(row[17] == 0, x, y) for x, y in zip(j0, j1)]
        near = [jnp.where(row[18] == 0, x, y) for x, y in zip(j0, j1)]
        far = [jnp.where(row[18] == 0, y, x) for x, y in zip(j0, j1)]
        gram = batched(left, right)
        cross = batched(near, far)
        of_pose = jnp.where(iota((128, CH), 0).astype(f32) == row[2], 1.0, 0.0).astype(bf16)
        inv = dot(inverse, of_pose)
        inv = slabs(inv[0:64] + inv[64:128] + inv[128:192])
        solved = []
        for j in range(8):
            total = inv[0][j : j + 1, :] * cross[0]
            for i in range(1, j + 1):
                total = total + inv[i][j : j + 1, :] * cross[i]
            solved.append(total)
        bt[a] = jnp.concatenate(solved, axis=0)
        outer = batched(solved, solved)
        keep_normal = row[11] * (1.0 - row[19])
        keep_panel = row[11] * row[19]
        values = [(g - o * row[15]) * keep_normal for g, o in zip(gram, outer)]
        values += [x * keep_panel for x in solved]
        values = jnp.concatenate(values, axis=0)
        high, low = split(values, 2)
        blk[a] = jnp.concatenate([high, low], axis=0)

    loop(chunks, blocks)

    def merge(a):
        line = [rows_s[a, at : at + 1, :] for at in range(24)]

        def from_chunk(b, total):
            other = jnp.broadcast_to(cols_s[b, :, 1:2], (CH, CH))
            same = jnp.where(other == line[9], 1.0, 0.0).astype(bf16)
            found = dot(blk[b], same)
            return total + found[0:128] + found[128:256]

        total = jnp.zeros((128, CH), f32)
        total = from_chunk(0, total) if chunks == 1 else lax.fori_loop(0, chunks, from_chunk, total)
        sixteenth = jnp.floor(line[12] * (1.0 / 16.0))
        pieces = rows // 128
        local = jnp.concatenate(
            [prior_ref[...], jnp.zeros((16 - pieces, 128), f32)], axis=0
        ) if pieces < 16 else prior_ref[...]
        steps = local.shape[0]
        parts = jnp.concatenate(split(local, 3), axis=0)
        of_row = jnp.where(
            (iota((3 * steps, CH), 0) % steps).astype(f32) == sixteenth, 1.0, 0.0
        ).astype(bf16)
        priors = dot(parts, of_row, ((0,), (0,)))
        within = line[12] - sixteenth * 16.0
        on_row = jnp.zeros((8, CH), f32)
        for at in range(16):
            on_row = on_row + jnp.where(within == float(at), priors[8 * at : 8 * at + 8, :], 0.0)
        on_row = on_row * (share * line[11])
        sub = iota((8, CH), 0)
        normal = [
            total[8 * k : 8 * k + 8, :] + jnp.where(sub == k, on_row, 0.0) for k in range(8)
        ]
        total = jnp.concatenate(normal + [total[64:128, :]], axis=0)
        value = dot(jnp.concatenate(split(total.T, 2), axis=1), table)
        keep = (iota((CH, 128), 1) // 8).astype(f32) == cols_s[a, :, 4:5]
        for k in range(8):
            tiles[pl.ds(a * CH * 8 + k, CH, stride=8), :] = jnp.where(
                keep, value[:, 128 * k : 128 * k + 128], 0.0
            )

    loop(chunks, merge)

    def waiting(a):
        pltpu.make_async_copy(listing.at[a], list_sm.at[a], sem_list.at[a]).wait()
        pltpu.make_async_copy(info.at[a], info_sm.at[a], sem_info.at[a]).wait()

    loop(chunks, waiting)
    extra_sm[0] = 0

    def tile_rows(slot, count=1):
        return pl.ds(pl.multiple_of(slot * 8, 8), 8 * count)

    def pairs(index):
        a, b = (0, 0) if chunks == 1 else (index // chunks, index % chunks)

        def one(key_now):
            number = key_now.astype(i32)
            m1, m2 = number >> 8, number & (CH - 1)
            joining = (m1 == m2) if chunks == 1 else ((m1 == m2) & (a == b))
            r1, c2 = info_sm[a, 0, m1], info_sm[b, 1, m2]
            group, within = c2 >> 4, c2 & 15
            code = r1 * groups + group
            code_f = code.astype(f32)
            key_next = jnp.min(jnp.where(keys[...] > key_now, keys[...], BIG))

            def search(chunk, best):
                at_one = (rows_s[chunk, 8:9, :] == code_f) & (rows_s[chunk, 20:21, :] > 0)
                slots = (iota((1, CH), 1) + chunk * CH).astype(f32)
                return jnp.minimum(best, jnp.min(jnp.where(at_one, slots, BIG)))

            slot = search(0, BIG) if chunks == 1 else lax.fori_loop(0, chunks, search, BIG)
            position = iota((8, CH), 1)
            total = jnp.zeros((8, 128), f32)
            for j in range(8):
                x = bt[a, 8 * j : 8 * j + 8, :]
                y = bt[b, 8 * j : 8 * j + 8, :]
                x = jnp.sum(jnp.where(position == m1, x, 0.0), axis=1, keepdims=True)
                y = jnp.sum(jnp.where(position == m2, y, 0.0), axis=1, keepdims=True)
                y = jnp.where(lane8 % 8 == row8, y, 0.0)
                y = jnp.sum(y, axis=0, keepdims=True)
                total = total + x * y
            total = jnp.where(lane8 // 8 == within, -total, 0.0)
            total = jnp.where(joining, tiles[tile_rows(a * CH + m1), :], total)
            added = extra_sm[0]
            slot = jnp.where(slot < BIG, slot, -1.0).astype(i32)

            def at_extra(at, slot):
                return jnp.where(extra_sm[1 + at] == code, chunks * CH + at, slot)

            slot = lax.fori_loop(0, added, at_extra, slot)
            fresh = slot < 0
            slot = jnp.where(fresh, chunks * CH + added, slot)
            where = tile_rows(slot)
            tiles[where, :] = jnp.where(fresh, 0.0, tiles[where, :]) + total

            @pl.when(fresh)
            def _():
                extra_sm[1 + added] = code
                extra_sm[0] = added + 1

            return key_next

        smallest = early if chunks == 1 else key_table(a, b)
        lax.while_loop(lambda key_now: key_now < BIG, one, smallest)

    loop(chunks * chunks, pairs)

    def tile_copy(slot, r, group, count=1):
        return pltpu.make_async_copy(
            tiles.at[tile_rows(slot, count), :],
            out_ref.at[tile_rows(r, count), pl.ds(pl.multiple_of(group * 128, 128), 128)],
            sem_out,
        )

    def send(a):
        def four(at, carry):
            for more in range(4):
                entry = list_sm[a, more, at]
                slot, r = a * CH + (entry & 255), (entry >> 8) & 255
                tile_copy(slot, r, entry >> 16).start()
            return carry
        lax.fori_loop(0, (list_sm[a, 4, 0] + 3) // 4, four, 0)

    loop(chunks, send)

    def send_extra(at, carry):
        code = extra_sm[1 + at]
        tile_copy(chunks * CH + at, code // groups, code % groups).start()
        return carry

    lax.fori_loop(0, extra_sm[0], send_extra, 0)

    def drain_four(at, carry):
        tile_copy(0, 0, 0, 4).wait()
        return carry

    def drain_one(at, carry):
        tile_copy(0, 0, 0).wait()
        return carry

    def drain(a):
        lax.fori_loop(0, (list_sm[a, 4, 0] + 3) // 4, drain_four, 0)

    loop(chunks, drain)
    lax.fori_loop(0, extra_sm[0], drain_one, 0)


def assemble_kernel(place, sizes, got_ref, prior_ref, filled_ref, out_ref,
                    jt, rows_s, cols_s, app, bt, blk, tiles, keys,
                    listing, info, list_sm, info_sm, extra_sm, sem_list, sem_info, sem_out,
                    squares, sem_sq):
    del filled_ref
    rows, cols, _ = sizes
    region, column = place()
    first = (region == 0) & (column * cols < rows)

    @pl.when(first)
    def _():
        first_region(place, sizes, got_ref, prior_ref, out_ref, app, squares, sem_sq)

    @pl.when(jnp.logical_not(first))
    def _():
        general(place, sizes, got_ref, prior_ref, out_ref, jt, rows_s, cols_s, app, bt, blk,
                tiles, keys, listing, info, list_sm, info_sm, extra_sm, sem_list, sem_info, sem_out)


def assemble(place, rows, cols, got, prior2, filled):
    count = got.shape[0] // SLOT * 8
    chunks = count // CH
    capacity = rows // 8 * (cols // 128)
    any_space = pl.BlockSpec(memory_space=pl.ANY)
    vmem = pl.BlockSpec(memory_space=pltpu.VMEM)
    return pl.pallas_call(
        functools.partial(assemble_kernel, place, (rows, cols, chunks)),
        out_shape=jax.ShapeDtypeStruct((rows, cols), f32),
        in_specs=[vmem, vmem, any_space],
        out_specs=any_space,
        scratch_shapes=[
            pltpu.VMEM((chunks, 128, CH), f32),
            pltpu.VMEM((chunks, 24, CH), f32),
            pltpu.VMEM((chunks, CH, 128), f32),
            pltpu.VMEM((64, 128), f32),
            pltpu.VMEM((chunks, 64, CH), f32),
            pltpu.VMEM((chunks, 256, CH), bf16),
            pltpu.VMEM(((count + capacity) * 8, 128), f32),
            pltpu.VMEM((CH, CH), f32),
            pltpu.VMEM((chunks, 8, 128), i32),
            pltpu.VMEM((chunks, 8, CH), i32),
            pltpu.SMEM((chunks, 8, 128), i32),
            pltpu.SMEM((chunks, 8, CH), i32),
            pltpu.SMEM((1 + capacity,), i32),
            pltpu.SemaphoreType.DMA((chunks,)),
            pltpu.SemaphoreType.DMA((chunks,)),
            pltpu.SemaphoreType.DMA,
            pltpu.VMEM((1024, 128), f32),
            pltpu.SemaphoreType.DMA((cols // 128,)),
        ],
        input_output_aliases={2: 0},
        compiler_params=pltpu.CompilerParams(vmem_limit_bytes=48 << 20),
        name="assemble",
    )(got, prior2, filled)


def place():
    return lax.axis_index("region"), lax.axis_index("col")


def body(jac, dest, near_pose, prior):
    regions, columns = lax.axis_size("region"), lax.axis_size("col")
    devices = regions * columns
    rows = prior.shape[0]
    cols = rows * regions // columns
    assert jac.shape[0] == 8 and devices * 8 % CH == 0
    assert rows % cols == 0 and rows // 8 <= 256 and regions <= 256
    assert cols // 8 <= 128 and rows // 8 * (cols // 128) <= 2048
    assert rows >= PANEL and cols >= PANEL and cols % 128 == 0 and columns % 8 == 0
    prior2 = prior.reshape(rows // 128, 128)
    packed = pack(place, jac, dest, near_pose, prior2, devices).reshape(devices, SLOT // 2, 2, 128)
    got = lax.all_to_all(packed, ("region", "col"), split_axis=0, concat_axis=0, tiled=True)
    got = got.reshape(devices * SLOT, 128)
    filled = fill(place, rows, cols, prior2)
    return assemble(place, rows, cols, got, prior2, filled)


def solution(mesh):
    return jax.shard_map(
        body,
        mesh=mesh,
        in_specs=(
            P(("region", "col"), None),
            P(("region", "col"), None),
            P(("region", "col"), None),
            P("region"),
        ),
        out_specs=P("region", "col"),
        check_vma=False,
    )
```

```python
import functools

import jax
import jax.numpy as jnp
from jax import lax
from jax.experimental import pallas as pl
from jax.experimental.pallas import tpu as pltpu
from jax.sharding import PartitionSpec as P

NB = 128
K_PANELS = 2
PANEL = NB * K_PANELS
PP = PANEL // 8
CH = 256
BIG = float(1 << 24)
f32, bf16, i32 = jnp.float32, jnp.bfloat16, jnp.int32


def iota(shape, dim):
    return lax.broadcasted_iota(i32, shape, dim)


def split(x, parts):
    out = []
    for _ in range(parts):
        top = x.astype(bf16)
        out.append(top)
        x = x - top.astype(f32)
    return out


def dot(a, b, dims=((1,), (0,))):
    return lax.dot_general(a, b, (dims, ((), ())), preferred_element_type=f32)


SLOT = 10
LABEL_AT = (0, 56, 64, 120)


def pack_kernel(place, jac_ref, dest_ref, near_ref, prior_ref, out_ref):
    _, column = place()
    shape = (8, 128)
    lane, row = iota(shape, 1), iota(shape, 0)
    fill_up = jnp.zeros((2, 120), f32)
    dest = jnp.concatenate([dest_ref[...].astype(f32), fill_up], axis=1)
    near = jnp.concatenate([near_ref[...].astype(f32), fill_up], axis=1)
    labels = jnp.zeros(shape, f32)
    for at, line in zip(LABEL_AT, (dest[0:1, :], near[0:1, :], dest[1:2, :], near[1:2, :])):
        line = jnp.broadcast_to(line, shape)
        labels = labels + (pltpu.roll(line, at, 1) if at else line)
    column = column % 8
    prior = jnp.broadcast_to(prior_ref[pl.ds(column // 4, 1), :], shape)
    weights = jnp.zeros(shape, f32)
    for at, part in enumerate(split(prior, 3)):
        moved = pltpu.roll(part.astype(f32), (4 + at - column % 4) % 4 * 32, 1)
        weights = jnp.where(lane // 32 == at, moved, weights)
    jac = jac_ref[...].astype(f32)
    turned = [jac if not at else pltpu.roll(jac, 2 * at, 0) for at in range(4)]
    pieces = []
    for at in range(SLOT):
        piece = jnp.zeros(shape, f32)
        for slot in range(8):
            first = SLOT * slot - 8 * at
            if -SLOT < first < 8:
                piece = jnp.where((row >= first) & (row < first + 8), turned[slot % 4], piece)
                piece = jnp.where(row == first + 8, labels, piece)
                piece = jnp.where(row == first + 9, weights, piece)
        pieces.append(piece)
    eight = jnp.concatenate(pieces, axis=0).astype(bf16)
    for at in range(out_ref.shape[0] // (8 * SLOT)):
        out_ref[8 * SLOT * at : 8 * SLOT * (at + 1), :] = eight


def pack(place, jac, dest, near_pose, prior2, devices):
    return pl.pallas_call(
        functools.partial(pack_kernel, place),
        out_shape=jax.ShapeDtypeStruct((devices * SLOT, 128), bf16),
        in_specs=[pl.BlockSpec(memory_space=pltpu.VMEM)] * 4,
        out_specs=pl.BlockSpec(memory_space=pltpu.VMEM),
        name="pack",
    )(jac, dest.T, near_pose.T, prior2)


def fill_kernel(place, sizes, prior_ref, out_ref, zeros, squares, sem, sem2):
    rows, cols = sizes
    region, column = place()
    pieces = rows // zeros.shape[0]
    zeros[...] = jnp.zeros_like(zeros)
    step = zeros.shape[0]
    copies = [
        pltpu.make_async_copy(zeros, out_ref.at[pl.ds(at * step, step), :], sem.at[at])
        for at in range(pieces)
    ]
    for copy in copies:
        copy.start()
    start = column * cols - region * rows
    own = (start >= 0) & (start < rows)

    @pl.when(own)
    def _():
        diagonal = iota((128, 128), 0) == iota((128, 128), 1)
        first = start // 128
        for at in range(cols // 128):
            squares[at] = jnp.where(diagonal, prior_ref[pl.ds(first + at, 1), :], 0.0)

    for copy in copies:
        copy.wait()

    @pl.when(own)
    def _():
        base = pl.multiple_of(start, 128)
        patches = [
            pltpu.make_async_copy(
                squares.at[at],
                out_ref.at[pl.ds(base + at * 128, 128), pl.ds(at * 128, 128)],
                sem2.at[at],
            )
            for at in range(cols // 128)
        ]
        for patch in patches:
            patch.start()
        for patch in patches:
            patch.wait()


def fill(place, rows, cols, prior2):
    step = min(256, rows)
    return pl.pallas_call(
        functools.partial(fill_kernel, place, (rows, cols)),
        out_shape=jax.ShapeDtypeStruct((rows, cols), f32),
        out_specs=pl.BlockSpec(memory_space=pl.ANY),
        scratch_shapes=[
            pltpu.VMEM((step, cols), f32),
            pltpu.VMEM((cols // 128, 128, 128), f32),
            pltpu.SemaphoreType.DMA((rows // step,)),
            pltpu.SemaphoreType.DMA((cols // 128,)),
        ],
        cost_estimate=pl.CostEstimate(flops=0, bytes_accessed=rows * cols * 4, transcendentals=0),
        name="fill",
    )(prior2)


def batched(left, right):
    out = []
    for k in range(8):
        total = left[0][k : k + 1, :] * right[0]
        for e in range(1, 8):
            total = total + left[e][k : k + 1, :] * right[e]
        out.append(total)
    return out


def slabs(block):
    return [block[8 * e : 8 * e + 8, :] for e in range(8)]


def to_columns(rows):
    full = jnp.concatenate([rows, jnp.zeros((120, CH), f32)], axis=0)
    return full.T


def cholesky(a):
    row = iota((8, 128), 0)
    columns, scales = [], []
    a = list(a)
    for j in range(8):
        pivot = a[j][j : j + 1, :]
        scale = lax.rsqrt(pivot)
        scale = scale * (1.5 - 0.5 * pivot * scale * scale)
        column = jnp.where(row >= j, a[j] * scale, 0.0)
        for k in range(j + 1, 8):
            a[k] = a[k] - column * column[k : k + 1, :]
        columns.append(column)
        scales.append(scale)
    inverse = []
    for i in range(8):
        x = jnp.where(row == i, 1.0, 0.0)
        for j in range(i, 8):
            value = x[j : j + 1, :] * scales[j]
            x = jnp.where(row == j, value, jnp.where(row > j, x - columns[j] * value, x))
        inverse.append(x)
    return columns, inverse


def loop(count, body):
    if count == 1:
        body(0)
    else:
        lax.fori_loop(0, count, lambda at, carry: (body(at), carry)[1], 0)


def expansion():
    row, lane = iota((8, 128), 0), iota((8, 128), 1)
    none = jnp.zeros((8, 128), f32)
    straight = jnp.where(lane % 8 == row, 1.0, 0.0)
    by_rows = [
        jnp.concatenate([straight if at == k else none for at in range(8)], axis=1)
        for k in range(8)
    ]
    by_columns = [
        jnp.concatenate(
            [jnp.where((row == at) & (lane % 8 == j), 1.0, 0.0) for at in range(8)], axis=1
        )
        for j in range(8)
    ]
    return jnp.concatenate((by_rows + by_columns) * 2, axis=0).astype(bf16)


def slot_rows(got_ref, a, at, per):
    block = got_ref[pl.ds(a * (CH // 8) * SLOT, per * SLOT), :].astype(f32)
    return jnp.concatenate([block[SLOT * d + at : SLOT * d + at + 1, :] for d in range(per)], axis=0)


def label_rows(got_ref, a):
    return slot_rows(got_ref, a, 8, CH // 8)


def jac_columns(got_ref, a):
    per = CH // 8
    block = got_ref[pl.ds(a * per * SLOT, per * SLOT), :].astype(f32)
    return jnp.concatenate([block[SLOT * d : SLOT * d + 8, :] for d in range(per)], axis=0).T


def spread(labels):
    lane8, row8 = iota((8, 128), 1), iota((8, 128), 0)
    out = []
    for at in LABEL_AT:
        halves = []
        for half in range(2):
            total = jnp.zeros((8, 128), f32)
            for part in range(2):
                from_row = 16 * half + 8 * part
                piece = labels[from_row : from_row + 8, :]
                piece = pltpu.roll(piece, (64 * part - at) % 128, 1, stride=8, stride_axis=0)
                total = total + jnp.where(lane8 // 8 == row8 + 8 * part, piece, 0.0)
            halves.append(jnp.sum(total, axis=0, keepdims=True))
        out.append(jnp.concatenate(halves, axis=1))
    return out


def on_diagonal(prior_row):
    kl, unknown = iota((64, PANEL), 0), iota((64, PANEL), 1)
    diagonal = jnp.where((kl // 8 == kl % 8) & (unknown % 8 == kl % 8), prior_row, 0.0)
    own_pose = jnp.where(iota((PANEL, 128), 0) // 8 == iota((PANEL, 128), 1), 1.0, 0.0).astype(bf16)
    first = dot(jnp.concatenate(split(diagonal, 3), axis=0), own_pose)
    kl = iota((64, 128), 0)
    spare = (kl // 8 == kl % 8) & (iota((64, 128), 1) >= PP)
    return first[0:64] + first[64:128] + first[128:192] + jnp.where(spare, 1.0, 0.0)


def first_region(place, sizes, got_ref, prior_ref, out_ref, app, squares, sem):
    rows, cols, chunks = sizes
    col_poses, groups = cols // 8, cols // 128
    _, column = place()
    column_f = column.astype(f32)
    start = pl.multiple_of(column * cols, 128)
    local = prior_ref[pl.ds(column * groups, groups), :]
    prior_row = jnp.concatenate([prior_ref[0:1, :], prior_ref[1:2, :]], axis=1)
    first = on_diagonal(prior_row)
    app[...] = jnp.zeros_like(app)

    def measure(a):
        jac_t = jac_columns(got_ref, a)
        d0, n0, d1, n1 = spread(label_rows(got_ref, a))
        grams, of_pose = [], []
        for at, (region_of, number) in enumerate(((d0, n0), (d1, n1))):
            side = slabs(jac_t[64 * at : 64 * at + 64, :])
            gram = jnp.concatenate(batched(side, side), axis=0)
            grams.append(jnp.concatenate(split(gram, 2), axis=0))
            pose = number - column_f * col_poses
            pose = jnp.where((region_of == 0) & (pose < col_poses), pose, -1.0)
            of_pose.append(jnp.where(iota((128, CH), 0).astype(f32) == pose, 1.0, 0.0).astype(bf16))
        total = dot(
            jnp.concatenate(grams, axis=1), jnp.concatenate(of_pose, axis=1), ((1,), (1,))
        )
        app[...] += total[0:64] + total[64:128]

    loop(chunks, measure)
    gram = app[...]
    factor, _ = cholesky(slabs(gram + first))
    table = expansion()
    by_rows, by_columns = table[0:64], table[64:128]

    def copy_of(at):
        return pltpu.make_async_copy(
            squares.at[pl.ds(at * 128, 128), :],
            out_ref.at[pl.ds(start + at * 128, 128), pl.ds(at * 128, 128)],
            sem.at[at],
        )

    def expanded(block, by, count):
        full = jnp.concatenate([block, jnp.zeros((64, 128), f32)], axis=0).T[0:count, :]
        high, low = (part[:, 0:64] for part in split(full, 2))
        both = jnp.concatenate([high, low], axis=1)
        return dot(both, jnp.concatenate([by, by], axis=0))

    value = expanded(gram, by_rows, 128)
    pose, lane = iota((128, 128), 0), iota((128, 128), 1)
    weights = [jnp.broadcast_to(local[at : at + 1, :], (16, 128)) for at in range(groups)]
    weights = jnp.concatenate(weights + [jnp.zeros((16, 128), f32)] * (8 - groups), axis=0)
    keep, lane_in = lane // 8 == pose % 16, lane % 8
    pieces = []
    for k in range(8):
        piece = jnp.where(keep, value[:, 128 * k : 128 * k + 128], 0.0)
        piece = piece + jnp.where(keep & (lane_in == k), weights, 0.0)
        pieces.append(piece[0:PP, :])
        squares[pl.ds(PANEL + k, 128 - PP, stride=8), :] = piece[PP:, :]
    for at in range(K_PANELS, groups):
        copy_of(at).start()
    value = expanded(jnp.concatenate(factor, axis=0), by_columns, PP)
    for k in range(8):
        piece = jnp.where(keep[0:PP, :], value[:, 128 * k : 128 * k + 128], 0.0)
        squares[pl.ds(k, PP, stride=8), :] = jnp.where(column == 0, piece, pieces[k])
    for at in range(K_PANELS):
        copy_of(at).start()
    for at in range(groups):
        copy_of(at).wait()


def general(place, sizes, got_ref, prior_ref, out_ref,
                    jt, rows_s, cols_s, app, bt, blk, tiles, keys,
                    listing, info, list_sm, info_sm, extra_sm, sem_list, sem_info, sem_out):
    rows, cols, chunks = sizes
    row_poses, col_poses, groups = rows // 8, cols // 8, cols // 128
    region, column = place()
    region_f, column_f = region.astype(f32), column.astype(f32)
    start = column * cols - region * rows
    own = (start >= 0) & (start < rows)
    share = jnp.where(own, 1.0, 0.0)
    lane8, row8 = iota((8, 128), 1), iota((8, 128), 0)
    before = iota((CH, CH), 0) < iota((CH, CH), 1)
    table = expansion()

    labels0 = label_rows(got_ref, 0)
    sent = slot_rows(got_ref, 0, 9, 8)
    panel_prior = sent
    for at in range(1, 3):
        panel_prior = panel_prior + pltpu.roll(sent, 128 - 32 * at, 1)
    panel_prior = jnp.where(lane8 < 32, panel_prior, 0.0)
    lined = jnp.zeros((8, 128), f32)
    for at in range(4):
        moved = panel_prior if at == 0 else pltpu.roll(panel_prior, 32 * at, 1)
        lined = lined + jnp.where(row8 % 4 == at, moved, 0.0)
    halves = [
        jnp.sum(jnp.where(row8 < 4, lined, 0.0), axis=0, keepdims=True),
        jnp.sum(jnp.where(row8 >= 4, lined, 0.0), axis=0, keepdims=True),
    ]
    prior_row = jnp.concatenate(halves, axis=1)
    app[...] = on_diagonal(prior_row)

    def measure(a):
        jac_t = jac_columns(got_ref, a)
        jt[a] = jac_t
        d0, n0, d1, n1 = spread(labels0 if chunks == 1 else label_rows(got_ref, a))
        c0 = d0 * row_poses + n0 - column_f * col_poses
        c1 = d1 * row_poses + n1 - column_f * col_poses
        one, none = jnp.ones_like(d0), jnp.zeros_like(d0)
        row0, row1 = d0 == region_f, d1 == region_f
        col0, col1 = (c0 >= 0) & (c0 < col_poses), (c1 >= 0) & (c1 < col_poses)
        pan0, pan1 = (d0 == 0) & (n0 < PP), (d1 == 0) & (n1 < PP)
        has_row = jnp.where(row0 | row1, one, none)
        has_col = jnp.where(col0 | col1, one, none)
        touches = jnp.where(pan0 | pan1, one, none)
        row_pose = jnp.where(row0, n0, n1)
        col_pose = jnp.where(col0, c0, c1)
        pan_side = jnp.where(pan0, none, one)
        pan_pose = jnp.where(pan0, n0, n1)
        row_in_panel = jnp.where((row0 & pan0) | (row1 & pan1), one, none)
        col_in_panel = jnp.where((col0 & pan0) | (col1 & pan1), one, none)
        relevant = has_row * has_col * (1.0 - row_in_panel)
        group = jnp.floor(col_pose * (1.0 / 16.0))
        tile = row_pose * groups + group
        cell = row_pose * col_poses + col_pose
        is_row = touches * has_row * (1.0 - row_in_panel)
        is_col = touches * has_col * (1.0 - col_in_panel)
        lines = [
            jnp.where(relevant > 0, tile, -1.0),
            jnp.where(relevant > 0, cell, -1.0),
            jnp.where(touches > 0, pan_pose, -1.0),
            jnp.where(is_row > 0, pan_pose, -1.0),
            col_pose - group * 16.0,
            none, none, none,
        ]
        more = [
            jnp.where(relevant > 0, tile, -2.0),
            jnp.where(relevant > 0, cell, -2.0),
            jnp.where(is_col > 0, pan_pose, -2.0),
            relevant,
            row_pose,
            group,
            col_pose,
            is_row * is_col,
            jnp.where(row0, none, one),
            jnp.where(col0, none, one),
            pan_side,
            col_in_panel,
            none, none, none, none,
        ]
        lines = jnp.concatenate(lines, axis=0)
        rows_s[a] = jnp.concatenate([lines] + more, axis=0)
        columns = to_columns(lines)
        cols_s[a] = columns
        j0, j1 = slabs(jac_t[0:64, :]), slabs(jac_t[64:128, :])
        near = [jnp.where(pan_side == 0, x, y) for x, y in zip(j0, j1)]
        gram = jnp.concatenate(batched(near, near), axis=0)
        of_pose = jnp.where(
            columns[:, 2:3] == iota((CH, 128), 1).astype(f32), 1.0, 0.0
        ).astype(bf16)
        total = dot(jnp.concatenate(split(gram, 3), axis=0), of_pose)
        app[...] += total[0:64] + total[64:128] + total[128:192]

    loop(chunks, measure)

    def earlier_of(a, at, at_right):
        def from_chunk(b, count):
            other = jnp.broadcast_to(cols_s[b, :, at : at + 1], (CH, CH))
            same = jnp.where(other == rows_s[a, at_right : at_right + 1, :], 1.0, 0.0)
            if chunks == 1:
                same = jnp.where(before, same, 0.0)
            else:
                here, all_of_it = jnp.where(b == a, 1.0, 0.0), jnp.where(b < a, 1.0, 0.0)
                same = jnp.where(before, same, 0.0) * here + same * all_of_it
            return count + jnp.sum(same, axis=0, keepdims=True)

        nothing = jnp.zeros((1, CH), f32)
        return from_chunk(0, nothing) if chunks == 1 else lax.fori_loop(0, chunks, from_chunk, nothing)

    def lists(a):
        relevant = rows_s[a, 11:12, :]
        kept = jnp.where(earlier_of(a, 0, 8) == 0, relevant, 0.0)
        lone = jnp.where(earlier_of(a, 1, 9) == 0, relevant, 0.0)
        joins = lone * (1.0 - kept)
        rows_s[a, 20:21, :] = kept
        count = jnp.sum(kept, axis=1, keepdims=True)
        upper = jnp.where(before, 1.0, 0.0).astype(bf16)
        rank = dot(jnp.broadcast_to(kept, (16, CH)).astype(bf16), upper)[0:1, :]
        slot = iota((CH, CH), 0)
        slot = (slot % 64 * 4 + slot // 64).astype(f32)
        slot = jnp.where(slot < count, slot, 0.0)
        chosen = jnp.where((rank == slot) & (kept > 0), 1.0, 0.0).astype(bf16)
        position = iota((1, CH), 1).astype(f32)
        data = jnp.concatenate(
            [rows_s[a, 12:13, :], rows_s[a, 13:14, :], position, jnp.zeros((13, CH), f32)], axis=0
        ).astype(bf16)
        found = dot(data, chosen, ((1,), (1,)))[0:8, :]
        code = found[2:3, :] + found[0:1, :] * 256.0 + found[1:2, :] * 65536.0
        line = [code[:, 0:128], pltpu.roll(code[:, 0:128], 64, 1)]
        line += [code[:, 128:256], pltpu.roll(code[:, 128:256], 64, 1)]
        line += [jnp.broadcast_to(count, (1, 128)), jnp.zeros((3, 128), f32)]
        listing[a] = jnp.concatenate(line, axis=0).astype(i32)
        pltpu.make_async_copy(listing.at[a], list_sm.at[a], sem_list.at[a]).start()
        info[a] = jnp.concatenate(
            [rows_s[a, 12:13, :], rows_s[a, 14:15, :], joins, jnp.zeros((5, CH), f32)], axis=0
        ).astype(i32)
        pltpu.make_async_copy(info.at[a], info_sm.at[a], sem_info.at[a]).start()

    loop(chunks, lists)

    def key_table(a, b):
        left = jnp.broadcast_to(cols_s[a, :, 3:4], (CH, CH))
        valid = jnp.where(left == rows_s[b, 10:11, :], 1.0, 0.0)
        same = iota((CH, CH), 0) == iota((CH, CH), 1)
        joins = info[a, 2:3, :].astype(f32)
        if chunks > 1:
            flag = jnp.where(a == b, 1.0, 0.0)
            joins = joins * flag + valid * (1.0 - flag)
        valid = jnp.where(same, joins, valid)
        key = (iota((CH, CH), 0) * CH + iota((CH, CH), 1)).astype(f32)
        key = jnp.where(valid > 0, key, BIG)
        keys[...] = key
        return jnp.min(key)

    early = key_table(0, 0) if chunks == 1 else None

    _, inverse = cholesky(slabs(app[...]))
    inverse = jnp.concatenate(split(jnp.concatenate(inverse, axis=0), 3), axis=0)

    def blocks(a):
        row = [rows_s[a, at : at + 1, :] for at in range(24)]
        jac_t = jt[a]
        j0, j1 = slabs(jac_t[0:64, :]), slabs(jac_t[64:128, :])
        left = [jnp.where(row[16] == 0, x, y) for x, y in zip(j0, j1)]
        right = [jnp.where(row[17] == 0, x, y) for x, y in zip(j0, j1)]
        near = [jnp.where(row[18] == 0, x, y) for x, y in zip(j0, j1)]
        far = [jnp.where(row[18] == 0, y, x) for x, y in zip(j0, j1)]
        gram = batched(left, right)
        cross = batched(near, far)
        of_pose = jnp.where(iota((128, CH), 0).astype(f32) == row[2], 1.0, 0.0).astype(bf16)
        inv = dot(inverse, of_pose)
        inv = slabs(inv[0:64] + inv[64:128] + inv[128:192])
        solved = []
        for j in range(8):
            total = inv[0][j : j + 1, :] * cross[0]
            for i in range(1, j + 1):
                total = total + inv[i][j : j + 1, :] * cross[i]
            solved.append(total)
        bt[a] = jnp.concatenate(solved, axis=0)
        outer = batched(solved, solved)
        keep_normal = row[11] * (1.0 - row[19])
        keep_panel = row[11] * row[19]
        values = [(g - o * row[15]) * keep_normal for g, o in zip(gram, outer)]
        values += [x * keep_panel for x in solved]
        values = jnp.concatenate(values, axis=0)
        high, low = split(values, 2)
        blk[a] = jnp.concatenate([high, low], axis=0)

    loop(chunks, blocks)

    def merge(a):
        line = [rows_s[a, at : at + 1, :] for at in range(24)]

        def from_chunk(b, total):
            other = jnp.broadcast_to(cols_s[b, :, 1:2], (CH, CH))
            same = jnp.where(other == line[9], 1.0, 0.0).astype(bf16)
            found = dot(blk[b], same)
            return total + found[0:128] + found[128:256]

        total = jnp.zeros((128, CH), f32)
        total = from_chunk(0, total) if chunks == 1 else lax.fori_loop(0, chunks, from_chunk, total)
        sixteenth = jnp.floor(line[12] * (1.0 / 16.0))
        pieces = rows // 128
        local = jnp.concatenate(
            [prior_ref[...], jnp.zeros((16 - pieces, 128), f32)], axis=0
        ) if pieces < 16 else prior_ref[...]
        steps = local.shape[0]
        parts = jnp.concatenate(split(local, 3), axis=0)
        of_row = jnp.where(
            (iota((3 * steps, CH), 0) % steps).astype(f32) == sixteenth, 1.0, 0.0
        ).astype(bf16)
        priors = dot(parts, of_row, ((0,), (0,)))
        within = line[12] - sixteenth * 16.0
        on_row = jnp.zeros((8, CH), f32)
        for at in range(16):
            on_row = on_row + jnp.where(within == float(at), priors[8 * at : 8 * at + 8, :], 0.0)
        on_row = on_row * (share * line[11])
        sub = iota((8, CH), 0)
        normal = [
            total[8 * k : 8 * k + 8, :] + jnp.where(sub == k, on_row, 0.0) for k in range(8)
        ]
        total = jnp.concatenate(normal + [total[64:128, :]], axis=0)
        value = dot(jnp.concatenate(split(total.T, 2), axis=1), table)
        keep = (iota((CH, 128), 1) // 8).astype(f32) == cols_s[a, :, 4:5]
        for k in range(8):
            tiles[pl.ds(a * CH * 8 + k, CH, stride=8), :] = jnp.where(
                keep, value[:, 128 * k : 128 * k + 128], 0.0
            )

    loop(chunks, merge)

    def waiting(a):
        pltpu.make_async_copy(listing.at[a], list_sm.at[a], sem_list.at[a]).wait()
        pltpu.make_async_copy(info.at[a], info_sm.at[a], sem_info.at[a]).wait()

    loop(chunks, waiting)
    extra_sm[0] = 0

    def tile_rows(slot, count=1):
        return pl.ds(pl.multiple_of(slot * 8, 8), 8 * count)

    def pairs(index):
        a, b = (0, 0) if chunks == 1 else (index // chunks, index % chunks)

        def one(key_now):
            number = key_now.astype(i32)
            m1, m2 = number >> 8, number & (CH - 1)
            joining = (m1 == m2) if chunks == 1 else ((m1 == m2) & (a == b))
            r1, c2 = info_sm[a, 0, m1], info_sm[b, 1, m2]
            group, within = c2 >> 4, c2 & 15
            code = r1 * groups + group
            code_f = code.astype(f32)
            key_next = jnp.min(jnp.where(keys[...] > key_now, keys[...], BIG))

            def search(chunk, best):
                at_one = (rows_s[chunk, 8:9, :] == code_f) & (rows_s[chunk, 20:21, :] > 0)
                slots = (iota((1, CH), 1) + chunk * CH).astype(f32)
                return jnp.minimum(best, jnp.min(jnp.where(at_one, slots, BIG)))

            slot = search(0, BIG) if chunks == 1 else lax.fori_loop(0, chunks, search, BIG)
            position = iota((8, CH), 1)
            total = jnp.zeros((8, 128), f32)
            for j in range(8):
                x = bt[a, 8 * j : 8 * j + 8, :]
                y = bt[b, 8 * j : 8 * j + 8, :]
                x = jnp.sum(jnp.where(position == m1, x, 0.0), axis=1, keepdims=True)
                y = jnp.sum(jnp.where(position == m2, y, 0.0), axis=1, keepdims=True)
                y = jnp.where(lane8 % 8 == row8, y, 0.0)
                y = jnp.sum(y, axis=0, keepdims=True)
                total = total + x * y
            total = jnp.where(lane8 // 8 == within, -total, 0.0)
            total = jnp.where(joining, tiles[tile_rows(a * CH + m1), :], total)
            added = extra_sm[0]
            slot = jnp.where(slot < BIG, slot, -1.0).astype(i32)

            def at_extra(at, slot):
                return jnp.where(extra_sm[1 + at] == code, chunks * CH + at, slot)

            slot = lax.fori_loop(0, added, at_extra, slot)
            fresh = slot < 0
            slot = jnp.where(fresh, chunks * CH + added, slot)
            where = tile_rows(slot)
            tiles[where, :] = jnp.where(fresh, 0.0, tiles[where, :]) + total

            @pl.when(fresh)
            def _():
                extra_sm[1 + added] = code
                extra_sm[0] = added + 1

            return key_next

        smallest = early if chunks == 1 else key_table(a, b)
        lax.while_loop(lambda key_now: key_now < BIG, one, smallest)

    loop(chunks * chunks, pairs)

    def tile_copy(slot, r, group, count=1):
        return pltpu.make_async_copy(
            tiles.at[tile_rows(slot, count), :],
            out_ref.at[tile_rows(r, count), pl.ds(pl.multiple_of(group * 128, 128), 128)],
            sem_out,
        )

    def send(a):
        def four(at, carry):
            for more in range(4):
                entry = list_sm[a, more, at]
                slot, r = a * CH + (entry & 255), (entry >> 8) & 255
                tile_copy(slot, r, entry >> 16).start()
            return carry
        lax.fori_loop(0, (list_sm[a, 4, 0] + 3) // 4, four, 0)

    loop(chunks, send)

    def send_extra(at, carry):
        code = extra_sm[1 + at]
        tile_copy(chunks * CH + at, code // groups, code % groups).start()
        return carry

    lax.fori_loop(0, extra_sm[0], send_extra, 0)

    def drain_four(at, carry):
        tile_copy(0, 0, 0, 4).wait()
        return carry

    def drain_one(at, carry):
        tile_copy(0, 0, 0).wait()
        return carry

    def drain(a):
        lax.fori_loop(0, (list_sm[a, 4, 0] + 3) // 4, drain_four, 0)

    loop(chunks, drain)
    lax.fori_loop(0, extra_sm[0], drain_one, 0)


def assemble_kernel(place, sizes, got_ref, prior_ref, filled_ref, out_ref,
                    jt, rows_s, cols_s, app, bt, blk, tiles, keys,
                    listing, info, list_sm, info_sm, extra_sm, sem_list, sem_info, sem_out,
                    squares, sem_sq):
    del filled_ref
    rows, cols, _ = sizes
    region, column = place()
    first = (region == 0) & (column * cols < rows)

    @pl.when(first)
    def _():
        first_region(place, sizes, got_ref, prior_ref, out_ref, app, squares, sem_sq)

    @pl.when(jnp.logical_not(first))
    def _():
        general(place, sizes, got_ref, prior_ref, out_ref, jt, rows_s, cols_s, app, bt, blk,
                tiles, keys, listing, info, list_sm, info_sm, extra_sm, sem_list, sem_info, sem_out)


def assemble(place, rows, cols, got, prior2, filled):
    count = got.shape[0] // SLOT * 8
    chunks = count // CH
    capacity = rows // 8 * (cols // 128)
    any_space = pl.BlockSpec(memory_space=pl.ANY)
    vmem = pl.BlockSpec(memory_space=pltpu.VMEM)
    return pl.pallas_call(
        functools.partial(assemble_kernel, place, (rows, cols, chunks)),
        out_shape=jax.ShapeDtypeStruct((rows, cols), f32),
        in_specs=[vmem, vmem, any_space],
        out_specs=any_space,
        scratch_shapes=[
            pltpu.VMEM((chunks, 128, CH), f32),
            pltpu.VMEM((chunks, 24, CH), f32),
            pltpu.VMEM((chunks, CH, 128), f32),
            pltpu.VMEM((64, 128), f32),
            pltpu.VMEM((chunks, 64, CH), f32),
            pltpu.VMEM((chunks, 256, CH), bf16),
            pltpu.VMEM(((count + capacity) * 8, 128), f32),
            pltpu.VMEM((CH, CH), f32),
            pltpu.VMEM((chunks, 8, 128), i32),
            pltpu.VMEM((chunks, 8, CH), i32),
            pltpu.SMEM((chunks, 8, 128), i32),
            pltpu.SMEM((chunks, 8, CH), i32),
            pltpu.SMEM((1 + capacity,), i32),
            pltpu.SemaphoreType.DMA((chunks,)),
            pltpu.SemaphoreType.DMA((chunks,)),
            pltpu.SemaphoreType.DMA,
            pltpu.VMEM((1024, 128), f32),
            pltpu.SemaphoreType.DMA((cols // 128,)),
        ],
        input_output_aliases={2: 0},
        compiler_params=pltpu.CompilerParams(vmem_limit_bytes=48 << 20),
        name="assemble",
    )(got, prior2, filled)


def place():
    return lax.axis_index("region"), lax.axis_index("col")


def body(jac, dest, near_pose, prior):
    regions, columns = lax.axis_size("region"), lax.axis_size("col")
    devices = regions * columns
    rows = prior.shape[0]
    cols = rows * regions // columns
    assert jac.shape[0] == 8 and devices * 8 % CH == 0
    assert rows % cols == 0 and rows // 8 <= 256 and regions <= 256
    assert cols // 8 <= 128 and rows // 8 * (cols // 128) <= 2048
    assert rows >= PANEL and cols >= PANEL and cols % 128 == 0 and columns % 8 == 0
    prior2 = prior.reshape(rows // 128, 128)
    packed = pack(place, jac, dest, near_pose, prior2, devices).reshape(devices, SLOT // 2, 2, 128)
    got = lax.all_to_all(packed, ("region", "col"), split_axis=0, concat_axis=0, tiled=True)
    got = got.reshape(devices * SLOT, 128)
    filled = fill(place, rows, cols, prior2)
    return assemble(place, rows, cols, got, prior2, filled)


def solution(mesh):
    return jax.shard_map(
        body,
        mesh=mesh,
        in_specs=(
            P(("region", "col"), None),
            P(("region", "col"), None),
            P(("region", "col"), None),
            P("region"),
        ),
        out_specs=P("region", "col"),
        check_vma=False,
    )
```

```python
import functools

import jax
import jax.numpy as jnp
from jax import lax
from jax.experimental import pallas as pl
from jax.experimental.pallas import tpu as pltpu
from jax.sharding import PartitionSpec as P

NB = 128
K_PANELS = 2
PANEL = NB * K_PANELS
PP = PANEL // 8
CH = 256
BIG = float(1 << 24)
f32, bf16, i32 = jnp.float32, jnp.bfloat16, jnp.int32


def iota(shape, dim):
    return lax.broadcasted_iota(i32, shape, dim)


def split(x, parts):
    out = []
    for _ in range(parts):
        top = x.astype(bf16)
        out.append(top)
        x = x - top.astype(f32)
    return out


def dot(a, b, dims=((1,), (0,))):
    return lax.dot_general(a, b, (dims, ((), ())), preferred_element_type=f32)


SLOT = 10
LABEL_AT = (0, 56, 64, 120)


def pack_kernel(place, jac_ref, dest_ref, near_ref, prior_ref, out_ref):
    _, column = place()
    shape = (8, 128)
    lane, row = iota(shape, 1), iota(shape, 0)
    fill_up = jnp.zeros((2, 120), f32)
    dest = jnp.concatenate([dest_ref[...].astype(f32), fill_up], axis=1)
    near = jnp.concatenate([near_ref[...].astype(f32), fill_up], axis=1)
    labels = jnp.zeros(shape, f32)
    for at, line in zip(LABEL_AT, (dest[0:1, :], near[0:1, :], dest[1:2, :], near[1:2, :])):
        line = jnp.broadcast_to(line, shape)
        labels = labels + (pltpu.roll(line, at, 1) if at else line)
    column = column % 8
    prior = jnp.broadcast_to(prior_ref[pl.ds(column // 4, 1), :], shape)
    weights = jnp.zeros(shape, f32)
    for at, part in enumerate(split(prior, 3)):
        moved = pltpu.roll(part.astype(f32), (4 + at - column % 4) % 4 * 32, 1)
        weights = jnp.where(lane // 32 == at, moved, weights)
    jac = jac_ref[...].astype(f32)
    turned = [jac if not at else pltpu.roll(jac, 2 * at, 0) for at in range(4)]
    pieces = []
    for at in range(SLOT):
        piece = jnp.zeros(shape, f32)
        for slot in range(8):
            first = SLOT * slot - 8 * at
            if -SLOT < first < 8:
                piece = jnp.where((row >= first) & (row < first + 8), turned[slot % 4], piece)
                piece = jnp.where(row == first + 8, labels, piece)
                piece = jnp.where(row == first + 9, weights, piece)
        pieces.append(piece)
    eight = jnp.concatenate(pieces, axis=0).astype(bf16)
    for at in range(out_ref.shape[0] // (8 * SLOT)):
        out_ref[8 * SLOT * at : 8 * SLOT * (at + 1), :] = eight


def pack(place, jac, dest, near_pose, prior2, devices):
    return pl.pallas_call(
        functools.partial(pack_kernel, place),
        out_shape=jax.ShapeDtypeStruct((devices * SLOT, 128), bf16),
        in_specs=[pl.BlockSpec(memory_space=pltpu.VMEM)] * 4,
        out_specs=pl.BlockSpec(memory_space=pltpu.VMEM),
        name="pack",
    )(jac, dest.T, near_pose.T, prior2)


def fill_kernel(place, sizes, prior_ref, out_ref, zeros, squares, sem, sem2):
    rows, cols = sizes
    region, column = place()
    pieces = rows // zeros.shape[0]
    zeros[...] = jnp.zeros_like(zeros)
    step = zeros.shape[0]
    copies = [
        pltpu.make_async_copy(zeros, out_ref.at[pl.ds(at * step, step), :], sem.at[at])
        for at in range(pieces)
    ]
    for copy in copies:
        copy.start()
    start = column * cols - region * rows
    own = (start >= 0) & (start < rows)

    @pl.when(own)
    def _():
        diagonal = iota((128, 128), 0) == iota((128, 128), 1)
        first = start // 128
        for at in range(cols // 128):
            squares[at] = jnp.where(diagonal, prior_ref[pl.ds(first + at, 1), :], 0.0)

    for copy in copies:
        copy.wait()

    @pl.when(own)
    def _():
        base = pl.multiple_of(start, 128)
        patches = [
            pltpu.make_async_copy(
                squares.at[at],
                out_ref.at[pl.ds(base + at * 128, 128), pl.ds(at * 128, 128)],
                sem2.at[at],
            )
            for at in range(cols // 128)
        ]
        for patch in patches:
            patch.start()
        for patch in patches:
            patch.wait()


def fill(place, rows, cols, prior2):
    step = min(256, rows)
    return pl.pallas_call(
        functools.partial(fill_kernel, place, (rows, cols)),
        out_shape=jax.ShapeDtypeStruct((rows, cols), f32),
        out_specs=pl.BlockSpec(memory_space=pl.ANY),
        scratch_shapes=[
            pltpu.VMEM((step, cols), f32),
            pltpu.VMEM((cols // 128, 128, 128), f32),
            pltpu.SemaphoreType.DMA((rows // step,)),
            pltpu.SemaphoreType.DMA((cols // 128,)),
        ],
        cost_estimate=pl.CostEstimate(flops=0, bytes_accessed=rows * cols * 4, transcendentals=0),
        name="fill",
    )(prior2)


def batched(left, right):
    out = []
    for k in range(8):
        total = left[0][k : k + 1, :] * right[0]
        for e in range(1, 8):
            total = total + left[e][k : k + 1, :] * right[e]
        out.append(total)
    return out


def slabs(block):
    return [block[8 * e : 8 * e + 8, :] for e in range(8)]


def to_columns(rows):
    full = jnp.concatenate([rows, jnp.zeros((120, CH), f32)], axis=0)
    return full.T


def cholesky(a):
    row = iota((8, 128), 0)
    columns, scales = [], []
    a = list(a)
    for j in range(8):
        pivot = a[j][j : j + 1, :]
        scale = lax.rsqrt(pivot)
        scale = scale * (1.5 - 0.5 * pivot * scale * scale)
        column = jnp.where(row >= j, a[j] * scale, 0.0)
        for k in range(j + 1, 8):
            a[k] = a[k] - column * column[k : k + 1, :]
        columns.append(column)
        scales.append(scale)
    inverse = []
    for i in range(8):
        x = jnp.where(row == i, 1.0, 0.0)
        for j in range(i, 8):
            value = x[j : j + 1, :] * scales[j]
            x = jnp.where(row == j, value, jnp.where(row > j, x - columns[j] * value, x))
        inverse.append(x)
    return columns, inverse


def loop(count, body):
    if count == 1:
        body(0)
    else:
        lax.fori_loop(0, count, lambda at, carry: (body(at), carry)[1], 0)


def expansion():
    row, lane = iota((8, 128), 0), iota((8, 128), 1)
    none = jnp.zeros((8, 128), f32)
    straight = jnp.where(lane % 8 == row, 1.0, 0.0)
    by_rows = [
        jnp.concatenate([straight if at == k else none for at in range(8)], axis=1)
        for k in range(8)
    ]
    by_columns = [
        jnp.concatenate(
            [jnp.where((row == at) & (lane % 8 == j), 1.0, 0.0) for at in range(8)], axis=1
        )
        for j in range(8)
    ]
    return jnp.concatenate((by_rows + by_columns) * 2, axis=0).astype(bf16)


def slot_rows(got_ref, a, at, per):
    block = got_ref[pl.ds(a * (CH // 8) * SLOT, per * SLOT), :].astype(f32)
    return jnp.concatenate([block[SLOT * d + at : SLOT * d + at + 1, :] for d in range(per)], axis=0)


def label_rows(got_ref, a):
    return slot_rows(got_ref, a, 8, CH // 8)


def jac_columns(got_ref, a):
    per = CH // 8
    block = got_ref[pl.ds(a * per * SLOT, per * SLOT), :].astype(f32)
    return jnp.concatenate([block[SLOT * d : SLOT * d + 8, :] for d in range(per)], axis=0).T


def spread(labels):
    lane8, row8 = iota((8, 128), 1), iota((8, 128), 0)
    out = []
    for at in LABEL_AT:
        halves = []
        for half in range(2):
            total = jnp.zeros((8, 128), f32)
            for part in range(2):
                from_row = 16 * half + 8 * part
                piece = labels[from_row : from_row + 8, :]
                piece = pltpu.roll(piece, (64 * part - at) % 128, 1, stride=8, stride_axis=0)
                total = total + jnp.where(lane8 // 8 == row8 + 8 * part, piece, 0.0)
            halves.append(jnp.sum(total, axis=0, keepdims=True))
        out.append(jnp.concatenate(halves, axis=1))
    return out


def on_diagonal(prior_row):
    kl, unknown = iota((64, PANEL), 0), iota((64, PANEL), 1)
    diagonal = jnp.where((kl // 8 == kl % 8) & (unknown % 8 == kl % 8), prior_row, 0.0)
    own_pose = jnp.where(iota((PANEL, 128), 0) // 8 == iota((PANEL, 128), 1), 1.0, 0.0).astype(bf16)
    first = dot(jnp.concatenate(split(diagonal, 3), axis=0), own_pose)
    kl = iota((64, 128), 0)
    spare = (kl // 8 == kl % 8) & (iota((64, 128), 1) >= PP)
    return first[0:64] + first[64:128] + first[128:192] + jnp.where(spare, 1.0, 0.0)


def first_region(place, sizes, got_ref, prior_ref, out_ref, app, squares, sem):
    rows, cols, chunks = sizes
    col_poses, groups = cols // 8, cols // 128
    _, column = place()
    column_f = column.astype(f32)
    start = pl.multiple_of(column * cols, 128)
    local = prior_ref[pl.ds(column * groups, groups), :]
    prior_row = jnp.concatenate([prior_ref[0:1, :], prior_ref[1:2, :]], axis=1)
    first = on_diagonal(prior_row)
    app[...] = jnp.zeros_like(app)

    def measure(a):
        jac_t = jac_columns(got_ref, a)
        d0, n0, d1, n1 = spread(label_rows(got_ref, a))
        grams, of_pose = [], []
        for at, (region_of, number) in enumerate(((d0, n0), (d1, n1))):
            side = slabs(jac_t[64 * at : 64 * at + 64, :])
            gram = jnp.concatenate(batched(side, side), axis=0)
            grams.append(jnp.concatenate(split(gram, 2), axis=0))
            pose = number - column_f * col_poses
            pose = jnp.where((region_of == 0) & (pose < col_poses), pose, -1.0)
            of_pose.append(jnp.where(iota((128, CH), 0).astype(f32) == pose, 1.0, 0.0).astype(bf16))
        total = dot(
            jnp.concatenate(grams, axis=1), jnp.concatenate(of_pose, axis=1), ((1,), (1,))
        )
        app[...] += total[0:64] + total[64:128]

    loop(chunks, measure)
    gram = app[...]
    factor, _ = cholesky(slabs(gram + first))
    table = expansion()
    by_rows, by_columns = table[0:64], table[64:128]

    def copy_of(at):
        return pltpu.make_async_copy(
            squares.at[pl.ds(at * 128, 128), :],
            out_ref.at[pl.ds(start + at * 128, 128), pl.ds(at * 128, 128)],
            sem.at[at],
        )

    def expanded(block, by, count):
        full = jnp.concatenate([block, jnp.zeros((64, 128), f32)], axis=0).T[0:count, :]
        high, low = (part[:, 0:64] for part in split(full, 2))
        both = jnp.concatenate([high, low], axis=1)
        return dot(both, jnp.concatenate([by, by], axis=0))

    value = expanded(gram, by_rows, 128)
    pose, lane = iota((128, 128), 0), iota((128, 128), 1)
    weights = [jnp.broadcast_to(local[at : at + 1, :], (16, 128)) for at in range(groups)]
    weights = jnp.concatenate(weights + [jnp.zeros((16, 128), f32)] * (8 - groups), axis=0)
    keep, lane_in = lane // 8 == pose % 16, lane % 8
    pieces = []
    for k in range(8):
        piece = jnp.where(keep, value[:, 128 * k : 128 * k + 128], 0.0)
        piece = piece + jnp.where(keep & (lane_in == k), weights, 0.0)
        pieces.append(piece[0:PP, :])
        squares[pl.ds(PANEL + k, 128 - PP, stride=8), :] = piece[PP:, :]
    for at in range(K_PANELS, groups):
        copy_of(at).start()
    value = expanded(jnp.concatenate(factor, axis=0), by_columns, PP)
    for k in range(8):
        piece = jnp.where(keep[0:PP, :], value[:, 128 * k : 128 * k + 128], 0.0)
        squares[pl.ds(k, PP, stride=8), :] = jnp.where(column == 0, piece, pieces[k])
    for at in range(K_PANELS):
        copy_of(at).start()
    for at in range(groups):
        copy_of(at).wait()


def general(place, sizes, got_ref, prior_ref, out_ref,
                    jt, rows_s, cols_s, app, bt, blk, tiles, keys,
                    listing, info, list_sm, info_sm, extra_sm, sem_list, sem_info, sem_out):
    rows, cols, chunks = sizes
    row_poses, col_poses, groups = rows // 8, cols // 8, cols // 128
    region, column = place()
    region_f, column_f = region.astype(f32), column.astype(f32)
    start = column * cols - region * rows
    own = (start >= 0) & (start < rows)
    share = jnp.where(own, 1.0, 0.0)
    lane8, row8 = iota((8, 128), 1), iota((8, 128), 0)
    before = iota((CH, CH), 0) < iota((CH, CH), 1)
    table = expansion()

    labels0 = label_rows(got_ref, 0)
    sent = slot_rows(got_ref, 0, 9, 8)
    panel_prior = sent
    for at in range(1, 3):
        panel_prior = panel_prior + pltpu.roll(sent, 128 - 32 * at, 1)
    panel_prior = jnp.where(lane8 < 32, panel_prior, 0.0)
    lined = jnp.zeros((8, 128), f32)
    for at in range(4):
        moved = panel_prior if at == 0 else pltpu.roll(panel_prior, 32 * at, 1)
        lined = lined + jnp.where(row8 % 4 == at, moved, 0.0)
    halves = [
        jnp.sum(jnp.where(row8 < 4, lined, 0.0), axis=0, keepdims=True),
        jnp.sum(jnp.where(row8 >= 4, lined, 0.0), axis=0, keepdims=True),
    ]
    prior_row = jnp.concatenate(halves, axis=1)
    app[...] = on_diagonal(prior_row)

    def measure(a):
        jac_t = jac_columns(got_ref, a)
        jt[a] = jac_t
        d0, n0, d1, n1 = spread(labels0 if chunks == 1 else label_rows(got_ref, a))
        c0 = d0 * row_poses + n0 - column_f * col_poses
        c1 = d1 * row_poses + n1 - column_f * col_poses
        one, none = jnp.ones_like(d0), jnp.zeros_like(d0)
        row0, row1 = d0 == region_f, d1 == region_f
        col0, col1 = (c0 >= 0) & (c0 < col_poses), (c1 >= 0) & (c1 < col_poses)
        pan0, pan1 = (d0 == 0) & (n0 < PP), (d1 == 0) & (n1 < PP)
        has_row = jnp.where(row0 | row1, one, none)
        has_col = jnp.where(col0 | col1, one, none)
        touches = jnp.where(pan0 | pan1, one, none)
        row_pose = jnp.where(row0, n0, n1)
        col_pose = jnp.where(col0, c0, c1)
        pan_side = jnp.where(pan0, none, one)
        pan_pose = jnp.where(pan0, n0, n1)
        row_in_panel = jnp.where((row0 & pan0) | (row1 & pan1), one, none)
        col_in_panel = jnp.where((col0 & pan0) | (col1 & pan1), one, none)
        relevant = has_row * has_col * (1.0 - row_in_panel)
        group = jnp.floor(col_pose * (1.0 / 16.0))
        tile = row_pose * groups + group
        cell = row_pose * col_poses + col_pose
        is_row = touches * has_row * (1.0 - row_in_panel)
        is_col = touches * has_col * (1.0 - col_in_panel)
        lines = [
            jnp.where(relevant > 0, tile, -1.0),
            jnp.where(relevant > 0, cell, -1.0),
            jnp.where(touches > 0, pan_pose, -1.0),
            jnp.where(is_row > 0, pan_pose, -1.0),
            col_pose - group * 16.0,
            none, none, none,
        ]
        more = [
            jnp.where(relevant > 0, tile, -2.0),
            jnp.where(relevant > 0, cell, -2.0),
            jnp.where(is_col > 0, pan_pose, -2.0),
            relevant,
            row_pose,
            group,
            col_pose,
            is_row * is_col,
            jnp.where(row0, none, one),
            jnp.where(col0, none, one),
            pan_side,
            col_in_panel,
            none, none, none, none,
        ]
        lines = jnp.concatenate(lines, axis=0)
        rows_s[a] = jnp.concatenate([lines] + more, axis=0)
        columns = to_columns(lines)
        cols_s[a] = columns
        j0, j1 = slabs(jac_t[0:64, :]), slabs(jac_t[64:128, :])
        near = [jnp.where(pan_side == 0, x, y) for x, y in zip(j0, j1)]
        gram = jnp.concatenate(batched(near, near), axis=0)
        of_pose = jnp.where(
            columns[:, 2:3] == iota((CH, 128), 1).astype(f32), 1.0, 0.0
        ).astype(bf16)
        total = dot(jnp.concatenate(split(gram, 2), axis=0), of_pose)
        app[...] += total[0:64] + total[64:128]

    loop(chunks, measure)

    def earlier_of(a, at, at_right):
        def from_chunk(b, count):
            other = jnp.broadcast_to(cols_s[b, :, at : at + 1], (CH, CH))
            same = jnp.where(other == rows_s[a, at_right : at_right + 1, :], 1.0, 0.0)
            if chunks == 1:
                same = jnp.where(before, same, 0.0)
            else:
                here, all_of_it = jnp.where(b == a, 1.0, 0.0), jnp.where(b < a, 1.0, 0.0)
                same = jnp.where(before, same, 0.0) * here + same * all_of_it
            return count + jnp.sum(same, axis=0, keepdims=True)

        nothing = jnp.zeros((1, CH), f32)
        return from_chunk(0, nothing) if chunks == 1 else lax.fori_loop(0, chunks, from_chunk, nothing)

    def lists(a):
        relevant = rows_s[a, 11:12, :]
        kept = jnp.where(earlier_of(a, 0, 8) == 0, relevant, 0.0)
        lone = jnp.where(earlier_of(a, 1, 9) == 0, relevant, 0.0)
        joins = lone * (1.0 - kept)
        rows_s[a, 20:21, :] = kept
        count = jnp.sum(kept, axis=1, keepdims=True)
        upper = jnp.where(before, 1.0, 0.0).astype(bf16)
        rank = dot(jnp.broadcast_to(kept, (16, CH)).astype(bf16), upper)[0:1, :]
        slot = iota((CH, CH), 0)
        slot = (slot % 64 * 4 + slot // 64).astype(f32)
        slot = jnp.where(slot < count, slot, 0.0)
        chosen = jnp.where((rank == slot) & (kept > 0), 1.0, 0.0).astype(bf16)
        position = iota((1, CH), 1).astype(f32)
        data = jnp.concatenate(
            [rows_s[a, 12:13, :], rows_s[a, 13:14, :], position, jnp.zeros((13, CH), f32)], axis=0
        ).astype(bf16)
        found = dot(data, chosen, ((1,), (1,)))[0:8, :]
        code = found[2:3, :] + found[0:1, :] * 256.0 + found[1:2, :] * 65536.0
        line = [code[:, 0:128], pltpu.roll(code[:, 0:128], 64, 1)]
        line += [code[:, 128:256], pltpu.roll(code[:, 128:256], 64, 1)]
        line += [jnp.broadcast_to(count, (1, 128)), jnp.zeros((3, 128), f32)]
        listing[a] = jnp.concatenate(line, axis=0).astype(i32)
        pltpu.make_async_copy(listing.at[a], list_sm.at[a], sem_list.at[a]).start()
        info[a] = jnp.concatenate(
            [rows_s[a, 12:13, :], rows_s[a, 14:15, :], joins, jnp.zeros((5, CH), f32)], axis=0
        ).astype(i32)
        pltpu.make_async_copy(info.at[a], info_sm.at[a], sem_info.at[a]).start()

    loop(chunks, lists)

    def key_table(a, b):
        left = jnp.broadcast_to(cols_s[a, :, 3:4], (CH, CH))
        valid = jnp.where(left == rows_s[b, 10:11, :], 1.0, 0.0)
        same = iota((CH, CH), 0) == iota((CH, CH), 1)
        joins = info[a, 2:3, :].astype(f32)
        if chunks > 1:
            flag = jnp.where(a == b, 1.0, 0.0)
            joins = joins * flag + valid * (1.0 - flag)
        valid = jnp.where(same, joins, valid)
        key = (iota((CH, CH), 0) * CH + iota((CH, CH), 1)).astype(f32)
        key = jnp.where(valid > 0, key, BIG)
        keys[...] = key
        return jnp.min(key)

    early = key_table(0, 0) if chunks == 1 else None

    _, inverse = cholesky(slabs(app[...]))
    inverse = jnp.concatenate(split(jnp.concatenate(inverse, axis=0), 3), axis=0)

    def blocks(a):
        row = [rows_s[a, at : at + 1, :] for at in range(24)]
        jac_t = jt[a]
        j0, j1 = slabs(jac_t[0:64, :]), slabs(jac_t[64:128, :])
        left = [jnp.where(row[16] == 0, x, y) for x, y in zip(j0, j1)]
        right = [jnp.where(row[17] == 0, x, y) for x, y in zip(j0, j1)]
        near = [jnp.where(row[18] == 0, x, y) for x, y in zip(j0, j1)]
        far = [jnp.where(row[18] == 0, y, x) for x, y in zip(j0, j1)]
        gram = batched(left, right)
        cross = batched(near, far)
        of_pose = jnp.where(iota((128, CH), 0).astype(f32) == row[2], 1.0, 0.0).astype(bf16)
        inv = dot(inverse, of_pose)
        inv = slabs(inv[0:64] + inv[64:128] + inv[128:192])
        solved = []
        for j in range(8):
            total = inv[0][j : j + 1, :] * cross[0]
            for i in range(1, j + 1):
                total = total + inv[i][j : j + 1, :] * cross[i]
            solved.append(total)
        bt[a] = jnp.concatenate(solved, axis=0)
        outer = batched(solved, solved)
        keep_normal = row[11] * (1.0 - row[19])
        keep_panel = row[11] * row[19]
        values = [(g - o * row[15]) * keep_normal for g, o in zip(gram, outer)]
        values += [x * keep_panel for x in solved]
        values = jnp.concatenate(values, axis=0)
        high, low = split(values, 2)
        blk[a] = jnp.concatenate([high, low], axis=0)

    loop(chunks, blocks)

    def merge(a):
        line = [rows_s[a, at : at + 1, :] for at in range(24)]

        def from_chunk(b, total):
            other = jnp.broadcast_to(cols_s[b, :, 1:2], (CH, CH))
            same = jnp.where(other == line[9], 1.0, 0.0).astype(bf16)
            found = dot(blk[b], same)
            return total + found[0:128] + found[128:256]

        total = jnp.zeros((128, CH), f32)
        total = from_chunk(0, total) if chunks == 1 else lax.fori_loop(0, chunks, from_chunk, total)
        sixteenth = jnp.floor(line[12] * (1.0 / 16.0))
        pieces = rows // 128
        local = jnp.concatenate(
            [prior_ref[...], jnp.zeros((16 - pieces, 128), f32)], axis=0
        ) if pieces < 16 else prior_ref[...]
        steps = local.shape[0]
        parts = jnp.concatenate(split(local, 3), axis=0)
        of_row = jnp.where(
            (iota((3 * steps, CH), 0) % steps).astype(f32) == sixteenth, 1.0, 0.0
        ).astype(bf16)
        priors = dot(parts, of_row, ((0,), (0,)))
        within = line[12] - sixteenth * 16.0
        on_row = jnp.zeros((8, CH), f32)
        for at in range(16):
            on_row = on_row + jnp.where(within == float(at), priors[8 * at : 8 * at + 8, :], 0.0)
        on_row = on_row * (share * line[11])
        sub = iota((8, CH), 0)
        normal = [
            total[8 * k : 8 * k + 8, :] + jnp.where(sub == k, on_row, 0.0) for k in range(8)
        ]
        total = jnp.concatenate(normal + [total[64:128, :]], axis=0)
        value = dot(jnp.concatenate(split(total.T, 2), axis=1), table)
        keep = (iota((CH, 128), 1) // 8).astype(f32) == cols_s[a, :, 4:5]
        for k in range(8):
            tiles[pl.ds(a * CH * 8 + k, CH, stride=8), :] = jnp.where(
                keep, value[:, 128 * k : 128 * k + 128], 0.0
            )

    loop(chunks, merge)

    def waiting(a):
        pltpu.make_async_copy(listing.at[a], list_sm.at[a], sem_list.at[a]).wait()
        pltpu.make_async_copy(info.at[a], info_sm.at[a], sem_info.at[a]).wait()

    loop(chunks, waiting)
    extra_sm[0] = 0

    def tile_rows(slot, count=1):
        return pl.ds(pl.multiple_of(slot * 8, 8), 8 * count)

    def pairs(index):
        a, b = (0, 0) if chunks == 1 else (index // chunks, index % chunks)

        def one(key_now):
            number = key_now.astype(i32)
            m1, m2 = number >> 8, number & (CH - 1)
            joining = (m1 == m2) if chunks == 1 else ((m1 == m2) & (a == b))
            r1, c2 = info_sm[a, 0, m1], info_sm[b, 1, m2]
            group, within = c2 >> 4, c2 & 15
            code = r1 * groups + group
            code_f = code.astype(f32)
            key_next = jnp.min(jnp.where(keys[...] > key_now, keys[...], BIG))

            def search(chunk, best):
                at_one = (rows_s[chunk, 8:9, :] == code_f) & (rows_s[chunk, 20:21, :] > 0)
                slots = (iota((1, CH), 1) + chunk * CH).astype(f32)
                return jnp.minimum(best, jnp.min(jnp.where(at_one, slots, BIG)))

            slot = search(0, BIG) if chunks == 1 else lax.fori_loop(0, chunks, search, BIG)
            position = iota((8, CH), 1)
            total = jnp.zeros((8, 128), f32)
            for j in range(8):
                x = bt[a, 8 * j : 8 * j + 8, :]
                y = bt[b, 8 * j : 8 * j + 8, :]
                x = jnp.sum(jnp.where(position == m1, x, 0.0), axis=1, keepdims=True)
                y = jnp.sum(jnp.where(position == m2, y, 0.0), axis=1, keepdims=True)
                y = jnp.where(lane8 % 8 == row8, y, 0.0)
                y = jnp.sum(y, axis=0, keepdims=True)
                total = total + x * y
            total = jnp.where(lane8 // 8 == within, -total, 0.0)
            total = jnp.where(joining, tiles[tile_rows(a * CH + m1), :], total)
            added = extra_sm[0]
            slot = jnp.where(slot < BIG, slot, -1.0).astype(i32)

            def at_extra(at, slot):
                return jnp.where(extra_sm[1 + at] == code, chunks * CH + at, slot)

            slot = lax.fori_loop(0, added, at_extra, slot)
            fresh = slot < 0
            slot = jnp.where(fresh, chunks * CH + added, slot)
            where = tile_rows(slot)
            tiles[where, :] = jnp.where(fresh, 0.0, tiles[where, :]) + total

            @pl.when(fresh)
            def _():
                extra_sm[1 + added] = code
                extra_sm[0] = added + 1

            return key_next

        smallest = early if chunks == 1 else key_table(a, b)
        lax.while_loop(lambda key_now: key_now < BIG, one, smallest)

    loop(chunks * chunks, pairs)

    def tile_copy(slot, r, group, count=1):
        return pltpu.make_async_copy(
            tiles.at[tile_rows(slot, count), :],
            out_ref.at[tile_rows(r, count), pl.ds(pl.multiple_of(group * 128, 128), 128)],
            sem_out,
        )

    def send(a):
        def four(at, carry):
            for more in range(4):
                entry = list_sm[a, more, at]
                slot, r = a * CH + (entry & 255), (entry >> 8) & 255
                tile_copy(slot, r, entry >> 16).start()
            return carry
        lax.fori_loop(0, (list_sm[a, 4, 0] + 3) // 4, four, 0)

    loop(chunks, send)

    def send_extra(at, carry):
        code = extra_sm[1 + at]
        tile_copy(chunks * CH + at, code // groups, code % groups).start()
        return carry

    lax.fori_loop(0, extra_sm[0], send_extra, 0)

    def drain_four(at, carry):
        tile_copy(0, 0, 0, 4).wait()
        return carry

    def drain_one(at, carry):
        tile_copy(0, 0, 0).wait()
        return carry

    def drain(a):
        lax.fori_loop(0, (list_sm[a, 4, 0] + 3) // 4, drain_four, 0)

    loop(chunks, drain)
    lax.fori_loop(0, extra_sm[0], drain_one, 0)


def assemble_kernel(place, sizes, got_ref, prior_ref, filled_ref, out_ref,
                    jt, rows_s, cols_s, app, bt, blk, tiles, keys,
                    listing, info, list_sm, info_sm, extra_sm, sem_list, sem_info, sem_out,
                    squares, sem_sq):
    del filled_ref
    rows, cols, _ = sizes
    region, column = place()
    first = (region == 0) & (column * cols < rows)

    @pl.when(first)
    def _():
        first_region(place, sizes, got_ref, prior_ref, out_ref, app, squares, sem_sq)

    @pl.when(jnp.logical_not(first))
    def _():
        general(place, sizes, got_ref, prior_ref, out_ref, jt, rows_s, cols_s, app, bt, blk,
                tiles, keys, listing, info, list_sm, info_sm, extra_sm, sem_list, sem_info, sem_out)


def assemble(place, rows, cols, got, prior2, filled):
    count = got.shape[0] // SLOT * 8
    chunks = count // CH
    capacity = rows // 8 * (cols // 128)
    any_space = pl.BlockSpec(memory_space=pl.ANY)
    vmem = pl.BlockSpec(memory_space=pltpu.VMEM)
    return pl.pallas_call(
        functools.partial(assemble_kernel, place, (rows, cols, chunks)),
        out_shape=jax.ShapeDtypeStruct((rows, cols), f32),
        in_specs=[vmem, vmem, any_space],
        out_specs=any_space,
        scratch_shapes=[
            pltpu.VMEM((chunks, 128, CH), f32),
            pltpu.VMEM((chunks, 24, CH), f32),
            pltpu.VMEM((chunks, CH, 128), f32),
            pltpu.VMEM((64, 128), f32),
            pltpu.VMEM((chunks, 64, CH), f32),
            pltpu.VMEM((chunks, 256, CH), bf16),
            pltpu.VMEM(((count + capacity) * 8, 128), f32),
            pltpu.VMEM((CH, CH), f32),
            pltpu.VMEM((chunks, 8, 128), i32),
            pltpu.VMEM((chunks, 8, CH), i32),
            pltpu.SMEM((chunks, 8, 128), i32),
            pltpu.SMEM((chunks, 8, CH), i32),
            pltpu.SMEM((1 + capacity,), i32),
            pltpu.SemaphoreType.DMA((chunks,)),
            pltpu.SemaphoreType.DMA((chunks,)),
            pltpu.SemaphoreType.DMA,
            pltpu.VMEM((1024, 128), f32),
            pltpu.SemaphoreType.DMA((cols // 128,)),
        ],
        input_output_aliases={2: 0},
        compiler_params=pltpu.CompilerParams(vmem_limit_bytes=48 << 20),
        name="assemble",
    )(got, prior2, filled)


def place():
    return lax.axis_index("region"), lax.axis_index("col")


def body(jac, dest, near_pose, prior):
    regions, columns = lax.axis_size("region"), lax.axis_size("col")
    devices = regions * columns
    rows = prior.shape[0]
    cols = rows * regions // columns
    assert jac.shape[0] == 8 and devices * 8 % CH == 0
    assert rows % cols == 0 and rows // 8 <= 256 and regions <= 256
    assert cols // 8 <= 128 and rows // 8 * (cols // 128) <= 2048
    assert rows >= PANEL and cols >= PANEL and cols % 128 == 0 and columns % 8 == 0
    prior2 = prior.reshape(rows // 128, 128)
    packed = pack(place, jac, dest, near_pose, prior2, devices).reshape(devices, SLOT // 2, 2, 128)
    got = lax.all_to_all(packed, ("region", "col"), split_axis=0, concat_axis=0, tiled=True)
    got = got.reshape(devices * SLOT, 128)
    filled = fill(place, rows, cols, prior2)
    return assemble(place, rows, cols, got, prior2, filled)


def solution(mesh):
    return jax.shard_map(
        body,
        mesh=mesh,
        in_specs=(
            P(("region", "col"), None),
            P(("region", "col"), None),
            P(("region", "col"), None),
            P("region"),
        ),
        out_specs=P("region", "col"),
        check_vma=False,
    )
```
